32 devices in a mesh: seq: 4 (over y, x), fsdp: 8 (over z, core).
Axes of the slice: x: 2, y: 2, z: 4, core: 2. Of those that a mesh axis runs over, the one named last changes fastest.
Arguments:
- tokens: bfloat16 [8, 2048, 768], P('fsdp', 'seq'), may hold values from -6 to 6
- segment: int32 [8, 2048], P('fsdp'), may hold values from 0 to 10, as said below
- padding: int32 [8, 2048], P('fsdp'), may hold values from 0 to 1, as said below
- triple_weight: bfloat16 [768, 2304], P('fsdp'), may hold values from -0.3125 to 0.3125
- query_bias: bfloat16 [768], P('fsdp'), may hold values from -2 to 2
- value_bias: bfloat16 [768], P('fsdp'), may hold values from -2 to 2
- output_weight: bfloat16 [768, 768], P('fsdp'), may hold values from -0.875 to 0.875
- output_bias: bfloat16 [768], P('fsdp'), may hold values from -2 to 2
- first_gain: bfloat16 [768], P('fsdp'), may hold values from 0.5 to 1.5
- first_shift: bfloat16 [768], P('fsdp'), may hold values from -2 to 2
- expand_weight: bfloat16 [768, 3072], P('fsdp'), may hold values from -0.21875 to 0.21875
- expand_bias: bfloat16 [3072], P('fsdp'), may hold values from -2 to 2
- shrink_weight: bfloat16 [3072, 768], P('fsdp'), may hold values from -0.109375 to 0.109375
- shrink_bias: bfloat16 [768], P('fsdp'), may hold values from -2 to 2
- second_gain: bfloat16 [768], P('fsdp'), may hold values from 0.5 to 1.5
- second_shift: bfloat16 [768], P('fsdp'), may hold values from -2 to 2
- cotangent: bfloat16 [8, 2048, 768], P('fsdp', 'seq'), may hold values from -6 to 6
Outputs:
- layer_out: bfloat16 [8, 2048, 768], P('fsdp', 'seq')
- tokens_grad: bfloat16 [8, 2048, 768], P('fsdp', 'seq')
- triple_grad: float32 [768, 2304], P('fsdp')
- query_bias_grad: float32 [768], P('fsdp')
- value_bias_grad: float32 [768], P('fsdp')
- output_grad: float32 [768, 768], P('fsdp')
- output_bias_grad: float32 [768], P('fsdp')
- first_gain_grad: float32 [768], P('fsdp')
- first_shift_grad: float32 [768], P('fsdp')
- expand_grad: float32 [768, 3072], P('fsdp')
- expand_bias_grad: float32 [3072], P('fsdp')
- shrink_grad: float32 [3072, 768], P('fsdp')
- shrink_bias_grad: float32 [768], P('fsdp')
- second_gain_grad: float32 [768], P('fsdp')
- second_shift_grad: float32 [768], P('fsdp')
The draws below stay inside these ranges and needn't reach their ends.
Inputs may be any that keep to these rules, and one draw needn't show every extreme that they name: `segment`: within a sequence the ids start at 0 and never fall; each id before the padding is one document of 200 to 2000 tokens; the padded positions at the end share one further id. The first sequence holds (2048 - 1) // 200 documents of 200 tokens before any others. `padding`: 1 on the documents, 0 on the positions after a sequence's last whole document.
All inputs are finite; a program needn't handle non-finite values.
Results may differ from the reference program's by a relative error of at most 0.017.
Values may be sent and summed in bfloat16 or wider, within the bound.
A program may use at most 192 MiB of HBM per device.

```python
import jax
import jax.numpy as jnp
from jax import lax

D = 768
HEADS = 12
HEAD_DIM = 64
FF = 3072
LENGTH = 2048
DOC_MIN = 200
DOC_MOST = 2000
SEQS = 8


def packing(key):
    count = LENGTH // DOC_MIN + 1
    filled = (LENGTH - 1) // DOC_MIN
    row_keys = jax.random.split(jax.random.fold_in(key, 7), SEQS)
    row_marks = jnp.arange(SEQS)

    def one_row(row_key, row_mark):
        sizes = jax.random.randint(row_key, (count,), DOC_MIN, DOC_MOST + 1)
        forced = (jnp.arange(count) < filled) & (row_mark == 0)
        sizes = jnp.where(forced, DOC_MIN, sizes)
        ends = jnp.cumsum(sizes)
        whole = ends <= LENGTH
        used = jnp.max(jnp.where(whole, ends, 0))
        places = jnp.arange(LENGTH)
        ids = jnp.sum((ends[None, :] <= places[:, None]).astype(jnp.int32), axis=1)
        live = (places < used).astype(jnp.int32)
        return (ids.astype(jnp.int32), live)
    return jax.vmap(one_row)(row_keys, row_marks)


def draw_segment(key, part):
    return packing(key)[0]


def draw_padding(key, part):
    return packing(key)[1]


def shard_levels(key, extent, cuts, least, high):
    level, own = 1.0, jax.random.fold_in(key, 6)
    for position, blocks in cuts:
        draws = jnp.exp(jax.random.uniform(jax.random.fold_in(own, position), (blocks,), jnp.float32, least / len(cuts), high / len(cuts)))
        level = level * jnp.repeat(draws, extent[position] // blocks).reshape([-1 if axis == position else 1 for axis in range(len(extent))])
    return level


def gaussian(rng, extent, deviation, bound, shards=(), dtype=jnp.bfloat16):
    factor_of = shard_levels(rng, extent, shards, -0.22, 0.18) if shards else 1.0
    values = jax.random.normal(rng, extent, jnp.float32) * deviation * factor_of
    return jnp.minimum(jnp.maximum(values, -bound), bound).astype(dtype)


def setup_inputs(seed: int = 0) -> dict:
    splits = jax.random.split(jax.random.key(seed), 18)
    return {
        "tokens": gaussian(splits[0], (SEQS, LENGTH, D), 1.0, 6.0, ((0, 8), (1, 4))),
        "segment": draw_segment(jax.random.fold_in(splits[17], 71), 0),
        "padding": draw_padding(jax.random.fold_in(splits[17], 71), 0),
        "triple_weight": gaussian(splits[3], (D, 3 * D), (D // 2) ** -0.5, 0.3125, ((0, 8),)),
        "query_bias": gaussian(splits[4], (D,), 0.3, 2.0, ((0, 8),)),
        "value_bias": gaussian(splits[5], (D,), 0.3, 2.0, ((0, 8),)),
        "output_weight": gaussian(splits[6], (D, D), (D // 16) ** -0.5, 0.875, ((0, 8),)),
        "output_bias": gaussian(splits[7], (D,), 0.3, 2.0, ((0, 8),)),
        "first_gain": jnp.clip(1.0 + 0.1 * jax.random.normal(splits[8], (D,), jnp.float32), 0.5, 1.5).astype(jnp.bfloat16),
        "first_shift": gaussian(splits[9], (D,), 0.3, 2.0, ((0, 8),)),
        "expand_weight": gaussian(splits[10], (D, FF), D ** -0.5, 0.21875, ((0, 8),)),
        "expand_bias": gaussian(splits[11], (FF,), 0.3, 2.0, ((0, 8),)),
        "shrink_weight": gaussian(splits[12], (FF, D), FF ** -0.5, 0.109375, ((0, 8),)),
        "shrink_bias": gaussian(splits[13], (D,), 0.3, 2.0, ((0, 8),)),
        "second_gain": jnp.clip(1.0 + 0.1 * jax.random.normal(splits[14], (D,), jnp.float32), 0.5, 1.5).astype(jnp.bfloat16),
        "second_shift": gaussian(splits[15], (D,), 0.3, 2.0, ((0, 8),)),
        "cotangent": gaussian(splits[16], (SEQS, LENGTH, D), 1.0, 6.0, ((0, 8), (1, 4))),
    }


EPS = 1e-06
MASKED = -1e+30
PRECISE = lax.Precision.HIGHEST

@jax.custom_vjp
def low(v):
    return lax.optimization_barrier(v.astype(jnp.bfloat16)).astype(jnp.float32)

@jax.custom_vjp
def low_back(v):
    return v

def low_keep(v):
    return (low(v), None)

def low_pass(kept, grad):
    return (grad,)

def back_keep(v):
    return (v, None)

def back_low(kept, grad):
    return (low(grad),)
low.defvjp(low_keep, low_pass)
low_back.defvjp(back_keep, back_low)

def matmul(left, right):
    return jnp.dot(left, right, precision=PRECISE)

def norm_apply(hidden, gain, shift):
    mean = lax.optimization_barrier(jnp.mean(hidden, axis=-1, keepdims=True))
    centered = hidden - mean
    spread = lax.optimization_barrier(jnp.mean(centered * centered, axis=-1, keepdims=True))
    return centered * lax.rsqrt(spread + EPS) * gain + shift

def attention(queries, keys_in, values, allowed):

    def one_head(parts):
        head_query, head_key, head_value = parts
        scores = low_back(matmul(head_query, head_key.T) * HEAD_DIM ** (-0.5))
        scores = jnp.where(allowed, scores, MASKED)
        probs = low(jax.nn.softmax(scores, axis=-1))
        return matmul(probs, head_value)
    return lax.map(jax.checkpoint(one_head), (queries, keys_in, values))

def layer(hidden, allowed, live, triple, query_bias, value_bias, output_weight, output_bias, first_gain, first_shift, expand_weight, expand_bias, shrink_weight, shrink_bias, second_gain, second_shift):
    zeros = jnp.zeros_like(query_bias)
    mixed = matmul(hidden, triple) + jnp.concatenate([query_bias, zeros, value_bias])
    mixed = low_back(low(mixed))
    split = mixed.reshape(LENGTH, 3, HEADS, HEAD_DIM).transpose(1, 2, 0, 3)
    context = attention(split[0], split[1], split[2], allowed)
    context = context.transpose(1, 0, 2).reshape(LENGTH, D) * live[:, None]
    context = low_back(low(context))
    attended = low_back(matmul(context, output_weight) + output_bias)
    normed = norm_apply(hidden + attended, first_gain, first_shift)
    expand = low_back(matmul(low(normed), expand_weight) + expand_bias)
    active = low(jax.nn.gelu(expand, approximate=False))
    shrink = low_back(matmul(active, shrink_weight) + shrink_bias)
    return norm_apply(normed + shrink, second_gain, second_shift)

def reference(tokens, segment, padding, triple_weight, query_bias, value_bias, output_weight, output_bias, first_gain, first_shift, expand_weight, expand_bias, shrink_weight, shrink_bias, second_gain, second_shift, cotangent):
    params = tuple((weight.astype(jnp.float32) for weight in (triple_weight, query_bias, value_bias, output_weight, output_bias, first_gain, first_shift, expand_weight, expand_bias, shrink_weight, shrink_bias, second_gain, second_shift)))

    def one_sequence(totals, inputs):
        seq_tokens, seq_segment, seq_padding, seq_cotangent = inputs
        allowed = (seq_segment[:, None] == seq_segment[None, :]) & (seq_padding[None, :] == 1)
        live = seq_padding.astype(jnp.float32)

        def forward(hidden, *weights):
            return layer(hidden, allowed, live, *weights)
        result, pullback = jax.vjp(forward, seq_tokens.astype(jnp.float32), *params)
        grads = pullback(seq_cotangent.astype(jnp.float32))
        totals = tuple((total + grad for total, grad in zip(totals, grads[1:])))
        return (totals, (result.astype(jnp.bfloat16), grads[0].astype(jnp.bfloat16)))
    start = tuple((jnp.zeros_like(weight) for weight in params))
    totals, (outputs, input_grads) = lax.scan(one_sequence, start, (tokens, segment, padding, cotangent))
    return (outputs, input_grads) + totals
```

```python
import functools

import jax
import jax.numpy as jnp
from jax import lax
from jax.experimental import pallas as pl
from jax.experimental.pallas import tpu as pltpu
from jax.sharding import PartitionSpec as P

HEADS = 12
HEAD_DIM = 64
EPS = 1e-06
MASKED = -1e30
MESH = pl.DeviceIdType.MESH
F32 = jnp.float32
BF16 = jnp.bfloat16
SEQ = 4
HL = HEADS // SEQ
LANES = 128


def ring(s):
    return (s + 1 - 2 * (s % 2), (s + 2) % 4, 3 - s)


class Net:
    def __init__(self, send, recv):
        self.send, self.recv, self.next = send, recv, 0
        self.pending = []

    def slot(self):
        self.next += 1
        return self.next - 1

    def start(self, i, src, dst, device):
        copy = pltpu.make_async_remote_copy(
            src_ref=src,
            dst_ref=dst,
            send_sem=self.send.at[i],
            recv_sem=self.recv.at[i],
            device_id=device,
            device_id_type=MESH,
        )
        copy.start()
        self.pending.append(copy)
        return copy

    def arrived(self, i, dst, device):
        pltpu.make_async_remote_copy(
            src_ref=dst,
            dst_ref=dst,
            send_sem=self.send.at[i],
            recv_sem=self.recv.at[i],
            device_id=device,
            device_id_type=MESH,
        ).wait_recv()

    def drain(self):
        for copy in self.pending:
            copy.wait_send()
        self.pending = []


def gather_kernel(
    zs,
    tok,
    seg,
    pad,
    trip,
    small,
    wo,
    we,
    ws,
    qa_out,
    ka_out,
    v_out,
    lse_out,
    tok_out,
    ctx_out,
    par_out,
    eb_out,
    wo_all,
    we_all,
    ws_all,
    tokbuf,
    wsend,
    wbuf,
    wpad,
    smallbuf,
    qa,
    ka,
    vv,
    qmask,
    kmask,
    ctxsend,
    ctxrecv,
    send,
    recv,
    local,
):
    s = lax.axis_index("seq")
    f = lax.axis_index("fsdp")
    z, c = f // 2, f % 2
    rows, width = tok.shape
    length = rows * SEQ
    part = wsend.shape[1]
    n = trip.shape[0]
    hw = HL * HEAD_DIM
    s1, s2, s3 = ring(s)
    zpeers = [((z + j) % zs, (z - j + zs) % zs) for j in range(1, zs)]
    sib = (s, z * 2 + 1 - c)

    for t in range(SEQ):

        @pl.when(s == t)
        def _(t=t):
            for j in range(3):
                wsend[:, j * hw : (j + 1) * hw] = trip[:, j * width + t * hw : j * width + (t + 1) * hw]

    barrier = pltpu.get_barrier_semaphore()
    partners = [(s1, f), (s2, f), (s3, f), sib] + [(s, zt * 2 + c) for zt, _ in zpeers]
    for partner in partners:
        pl.semaphore_signal(barrier, inc=1, device_id=partner, device_id_type=MESH)
    pl.semaphore_wait(barrier, len(partners))

    net = Net(send, recv)
    half = rows // 2
    lo, hi = pl.ds(0, half), pl.ds(half, half)

    t_1lo, t_1hi, t_2lo, t_2hi, t_3lo, t_3hi = [net.slot() for _ in range(6)]
    net.start(t_1lo, tok.at[lo], tokbuf.at[s, lo], (s1, f))
    net.start(t_2hi, tok.at[hi], tokbuf.at[s, hi], (s2, f))
    w_z = [net.slot() for _ in zpeers]
    p_z = [net.slot() for _ in zpeers]
    w_sib = [net.slot() for _ in range(zs)]
    p_sib = [net.slot() for _ in range(zs)]
    first = []
    for j, (zt, _) in enumerate(zpeers):
        first.append(net.start(w_z[j], wsend, wbuf.at[z, c], (s, zt * 2 + c)))
        net.start(p_z[j], small, smallbuf.at[z, c], (s, zt * 2 + c))
    net.start(w_sib[0], wsend, wbuf.at[z, c], sib)
    net.start(p_sib[0], small, smallbuf.at[z, c], sib)
    net.start(t_1hi, tok.at[hi], tokbuf.at[s, hi], (s1, f))
    net.start(t_2lo, tok.at[lo], tokbuf.at[s, lo], (s2, f))
    wbuf[z, c] = wsend[...]
    smallbuf[z, c] = small[...]
    tokbuf[s] = tok[...]

    row_id = lax.broadcasted_iota(jnp.int32, (LANES, length), 0) - HEAD_DIM
    seg_row = jnp.broadcast_to(seg[...], (LANES, length))
    pad_row = jnp.broadcast_to(pad[...], (LANES, length))
    here = (row_id == seg_row) & (row_id >= 0)
    live_row = row_id == 32
    q_t = jnp.where(live_row, pad_row.astype(F32), jnp.where(here, 1.0, 0.0))
    qmask[...] = q_t.T
    inside = (row_id >= 0) & (row_id < 16)
    k_t = jnp.where(inside & jnp.logical_not(here & (pad_row == 1)), MASKED, 0.0)
    k_t = jnp.where((row_id >= 16) & (row_id < 19), 1.0, k_t)
    kmask[...] = k_t.T.astype(BF16)

    net.arrived(t_1lo, tokbuf.at[s1, lo], (s1, f))
    net.start(t_3lo, tokbuf.at[s1, lo], tokbuf.at[s1, lo], (s2, f))
    net.arrived(t_2hi, tokbuf.at[s2, hi], (s2, f))
    net.start(t_3hi, tokbuf.at[s2, hi], tokbuf.at[s2, hi], (s1, f))

    for j, (_, zf) in enumerate(zpeers):
        net.arrived(w_z[j], wbuf.at[zf, c], (s, zf * 2 + c))
        net.start(w_sib[j + 1], wbuf.at[zf, c], wbuf.at[zf, c], sib)
        net.arrived(p_z[j], smallbuf.at[zf, c], (s, zf * 2 + c))
        net.start(p_sib[j + 1], smallbuf.at[zf, c], smallbuf.at[zf, c], sib)

    weights = ((wo, wo_all), (we, we_all), (ws, ws_all))
    f_z = [[net.slot() for _ in weights] for _ in zpeers]
    for j, (zt, _) in enumerate(zpeers):
        for i, (mine, full) in enumerate(weights):
            net.start(f_z[j][i], mine.at[s], full.at[z, c, s], (s, zt * 2 + c))
    f_sib = [[net.slot() for _ in weights] for _ in range(zs)]
    own = []
    for i, (mine, full) in enumerate(weights):
        net.start(f_sib[0][i], mine, full.at[z, c], sib)
        copy = pltpu.make_async_copy(mine, full.at[z, c], local.at[i])
        copy.start()
        own.append(copy)

    net.arrived(w_sib[0], wbuf.at[z, 1 - c], sib)
    net.arrived(p_sib[0], smallbuf.at[z, 1 - c], sib)
    for j, (_, zf) in enumerate(zpeers):
        net.arrived(w_sib[j + 1], wbuf.at[zf, 1 - c], sib)
        net.arrived(p_sib[j + 1], smallbuf.at[zf, 1 - c], sib)

    for zi in range(zs):
        for ci in range(2):
            fi = zi * 2 + ci
            block = smallbuf[zi, ci].astype(F32)
            par_out[:, fi * n : (fi + 1) * n] = block[:, :n]
            for r in range(4):
                at = fi * 4 * n + r * n
                eb_out[:, at : at + n] = block[8 + r : 9 + r, :n]

    wpad[...] = jnp.zeros_like(wpad)
    for zi in range(zs):
        for ci in range(2):
            fi = zi * 2 + ci
            for k in range(3 * HL):
                wpad[fi * n : (fi + 1) * n, k * LANES : k * LANES + HEAD_DIM] = wbuf[
                    zi, ci, :, k * HEAD_DIM : (k + 1) * HEAD_DIM
                ]
    bias = jnp.zeros((2, HL * LANES), F32)
    zero = jnp.zeros((2, HEAD_DIM), F32)
    for t in range(SEQ):
        pieces = []
        for h in range(HL):
            pieces += [par_out[0:2, t * hw + h * HEAD_DIM : t * hw + (h + 1) * HEAD_DIM], zero]
        bias = jnp.where(s == t, jnp.concatenate(pieces, axis=1), bias)
    lane = lax.broadcasted_iota(jnp.int32, (1, LANES), 1)
    ones_lane = jnp.where((lane == HEAD_DIM) | (lane == HEAD_DIM + 1), 1.0, 0.0)

    tile = min(128, rows)

    def project(block):
        @pl.loop(0, rows // tile)
        def _(i):
            at = pl.multiple_of(i * tile, tile)
            out = pl.multiple_of(block * rows + i * tile, tile)
            mixed = jnp.dot(tokbuf[block, pl.ds(at, tile), :], wpad[...], preferred_element_type=F32)
            qm = qmask[pl.ds(out, tile), :]
            qm = jnp.where(lane < HEAD_DIM + 16, qm, 0.0).astype(BF16)
            km = kmask[pl.ds(out, tile), :]
            for h in range(HL):
                q = mixed[:, h * LANES : (h + 1) * LANES] + bias[0:1, h * LANES : (h + 1) * LANES]
                qa[h, pl.ds(out, tile), :] = q.astype(BF16) * BF16(HEAD_DIM**-0.5) + qm
                k = mixed[:, (HL + h) * LANES : (HL + h + 1) * LANES]
                ka[h, pl.ds(out, tile), :] = k.astype(BF16) + km
                v = mixed[:, (2 * HL + h) * LANES : (2 * HL + h + 1) * LANES]
                v = v + bias[1:2, h * LANES : (h + 1) * LANES] + ones_lane
                vv[h, pl.ds(out, tile), :] = v.astype(BF16)

    project(s)
    net.arrived(t_1hi, tokbuf.at[s1, hi], (s1, f))
    project(s1)
    net.arrived(t_2lo, tokbuf.at[s2, lo], (s2, f))
    project(s2)
    net.arrived(t_3lo, tokbuf.at[s3, lo], (s2, f))
    net.arrived(t_3hi, tokbuf.at[s3, hi], (s1, f))
    project(s3)

    f_1 = [[net.slot() for _ in weights] for _ in zpeers]
    f_2 = [[net.slot() for _ in weights] for _ in zpeers]
    f_3lo = [[net.slot() for _ in weights] for _ in zpeers]
    f_3hi = [[net.slot() for _ in weights] for _ in zpeers]

    def spread(j):
        zf = zpeers[j][1]
        for i, (_, full) in enumerate(weights):
            net.arrived(f_z[j][i], full.at[zf, c, s], (s, zf * 2 + c))
            net.start(f_1[j][i], full.at[zf, c, s], full.at[zf, c, s], (s1, f))
            net.start(f_2[j][i], full.at[zf, c, s], full.at[zf, c, s], (s2, f))

    def halves(full, zf, src, which):
        w = full.shape[-1] // 2
        return full.at[zf, c, src, :, pl.ds(which * w, w)]

    def pass_on(j):
        zf = zpeers[j][1]
        for i, (_, full) in enumerate(weights):
            net.arrived(f_1[j][i], full.at[zf, c, s1], (s1, f))
            net.start(f_3lo[j][i], halves(full, zf, s1, 0), halves(full, zf, s1, 0), (s2, f))
            net.arrived(f_2[j][i], full.at[zf, c, s2], (s2, f))
            net.start(f_3hi[j][i], halves(full, zf, s2, 1), halves(full, zf, s2, 1), (s1, f))

    def finish(j):
        zf = zpeers[j][1]
        for i, (_, full) in enumerate(weights):
            net.arrived(f_3lo[j][i], halves(full, zf, s3, 0), (s2, f))
            net.arrived(f_3hi[j][i], halves(full, zf, s3, 1), (s1, f))
            net.start(f_sib[j + 1][i], full.at[zf, c], full.at[zf, c], sib)

    c_1, c_2, c_3 = [net.slot() for _ in range(3)]
    qt = min(256, rows)

    def attend(block):
        @pl.loop(0, HL)
        def _(h):
            @pl.loop(0, rows // qt)
            def _(i):
                at = pl.multiple_of(block * rows + i * qt, qt)
                scores = lax.dot_general(
                    qa[h, pl.ds(at, qt), :],
                    ka[h],
                    (((1,), (1,)), ((), ())),
                    preferred_element_type=F32,
                )
                top = jnp.max(scores, axis=-1, keepdims=True)
                probs = jnp.exp(scores - top).astype(BF16)
                out = jnp.dot(probs, vv[h], preferred_element_type=F32)
                total = out[:, HEAD_DIM : HEAD_DIM + 1]
                live = qmask[pl.ds(at, qt), HEAD_DIM + 32 : HEAD_DIM + 33]
                ctx = (out * (live / total)).astype(BF16)[:, :HEAD_DIM]
                lse = jnp.where(live > 0.0, top + jnp.log(total), -MASKED)
                lse_out[pl.ds(h, 1), pl.ds(at, qt)] = jnp.broadcast_to(lse, (qt, LANES)).T[0:1]
                here = pl.multiple_of(i * qt, qt)
                per = rows // 2 // qt
                down = pl.multiple_of(rows + (i % per) * qt, qt)

                @pl.when(h == 0)
                def _():
                    ctxsend[block, pl.ds(here, qt), 0:HEAD_DIM] = ctx

                @pl.when(h == 1)
                def _():
                    ctxsend[block, pl.ds(here, qt), HEAD_DIM:LANES] = ctx

                @pl.when((h == 2) & (i < per))
                def _():
                    ctxsend[block, pl.ds(down, qt), 0:HEAD_DIM] = ctx

                @pl.when((h == 2) & (i >= per))
                def _():
                    ctxsend[block, pl.ds(down, qt), HEAD_DIM:LANES] = ctx

    attend(s3)
    net.start(c_3, ctxsend.at[s3], ctxrecv.at[s], (s3, f))
    for j in range(zs - 1):
        spread(j)
    attend(s1)
    net.start(c_1, ctxsend.at[s1], ctxrecv.at[s], (s1, f))
    attend(s2)
    net.start(c_2, ctxsend.at[s2], ctxrecv.at[s], (s2, f))
    for j in range(zs - 1):
        pass_on(j)
    attend(s)
    ctxrecv[s] = ctxsend[s]
    outs = []
    for i, (src, dst) in enumerate(((qa, qa_out), (ka, ka_out), (vv, v_out), (tokbuf, tok_out))):
        copy = pltpu.make_async_copy(src, dst, local.at[3 + i])
        copy.start()
        outs.append(copy)
    net.arrived(c_3, ctxrecv.at[s3], (s3, f))
    net.arrived(c_1, ctxrecv.at[s1], (s1, f))
    net.arrived(c_2, ctxrecv.at[s2], (s2, f))
    for t in range(SEQ):
        at = t * hw
        ctx_out[:, at : at + LANES] = ctxrecv[t, 0:rows, :]
        ctx_out[0:half, at + LANES : at + hw] = ctxrecv[t, rows : rows + half, 0:HEAD_DIM]
        ctx_out[half:rows, at + LANES : at + hw] = ctxrecv[t, rows : rows + half, HEAD_DIM:LANES]
    for j in range(zs - 1):
        finish(j)
    for i, (_, full) in enumerate(weights):
        net.arrived(f_sib[0][i], full.at[z, 1 - c], sib)
        for j, (_, zf) in enumerate(zpeers):
            net.arrived(f_sib[j + 1][i], full.at[zf, 1 - c], sib)
    for copy in own + outs:
        copy.wait()
    net.drain()


def gather_slots(zs):
    p = zs - 1
    return 6 + 2 * p + 2 * zs + 3 * p + 3 * zs + 12 * p + 3


def gather_call(tokens, segment, padding, triple, small, wo, we, ws):
    rows, width = tokens.shape
    length = rows * SEQ
    n = triple.shape[0]
    shards = width // n
    zs = shards // 2
    hw = HL * HEAD_DIM
    ff = we.shape[1]
    slots = gather_slots(zs)
    vm = pl.BlockSpec(memory_space=pltpu.VMEM)
    hbm = pl.BlockSpec(memory_space=pl.ANY)
    q, qs = n // SEQ, ws.shape[0] // SEQ
    out_shape = (
        jax.ShapeDtypeStruct((HL, length, LANES), BF16),
        jax.ShapeDtypeStruct((HL, length, LANES), BF16),
        jax.ShapeDtypeStruct((HL, length, LANES), BF16),
        jax.ShapeDtypeStruct((8, length), F32),
        jax.ShapeDtypeStruct((SEQ, rows, width), BF16),
        jax.ShapeDtypeStruct((rows, width), BF16),
        jax.ShapeDtypeStruct((16, width), F32),
        jax.ShapeDtypeStruct((1, ff), F32),
        jax.ShapeDtypeStruct((zs, 2, SEQ, q, width), BF16),
        jax.ShapeDtypeStruct((zs, 2, SEQ, q, ff), BF16),
        jax.ShapeDtypeStruct((zs, 2, SEQ, qs, width), BF16),
    )
    outs = pl.pallas_call(
        functools.partial(gather_kernel, zs),
        out_shape=out_shape,
        in_specs=[vm, vm, vm, vm, vm, hbm, hbm, hbm],
        out_specs=(hbm, hbm, hbm, vm, hbm, vm, vm, vm, hbm, hbm, hbm),
        scratch_shapes=[
            pltpu.VMEM((SEQ, rows, width), BF16),
            pltpu.VMEM((n, 3 * hw), BF16),
            pltpu.VMEM((zs, 2, n, 3 * hw), BF16),
            pltpu.VMEM((width, 3 * HL * LANES), BF16),
            pltpu.VMEM((zs, 2, 16, LANES), BF16),
            pltpu.VMEM((HL, length, LANES), BF16),
            pltpu.VMEM((HL, length, LANES), BF16),
            pltpu.VMEM((HL, length, LANES), BF16),
            pltpu.VMEM((length, LANES), F32),
            pltpu.VMEM((length, LANES), BF16),
            pltpu.VMEM((SEQ, rows + rows // 2, LANES), BF16),
            pltpu.VMEM((SEQ, rows + rows // 2, LANES), BF16),
            pltpu.SemaphoreType.DMA((slots,)),
            pltpu.SemaphoreType.DMA((slots,)),
            pltpu.SemaphoreType.DMA((8,)),
        ],
        compiler_params=pltpu.CompilerParams(
            collective_id=0, has_side_effects=True, vmem_limit_bytes=60 << 20
        ),
        name="gather_attend",
    )(
        tokens,
        segment,
        padding,
        triple,
        small,
        wo.reshape(SEQ, q, width),
        we.reshape(SEQ, q, ff),
        ws.reshape(SEQ, qs, width),
    )
    qa, ka, vv, lse, tok, ctx, par, eb, wof, wef, wsf = outs
    return (
        qa,
        ka,
        vv,
        lse,
        tok,
        ctx,
        par,
        eb,
        wof.reshape(width, width),
        wef.reshape(width, ff),
        wsf.reshape(ff, width),
    )


def pack_small(query_bias, value_bias, output_bias, first_gain, first_shift, shrink_bias, second_gain, second_shift, expand_bias):
    n = query_bias.shape[0]
    rows = [query_bias, value_bias, output_bias, first_gain, first_shift, shrink_bias, second_gain, second_shift]
    table = jnp.concatenate([jnp.stack(rows), expand_bias.reshape(4, n)], axis=0)
    return jnp.pad(table, ((0, 4), (0, LANES - n)))


def layer_norm(hidden, gain, shift):
    center = hidden - jnp.mean(hidden, axis=-1, keepdims=True)
    spread = jnp.mean(center * center, axis=-1, keepdims=True)
    return center * lax.rsqrt(spread + EPS) * gain + shift


def exact_gelu(values):
    return jax.nn.gelu(values, approximate=False)


def masked_scores(query_rows, keys_all, seg_rows, seg_all, pad_all, scale):
    scores = (
        jnp.einsum("qhd,khd->hqk", query_rows, keys_all, preferred_element_type=jnp.float32) * scale
    )
    allowed = (seg_rows[:, None] == seg_all[None, :]) & (pad_all[None, :] == 1)
    return jnp.where(allowed[None], scores, MASKED)


def attend_backward(
    queries, keys_all, values, grad_context, logsums, seg_all, pad_all, block, scale
):
    length, heads_here, head_size = queries.shape

    def one_block(carry, index):
        grad_keys, grad_values = carry
        start = index * block
        query_rows = lax.dynamic_slice_in_dim(queries, start, block, 0)
        grad_rows = lax.dynamic_slice_in_dim(grad_context, start, block, 0)
        seg_rows = lax.dynamic_slice_in_dim(seg_all, start, block, 0)
        scores = masked_scores(query_rows, keys_all, seg_rows, seg_all, pad_all, scale)
        probs = jnp.exp(scores - logsums[index][..., None])
        grad_probs = jnp.einsum(
            "qhd,khd->hqk", grad_rows, values, preferred_element_type=jnp.float32
        )
        inner = jnp.sum(probs * grad_probs, axis=-1, keepdims=True)
        grad_scores = (probs * (grad_probs - inner)).astype(jnp.bfloat16)
        grad_query = (
            jnp.einsum("hqk,khd->qhd", grad_scores, keys_all, preferred_element_type=jnp.float32)
            * scale
        )
        grad_keys = (
            grad_keys
            + jnp.einsum(
                "hqk,qhd->khd", grad_scores, query_rows, preferred_element_type=jnp.float32
            )
            * scale
        )
        grad_values = grad_values + jnp.einsum(
            "hqk,qhd->khd",
            probs.astype(jnp.bfloat16),
            grad_rows,
            preferred_element_type=jnp.float32,
        )
        return ((grad_keys, grad_values), grad_query.astype(jnp.bfloat16))

    empty = jnp.zeros((length, heads_here, head_size), jnp.float32)
    (grad_keys, grad_values), grad_queries = lax.scan(
        one_block, (empty, empty), jnp.arange(length // block)
    )
    grad_queries = grad_queries.reshape(length, heads_here, head_size)
    return (grad_queries, grad_keys.astype(jnp.bfloat16), grad_values.astype(jnp.bfloat16))


def body(
    tokens,
    segment,
    padding,
    triple_weight,
    query_bias,
    value_bias,
    output_weight,
    output_bias,
    first_gain,
    first_shift,
    expand_weight,
    expand_bias,
    shrink_weight,
    shrink_bias,
    second_gain,
    second_shift,
    cotangent,
):
    groups, rows, width = tokens.shape
    seq_count = lax.axis_size("seq")
    length = rows * seq_count
    heads_here = HEADS // seq_count
    local_width = width // seq_count
    block = min(512, length)
    scale = HEAD_DIM ** (-0.5)
    flat_rows = groups * rows
    small = pack_small(
        query_bias,
        value_bias,
        output_bias,
        first_gain,
        first_shift,
        shrink_bias,
        second_gain,
        second_shift,
        expand_bias,
    )
    qa, ka, vv, lse, tok, context_flat, par, eb, output_full, expand_full, shrink_full = gather_call(
        tokens[0], segment, padding, triple_weight, small, output_weight, expand_weight, shrink_weight
    )
    head_queries = (qa[:, :, :HEAD_DIM] * 8).transpose(1, 0, 2)[None]
    head_keys = ka[:, :, :HEAD_DIM].transpose(1, 0, 2)[None]
    head_values = vv[:, :, :HEAD_DIM].transpose(1, 0, 2)[None]
    logsums = lse[:HL].reshape(HL, length // block, block).transpose(1, 0, 2)[None]
    outbias_full, gain_one, shift_one, shrbias_full, gain_two, shift_two = [par[r] for r in range(2, 8)]
    expbias_full = eb[0]
    flat = tokens.reshape(flat_rows, width)
    attended = jnp.dot(
        context_flat, output_full, preferred_element_type=jnp.float32
    ) + outbias_full.astype(jnp.float32)
    first = flat.astype(jnp.float32) + attended
    normed, first_pull = jax.vjp(
        layer_norm, first, gain_one.astype(jnp.float32), shift_one.astype(jnp.float32)
    )
    normed_low = normed.astype(jnp.bfloat16)
    expand = jnp.dot(
        normed_low, expand_full, preferred_element_type=jnp.float32
    ) + expbias_full.astype(jnp.float32)
    active_full, gelu_pull = jax.vjp(exact_gelu, expand)
    active = active_full.astype(jnp.bfloat16)
    shrink = jnp.dot(active, shrink_full, preferred_element_type=jnp.float32) + shrbias_full.astype(
        jnp.float32
    )
    second = normed + shrink
    result, second_pull = jax.vjp(
        layer_norm, second, gain_two.astype(jnp.float32), shift_two.astype(jnp.float32)
    )
    layer_out = result.astype(jnp.bfloat16).reshape(groups, rows, width)
    back_triple = lax.all_gather(triple_weight, "fsdp", axis=0, tiled=True)
    back_output, back_expand, back_shrink = output_full, expand_full, shrink_full
    grad_out = cotangent.reshape(flat_rows, width).astype(jnp.float32)
    grad_second, second_gain_grad, second_shift_grad = second_pull(grad_out)
    shrink_low = grad_second.astype(jnp.bfloat16)
    shrink_grad = jnp.dot(active.T, shrink_low, preferred_element_type=jnp.float32)
    shrink_bias_grad = jnp.sum(shrink_low, axis=0, dtype=jnp.float32)
    grad_active = jnp.dot(shrink_low, back_shrink.T, preferred_element_type=jnp.float32)
    (grad_expand,) = gelu_pull(grad_active)
    expand_low = grad_expand.astype(jnp.bfloat16)
    expand_grad = jnp.dot(normed_low.T, expand_low, preferred_element_type=jnp.float32)
    expand_bias_grad = jnp.sum(expand_low, axis=0, dtype=jnp.float32)
    grad_normed = grad_second + jnp.dot(
        expand_low, back_expand.T, preferred_element_type=jnp.float32
    )
    grad_first, first_gain_grad, first_shift_grad = first_pull(grad_normed)
    attended_low = grad_first.astype(jnp.bfloat16)
    output_grad = jnp.dot(context_flat.T, attended_low, preferred_element_type=jnp.float32)
    output_bias_grad = jnp.sum(attended_low, axis=0, dtype=jnp.float32)
    grad_context = jnp.dot(attended_low, back_output.T, preferred_element_type=jnp.float32).astype(
        jnp.bfloat16
    )
    head_grads = lax.all_to_all(
        grad_context.reshape(groups, rows, width), "seq", split_axis=2, concat_axis=1, tiled=True
    )
    head_grads = (head_grads * padding.astype(jnp.bfloat16)[..., None]).reshape(
        groups, length, heads_here, HEAD_DIM
    )

    def backward_one(parts):
        return attend_backward(
            parts[0], parts[1], parts[2], parts[3], parts[4], parts[5], parts[6], block, scale
        )

    grad_queries, grad_keys, grad_values = lax.map(
        backward_one, (head_queries, head_keys, head_values, head_grads, logsums, segment, padding)
    )
    token_queries, token_keys, token_values = (
        lax.all_to_all(
            grad_queries.reshape(groups, length, local_width),
            "seq",
            split_axis=1,
            concat_axis=2,
            tiled=True,
        ),
        lax.all_to_all(
            grad_keys.reshape(groups, length, local_width),
            "seq",
            split_axis=1,
            concat_axis=2,
            tiled=True,
        ),
        lax.all_to_all(
            grad_values.reshape(groups, length, local_width),
            "seq",
            split_axis=1,
            concat_axis=2,
            tiled=True,
        ),
    )
    grad_mixed = jnp.concatenate([token_queries, token_keys, token_values], axis=-1).reshape(
        flat_rows, 3 * width
    )
    triple_grad = jnp.dot(flat.T, grad_mixed, preferred_element_type=jnp.float32)
    query_bias_grad = jnp.sum(token_queries.reshape(flat_rows, width), axis=0, dtype=jnp.float32)
    value_bias_grad = jnp.sum(token_values.reshape(flat_rows, width), axis=0, dtype=jnp.float32)
    tokens_grad = grad_first + jnp.dot(
        grad_mixed, back_triple.T, preferred_element_type=jnp.float32
    )
    tokens_grad = tokens_grad.astype(jnp.bfloat16).reshape(groups, rows, width)
    shards = (
        lax.psum_scatter(triple_grad, "fsdp", scatter_dimension=0, tiled=True),
        lax.psum_scatter(query_bias_grad, "fsdp", scatter_dimension=0, tiled=True),
        lax.psum_scatter(value_bias_grad, "fsdp", scatter_dimension=0, tiled=True),
        lax.psum_scatter(output_grad, "fsdp", scatter_dimension=0, tiled=True),
        lax.psum_scatter(output_bias_grad, "fsdp", scatter_dimension=0, tiled=True),
        lax.psum_scatter(first_gain_grad, "fsdp", scatter_dimension=0, tiled=True),
        lax.psum_scatter(first_shift_grad, "fsdp", scatter_dimension=0, tiled=True),
        lax.psum_scatter(expand_grad, "fsdp", scatter_dimension=0, tiled=True),
        lax.psum_scatter(expand_bias_grad, "fsdp", scatter_dimension=0, tiled=True),
        lax.psum_scatter(shrink_grad, "fsdp", scatter_dimension=0, tiled=True),
        lax.psum_scatter(shrink_bias_grad, "fsdp", scatter_dimension=0, tiled=True),
        lax.psum_scatter(second_gain_grad, "fsdp", scatter_dimension=0, tiled=True),
        lax.psum_scatter(second_shift_grad, "fsdp", scatter_dimension=0, tiled=True),
    )
    summed = (
        lax.psum(shards[0].astype(jnp.bfloat16), "seq").astype(jnp.float32),
        lax.psum(shards[1].astype(jnp.bfloat16), "seq").astype(jnp.float32),
        lax.psum(shards[2].astype(jnp.bfloat16), "seq").astype(jnp.float32),
        lax.psum(shards[3].astype(jnp.bfloat16), "seq").astype(jnp.float32),
        lax.psum(shards[4].astype(jnp.bfloat16), "seq").astype(jnp.float32),
        lax.psum(shards[5].astype(jnp.bfloat16), "seq").astype(jnp.float32),
        lax.psum(shards[6].astype(jnp.bfloat16), "seq").astype(jnp.float32),
        lax.psum(shards[7].astype(jnp.bfloat16), "seq").astype(jnp.float32),
        lax.psum(shards[8].astype(jnp.bfloat16), "seq").astype(jnp.float32),
        lax.psum(shards[9].astype(jnp.bfloat16), "seq").astype(jnp.float32),
        lax.psum(shards[10].astype(jnp.bfloat16), "seq").astype(jnp.float32),
        lax.psum(shards[11].astype(jnp.bfloat16), "seq").astype(jnp.float32),
        lax.psum(shards[12].astype(jnp.bfloat16), "seq").astype(jnp.float32),
    )
    return (layer_out, tokens_grad) + tuple(summed)


def solution(mesh):
    return jax.shard_map(
        body,
        mesh=mesh,
        in_specs=(
            P("fsdp", "seq", None),
            P("fsdp", None),
            P("fsdp", None),
            P("fsdp", None),
            P("fsdp"),
            P("fsdp"),
            P("fsdp", None),
            P("fsdp"),
            P("fsdp"),
            P("fsdp"),
            P("fsdp", None),
            P("fsdp"),
            P("fsdp", None),
            P("fsdp"),
            P("fsdp"),
            P("fsdp"),
            P("fsdp", "seq", None),
        ),
        out_specs=(
            P("fsdp", "seq", None),
            P("fsdp", "seq", None),
            P("fsdp", None),
            P("fsdp"),
            P("fsdp"),
            P("fsdp", None),
            P("fsdp"),
            P("fsdp"),
            P("fsdp"),
            P("fsdp", None),
            P("fsdp"),
            P("fsdp", None),
            P("fsdp"),
            P("fsdp"),
            P("fsdp"),
        ),
        check_vma=False,
    )
```

```python
import functools

import jax
import jax.numpy as jnp
from jax import lax
from jax.experimental import pallas as pl
from jax.experimental.pallas import tpu as pltpu
from jax.sharding import PartitionSpec as P

HEADS = 12
HEAD_DIM = 64
EPS = 1e-06
MASKED = -1e30
MESH = pl.DeviceIdType.MESH
F32 = jnp.float32
BF16 = jnp.bfloat16
SEQ = 4
HL = HEADS // SEQ
LANES = 128


def ring(s):
    return (s + 1 - 2 * (s % 2), (s + 2) % 4, 3 - s)


class Net:
    def __init__(self, send, recv):
        self.send, self.recv, self.next = send, recv, 0
        self.pending = []

    def slot(self):
        self.next += 1
        return self.next - 1

    def start(self, i, src, dst, device):
        copy = pltpu.make_async_remote_copy(
            src_ref=src,
            dst_ref=dst,
            send_sem=self.send.at[i],
            recv_sem=self.recv.at[i],
            device_id=device,
            device_id_type=MESH,
        )
        copy.start()
        self.pending.append(copy)
        return copy

    def arrived(self, i, dst, device):
        pltpu.make_async_remote_copy(
            src_ref=dst,
            dst_ref=dst,
            send_sem=self.send.at[i],
            recv_sem=self.recv.at[i],
            device_id=device,
            device_id_type=MESH,
        ).wait_recv()

    def drain(self):
        for copy in self.pending:
            copy.wait_send()
        self.pending = []


def gather_kernel(
    zs,
    tok,
    seg,
    pad,
    trip,
    small,
    wo,
    we,
    ws,
    qa_out,
    ka_out,
    v_out,
    own_out,
    tok_out,
    ctx_out,
    par_out,
    eb_out,
    wo_all,
    we_all,
    ws_all,
    tokbuf,
    wsend,
    wbuf,
    wpad,
    smallbuf,
    qa,
    ka,
    vv,
    qmask,
    kmask,
    ctxsend,
    ctxrecv,
    send,
    recv,
    local,
):
    s = lax.axis_index("seq")
    f = lax.axis_index("fsdp")
    z, c = f // 2, f % 2
    rows, width = tok.shape
    length = rows * SEQ
    part = wsend.shape[1]
    n = trip.shape[0]
    hw = HL * HEAD_DIM
    s1, s2, s3 = ring(s)
    zpeers = [((z + j) % zs, (z - j + zs) % zs) for j in range(1, zs)]
    sib = (s, z * 2 + 1 - c)

    for t in range(SEQ):

        @pl.when(s == t)
        def _(t=t):
            for j in range(3):
                wsend[:, j * hw : (j + 1) * hw] = trip[:, j * width + t * hw : j * width + (t + 1) * hw]

    barrier = pltpu.get_barrier_semaphore()
    partners = [(s1, f), (s2, f), (s3, f), sib] + [(s, zt * 2 + c) for zt, _ in zpeers]
    for partner in partners:
        pl.semaphore_signal(barrier, inc=1, device_id=partner, device_id_type=MESH)
    pl.semaphore_wait(barrier, len(partners))

    net = Net(send, recv)
    half = rows // 2
    lo, hi = pl.ds(0, half), pl.ds(half, half)

    t_1lo, t_1hi, t_2lo, t_2hi, t_3lo, t_3hi = [net.slot() for _ in range(6)]
    net.start(t_1lo, tok.at[lo], tokbuf.at[s, lo], (s1, f))
    net.start(t_2hi, tok.at[hi], tokbuf.at[s, hi], (s2, f))
    w_z = [net.slot() for _ in zpeers]
    p_z = [net.slot() for _ in zpeers]
    w_sib = [net.slot() for _ in range(zs)]
    p_sib = [net.slot() for _ in range(zs)]
    first = []
    for j, (zt, _) in enumerate(zpeers):
        first.append(net.start(w_z[j], wsend, wbuf.at[z, c], (s, zt * 2 + c)))
        net.start(p_z[j], small, smallbuf.at[z, c], (s, zt * 2 + c))
    net.start(w_sib[0], wsend, wbuf.at[z, c], sib)
    net.start(p_sib[0], small, smallbuf.at[z, c], sib)
    net.start(t_1hi, tok.at[hi], tokbuf.at[s, hi], (s1, f))
    net.start(t_2lo, tok.at[lo], tokbuf.at[s, lo], (s2, f))
    wbuf[z, c] = wsend[...]
    smallbuf[z, c] = small[...]
    tokbuf[s] = tok[...]

    row_id = lax.broadcasted_iota(jnp.int32, (LANES, length), 0) - HEAD_DIM
    seg_row = jnp.broadcast_to(seg[...], (LANES, length))
    pad_row = jnp.broadcast_to(pad[...], (LANES, length))
    here = (row_id == seg_row) & (row_id >= 0)
    live_row = row_id == 32
    q_t = jnp.where(live_row, pad_row.astype(F32), jnp.where(here, 1.0, 0.0))
    qmask[...] = q_t.T
    inside = (row_id >= 0) & (row_id < 16)
    k_t = jnp.where(inside & jnp.logical_not(here & (pad_row == 1)), MASKED, 0.0)
    k_t = jnp.where((row_id >= 16) & (row_id < 19), 1.0, k_t)
    kmask[...] = k_t.T.astype(BF16)

    net.arrived(t_1lo, tokbuf.at[s1, lo], (s1, f))
    net.start(t_3lo, tokbuf.at[s1, lo], tokbuf.at[s1, lo], (s2, f))
    net.arrived(t_2hi, tokbuf.at[s2, hi], (s2, f))
    net.start(t_3hi, tokbuf.at[s2, hi], tokbuf.at[s2, hi], (s1, f))

    for j, (_, zf) in enumerate(zpeers):
        net.arrived(w_z[j], wbuf.at[zf, c], (s, zf * 2 + c))
        net.start(w_sib[j + 1], wbuf.at[zf, c], wbuf.at[zf, c], sib)
        net.arrived(p_z[j], smallbuf.at[zf, c], (s, zf * 2 + c))
        net.start(p_sib[j + 1], smallbuf.at[zf, c], smallbuf.at[zf, c], sib)

    weights = ((wo, wo_all), (we, we_all), (ws, ws_all))
    f_z = [[net.slot() for _ in weights] for _ in zpeers]
    for j, (zt, _) in enumerate(zpeers):
        for i, (mine, full) in enumerate(weights):
            net.start(f_z[j][i], mine.at[s], full.at[z, c, s], (s, zt * 2 + c))
    f_sib = [[net.slot() for _ in weights] for _ in range(zs)]
    own = []
    for i, (mine, full) in enumerate(weights):
        net.start(f_sib[0][i], mine, full.at[z, c], sib)
        copy = pltpu.make_async_copy(mine, full.at[z, c], local.at[i])
        copy.start()
        own.append(copy)

    net.arrived(w_sib[0], wbuf.at[z, 1 - c], sib)
    net.arrived(p_sib[0], smallbuf.at[z, 1 - c], sib)
    for j, (_, zf) in enumerate(zpeers):
        net.arrived(w_sib[j + 1], wbuf.at[zf, 1 - c], sib)
        net.arrived(p_sib[j + 1], smallbuf.at[zf, 1 - c], sib)

    for zi in range(zs):
        for ci in range(2):
            fi = zi * 2 + ci
            block = smallbuf[zi, ci].astype(F32)
            par_out[:, fi * n : (fi + 1) * n] = block[:, :n]
            for r in range(4):
                at = fi * 4 * n + r * n
                eb_out[:, at : at + n] = block[8 + r : 9 + r, :n]

    wpad[...] = jnp.zeros_like(wpad)
    for zi in range(zs):
        for ci in range(2):
            fi = zi * 2 + ci
            for k in range(3 * HL):
                wpad[fi * n : (fi + 1) * n, k * LANES : k * LANES + HEAD_DIM] = wbuf[
                    zi, ci, :, k * HEAD_DIM : (k + 1) * HEAD_DIM
                ]
    bias = jnp.zeros((2, HL * LANES), F32)
    zero = jnp.zeros((2, HEAD_DIM), F32)
    for t in range(SEQ):
        pieces = []
        for h in range(HL):
            pieces += [par_out[0:2, t * hw + h * HEAD_DIM : t * hw + (h + 1) * HEAD_DIM], zero]
        bias = jnp.where(s == t, jnp.concatenate(pieces, axis=1), bias)
    lane = lax.broadcasted_iota(jnp.int32, (1, LANES), 1)
    ones_lane = jnp.where((lane == HEAD_DIM) | (lane == HEAD_DIM + 1), 1.0, 0.0)

    tile = min(128, rows)

    def project(block):
        @pl.loop(0, rows // tile)
        def _(i):
            at = pl.multiple_of(i * tile, tile)
            out = pl.multiple_of(block * rows + i * tile, tile)
            mixed = jnp.dot(tokbuf[block, pl.ds(at, tile), :], wpad[...], preferred_element_type=F32)
            qm = qmask[pl.ds(out, tile), :]
            qm = jnp.where(lane < HEAD_DIM + 16, qm, 0.0).astype(BF16)
            km = kmask[pl.ds(out, tile), :]
            for h in range(HL):
                q = mixed[:, h * LANES : (h + 1) * LANES] + bias[0:1, h * LANES : (h + 1) * LANES]
                qa[h, pl.ds(out, tile), :] = q.astype(BF16) * BF16(HEAD_DIM**-0.5) + qm
                k = mixed[:, (HL + h) * LANES : (HL + h + 1) * LANES]
                ka[h, pl.ds(out, tile), :] = k.astype(BF16) + km
                v = mixed[:, (2 * HL + h) * LANES : (2 * HL + h + 1) * LANES]
                v = v + bias[1:2, h * LANES : (h + 1) * LANES] + ones_lane
                vv[h, pl.ds(out, tile), :] = v.astype(BF16)

    project(s)
    net.arrived(t_1hi, tokbuf.at[s1, hi], (s1, f))
    project(s1)
    net.arrived(t_2lo, tokbuf.at[s2, lo], (s2, f))
    project(s2)
    net.arrived(t_3lo, tokbuf.at[s3, lo], (s2, f))
    net.arrived(t_3hi, tokbuf.at[s3, hi], (s1, f))
    project(s3)

    f_1 = [[net.slot() for _ in weights] for _ in zpeers]
    f_2 = [[net.slot() for _ in weights] for _ in zpeers]
    f_3lo = [[net.slot() for _ in weights] for _ in zpeers]
    f_3hi = [[net.slot() for _ in weights] for _ in zpeers]

    def spread(j):
        zf = zpeers[j][1]
        for i, (_, full) in enumerate(weights):
            net.arrived(f_z[j][i], full.at[zf, c, s], (s, zf * 2 + c))
            net.start(f_1[j][i], full.at[zf, c, s], full.at[zf, c, s], (s1, f))
            net.start(f_2[j][i], full.at[zf, c, s], full.at[zf, c, s], (s2, f))

    def halves(full, zf, src, which):
        w = full.shape[-1] // 2
        return full.at[zf, c, src, :, pl.ds(which * w, w)]

    def pass_on(j):
        zf = zpeers[j][1]
        for i, (_, full) in enumerate(weights):
            net.arrived(f_1[j][i], full.at[zf, c, s1], (s1, f))
            net.start(f_3lo[j][i], halves(full, zf, s1, 0), halves(full, zf, s1, 0), (s2, f))
            net.arrived(f_2[j][i], full.at[zf, c, s2], (s2, f))
            net.start(f_3hi[j][i], halves(full, zf, s2, 1), halves(full, zf, s2, 1), (s1, f))

    def finish(j):
        zf = zpeers[j][1]
        for i, (_, full) in enumerate(weights):
            net.arrived(f_3lo[j][i], halves(full, zf, s3, 0), (s2, f))
            net.arrived(f_3hi[j][i], halves(full, zf, s3, 1), (s1, f))
            net.start(f_sib[j + 1][i], full.at[zf, c], full.at[zf, c], sib)

    c_1, c_2, c_3 = [net.slot() for _ in range(3)]
    qt = min(256, rows)

    def attend(block):
        @pl.loop(0, HL)
        def _(h):
            @pl.loop(0, rows // qt)
            def _(i):
                at = pl.multiple_of(block * rows + i * qt, qt)
                scores = lax.dot_general(
                    qa[h, pl.ds(at, qt), :],
                    ka[h],
                    (((1,), (1,)), ((), ())),
                    preferred_element_type=F32,
                )
                top = jnp.max(scores, axis=-1, keepdims=True)
                probs = jnp.exp(scores - top).astype(BF16)
                out = jnp.dot(probs, vv[h], preferred_element_type=F32)
                total = out[:, HEAD_DIM : HEAD_DIM + 1]
                live = qmask[pl.ds(at, qt), HEAD_DIM + 32 : HEAD_DIM + 33]
                ctx = (out * (live / total)).astype(BF16)[:, :HEAD_DIM]
                lse = jnp.where(live > 0.0, top + jnp.log(total), -MASKED)
                lse = -lse
                hi = lse.astype(BF16).astype(F32)
                mid = (lse - hi).astype(BF16).astype(F32)
                rest = lse - hi - mid
                base = HEAD_DIM + 16
                extra = jnp.where(lane == base, hi, jnp.where(lane == base + 1, mid, jnp.where(lane == base + 2, rest, 0.0)))
                qa[h, pl.ds(at, qt), :] = qa[h, pl.ds(at, qt), :] + extra.astype(BF16)
                per = half // qt
                down = pl.multiple_of((i % per) * qt, qt)

                @pl.when(i < per)
                def _():
                    ctxsend[block, h, pl.ds(down, qt), 0:HEAD_DIM] = ctx

                @pl.when(i >= per)
                def _():
                    ctxsend[block, h, pl.ds(down, qt), HEAD_DIM:LANES] = ctx

    attend(s3)
    net.start(c_3, ctxsend.at[s3], ctxrecv.at[s], (s3, f))
    for j in range(zs - 1):
        spread(j)
    attend(s1)
    net.start(c_1, ctxsend.at[s1], ctxrecv.at[s], (s1, f))
    attend(s2)
    net.start(c_2, ctxsend.at[s2], ctxrecv.at[s], (s2, f))
    for j in range(zs - 1):
        pass_on(j)
    attend(s)
    ctxrecv[s] = ctxsend[s]
    outs = []
    for i, (src, dst) in enumerate(((qa, qa_out), (ka, ka_out), (vv, v_out), (tokbuf, tok_out), (ctxsend, own_out))):
        copy = pltpu.make_async_copy(src, dst, local.at[3 + i])
        copy.start()
        outs.append(copy)
    net.arrived(c_3, ctxrecv.at[s3], (s3, f))
    net.arrived(c_1, ctxrecv.at[s1], (s1, f))
    net.arrived(c_2, ctxrecv.at[s2], (s2, f))
    for t in range(SEQ):
        for h in range(HL):
            at = t * hw + h * HEAD_DIM
            ctx_out[0:half, at : at + HEAD_DIM] = ctxrecv[t, h, :, 0:HEAD_DIM]
            ctx_out[half:rows, at : at + HEAD_DIM] = ctxrecv[t, h, :, HEAD_DIM:LANES]
    for j in range(zs - 1):
        finish(j)
    for i, (_, full) in enumerate(weights):
        net.arrived(f_sib[0][i], full.at[z, 1 - c], sib)
        for j, (_, zf) in enumerate(zpeers):
            net.arrived(f_sib[j + 1][i], full.at[zf, 1 - c], sib)
    for copy in own + outs:
        copy.wait()
    net.drain()


def gather_slots(zs):
    p = zs - 1
    return 6 + 2 * p + 2 * zs + 3 * p + 3 * zs + 12 * p + 3


def gather_call(tokens, segment, padding, triple, small, wo, we, ws):
    rows, width = tokens.shape
    length = rows * SEQ
    n = triple.shape[0]
    shards = width // n
    zs = shards // 2
    hw = HL * HEAD_DIM
    ff = we.shape[1]
    slots = gather_slots(zs)
    vm = pl.BlockSpec(memory_space=pltpu.VMEM)
    hbm = pl.BlockSpec(memory_space=pl.ANY)
    q, qs = n // SEQ, ws.shape[0] // SEQ
    out_shape = (
        jax.ShapeDtypeStruct((HL, length, LANES), BF16),
        jax.ShapeDtypeStruct((HL, length, LANES), BF16),
        jax.ShapeDtypeStruct((HL, length, LANES), BF16),
        jax.ShapeDtypeStruct((SEQ, HL, rows // 2, LANES), BF16),
        jax.ShapeDtypeStruct((SEQ, rows, width), BF16),
        jax.ShapeDtypeStruct((rows, width), BF16),
        jax.ShapeDtypeStruct((16, width), F32),
        jax.ShapeDtypeStruct((1, ff), F32),
        jax.ShapeDtypeStruct((zs, 2, SEQ, q, width), BF16),
        jax.ShapeDtypeStruct((zs, 2, SEQ, q, ff), BF16),
        jax.ShapeDtypeStruct((zs, 2, SEQ, qs, width), BF16),
    )
    outs = pl.pallas_call(
        functools.partial(gather_kernel, zs),
        out_shape=out_shape,
        in_specs=[vm, vm, vm, vm, vm, hbm, hbm, hbm],
        out_specs=(hbm, hbm, hbm, hbm, hbm, vm, vm, vm, hbm, hbm, hbm),
        scratch_shapes=[
            pltpu.VMEM((SEQ, rows, width), BF16),
            pltpu.VMEM((n, 3 * hw), BF16),
            pltpu.VMEM((zs, 2, n, 3 * hw), BF16),
            pltpu.VMEM((width, 3 * HL * LANES), BF16),
            pltpu.VMEM((zs, 2, 16, LANES), BF16),
            pltpu.VMEM((HL, length, LANES), BF16),
            pltpu.VMEM((HL, length, LANES), BF16),
            pltpu.VMEM((HL, length, LANES), BF16),
            pltpu.VMEM((length, LANES), F32),
            pltpu.VMEM((length, LANES), BF16),
            pltpu.VMEM((SEQ, HL, rows // 2, LANES), BF16),
            pltpu.VMEM((SEQ, HL, rows // 2, LANES), BF16),
            pltpu.SemaphoreType.DMA((slots,)),
            pltpu.SemaphoreType.DMA((slots,)),
            pltpu.SemaphoreType.DMA((8,)),
        ],
        compiler_params=pltpu.CompilerParams(
            collective_id=0, has_side_effects=True, vmem_limit_bytes=60 << 20
        ),
        name="gather_attend",
    )(
        tokens,
        segment,
        padding,
        triple,
        small,
        wo.reshape(SEQ, q, width),
        we.reshape(SEQ, q, ff),
        ws.reshape(SEQ, qs, width),
    )
    qa, ka, vv, own, tok, ctx, par, eb, wof, wef, wsf = outs
    return (
        qa,
        ka,
        vv,
        own,
        tok,
        ctx,
        par,
        eb,
        wof.reshape(width, width),
        wef.reshape(width, ff),
        wsf.reshape(ff, width),
    )


def pack_small(query_bias, value_bias, output_bias, first_gain, first_shift, shrink_bias, second_gain, second_shift, expand_bias):
    n = query_bias.shape[0]
    rows = [query_bias, value_bias, output_bias, first_gain, first_shift, shrink_bias, second_gain, second_shift]
    table = jnp.concatenate([jnp.stack(rows), expand_bias.reshape(4, n)], axis=0)
    return jnp.pad(table, ((0, 4), (0, LANES - n)))


def collect_kernel(
    zs,
    qa_hbm,
    ka_hbm,
    v_hbm,
    own_hbm,
    tok_hbm,
    trip,
    dctx,
    gfirst,
    vecs,
    ebg,
    go,
    ge,
    gs,
    tg_out,
    trip_out,
    bias_out,
    small_out,
    go_out,
    ge_out,
    gs_out,
    qa,
    ka,
    vv,
    own,
    tok,
    tok_t,
    k_t,
    dsend,
    drecv,
    da,
    dq_t,
    acc_k,
    acc_v,
    gm,
    gsend,
    grecv,
    gmr,
    wland,
    wfull,
    tsend,
    tcore,
    tz,
    tfin,
    svec,
    svcore,
    svz,
    svseq,
    ao,
    ae,
    a_s,
    co,
    ce,
    cs,
    xo,
    xe,
    xs,
    yo,
    ye,
    ys,
    x2o,
    x2e,
    x2s,
    y2o,
    y2e,
    y2s,
    zo,
    ze,
    zsm,
    fo,
    fe,
    fs,
    send,
    recv,
    local,
):
    s = lax.axis_index("seq")
    f = lax.axis_index("fsdp")
    z, c = f // 2, f % 2
    rows, width = dctx.shape
    half = rows // 2
    length = rows * SEQ
    n = trip.shape[0]
    hw = HL * HEAD_DIM
    s1, s2, s3 = ring(s)
    zpeers = [((z + j) % zs, (z - j + zs) % zs) for j in range(1, zs)]
    sib = (s, z * 2 + 1 - c)
    net = Net(send, recv)
    lane = lax.broadcasted_iota(jnp.int32, (1, LANES), 1)

    loads = []
    pairs = ((qa_hbm, qa), (ka_hbm, ka), (v_hbm, vv), (own_hbm, own), (tok_hbm, tok))
    grads = ((go, ao), (ge, ae), (gs, a_s))
    for i, (src, dst) in enumerate(pairs):
        copy = pltpu.make_async_copy(src, dst, local.at[i])
        copy.start()
        loads.append(copy)
    for i, (src, dst) in enumerate(grads):
        copy = pltpu.make_async_copy(src.at[:, c], dst, local.at[5 + i])
        copy.start()
        loads.append(copy)

    for t in range(SEQ):
        for h in range(HL):
            at = t * hw + h * HEAD_DIM
            dsend[t, h, :, 0:HEAD_DIM] = dctx[0:half, at : at + HEAD_DIM]
            dsend[t, h, :, HEAD_DIM:LANES] = dctx[half:rows, at : at + HEAD_DIM]

    barrier = pltpu.get_barrier_semaphore()
    partners = [(s1, f), (s2, f), (s3, f), sib] + [(s, zt * 2 + c) for zt, _ in zpeers]
    for partner in partners:
        pl.semaphore_signal(barrier, inc=1, device_id=partner, device_id_type=MESH)
    pl.semaphore_wait(barrier, len(partners))

    d_sem = [[net.slot() for _ in range(3)] for _ in range(HL)]
    for h in range(HL):
        for k, peer in enumerate((s3, s1, s2)):
            net.start(d_sem[h][k], dsend.at[peer, h], drecv.at[s, h], (peer, f))
    drecv[s] = dsend[s]
    order = (2, 1, 0)
    srcs, mine, core = (go, ge, gs), (ao, ae, a_s), (co, ce, cs)
    c_sem = [net.slot() for _ in range(3)]
    for i in order:
        net.start(c_sem[i], srcs[i].at[:, 1 - c], core[i], sib)
    v_core = net.slot()
    v_z = [net.slot() for _ in zpeers]
    v_seq = [net.slot() for _ in range(3)]
    for zi in range(zs):
        for ci in range(2):
            fi = zi * 2 + ci
            svec[ci, zi] = jnp.zeros((16, LANES), F32)
            svec[ci, zi, 0:8, 0:n] = vecs[:, fi * n : (fi + 1) * n]
            for r in range(4):
                at = fi * 4 * n + r * n
                svec[ci, zi, 8 + r : 9 + r, 0:n] = ebg[:, at : at + n]
    net.start(v_core, svec.at[1 - c], svcore, sib)
    w_z = [net.slot() for _ in zpeers]
    w_sib = [net.slot() for _ in range(zs)]
    for j, (zt, _) in enumerate(zpeers):
        net.start(w_z[j], trip, wland.at[z, c], (s, zt * 2 + c))
    net.start(w_sib[0], trip, wland.at[z, c], sib)
    wland[z, c] = trip[...]

    xr, yr, x2r, y2r, zr, fin = (xo, xe, xs), (yo, ye, ys), (x2o, x2e, x2s), (y2o, y2e, y2s), (zo, ze, zsm), (fo, fe, fs)
    x_sem = [[net.slot() for _ in range(4)] for _ in range(3)]
    x2_sem = [[net.slot() for _ in range(2)] for _ in range(3)]
    z_sem = [[net.slot() for _ in zpeers] for _ in range(3)]
    a_sem = [[net.slot() for _ in range(4)] for _ in range(3)]

    def cols(i, which):
        w = mine[i].shape[-1] // 2
        return pl.ds(which * w, w)

    def plane_start(i):
        loads[5 + i].wait()
        net.arrived(c_sem[i], core[i], sib)

        @pl.loop(0, zs * SEQ)
        def _(k):
            zi, qi = k // SEQ, k % SEQ
            mine[i][zi, qi] = (mine[i][zi, qi].astype(F32) + core[i][zi, qi].astype(F32)).astype(BF16)

        x, y = cols(i, 0), cols(i, 1)
        net.start(x_sem[i][0], mine[i].at[:, s3, :, x], xr[i].at[:, 1], (s1, f))
        net.start(x_sem[i][2], mine[i].at[:, s3, :, y], yr[i].at[:, 1], (s2, f))
        net.start(x_sem[i][1], mine[i].at[:, s1, :, x], xr[i].at[:, 0], (s1, f))
        net.start(x_sem[i][3], mine[i].at[:, s2, :, y], yr[i].at[:, 0], (s2, f))

    def add_into(i, part, qi, which, from_ref):
        w = mine[i].shape[-1] // 2

        @pl.loop(0, zs)
        def _(zi):
            a = mine[i][zi, qi, :, which * w : (which + 1) * w].astype(F32)
            b = (from_ref[zi] if part is None else from_ref[zi, part]).astype(F32)
            mine[i][zi, qi, :, which * w : (which + 1) * w] = (a + b).astype(BF16)

    def plane_second(i):
        net.arrived(x_sem[i][0], xr[i].at[:, 1], (s1, f))
        add_into(i, 1, s2, 0, xr[i])
        net.start(x2_sem[i][0], mine[i].at[:, s2, :, cols(i, 0)], x2r[i], (s2, f))
        net.arrived(x_sem[i][2], yr[i].at[:, 1], (s2, f))
        add_into(i, 1, s1, 1, yr[i])
        net.start(x2_sem[i][1], mine[i].at[:, s1, :, cols(i, 1)], y2r[i], (s1, f))
        net.arrived(x_sem[i][1], xr[i].at[:, 0], (s1, f))
        add_into(i, 0, s, 0, xr[i])
        net.arrived(x_sem[i][3], yr[i].at[:, 0], (s2, f))
        add_into(i, 0, s, 1, yr[i])

    def along_z(i):
        net.arrived(x2_sem[i][0], x2r[i], (s2, f))
        add_into(i, None, s, 0, x2r[i])
        net.arrived(x2_sem[i][1], y2r[i], (s1, f))
        add_into(i, None, s, 1, y2r[i])
        for j, (zt, _) in enumerate(zpeers):
            net.start(z_sem[i][j], mine[i].at[zt, s], zr[i].at[j], (s, zt * 2 + c))

    def own_rows(i):
        total = mine[i][z, s].astype(F32)
        for j, (_, zf) in enumerate(zpeers):
            net.arrived(z_sem[i][j], zr[i].at[j], (s, zf * 2 + c))
            total = total + zr[i][j].astype(F32)
        fin[i][s] = total.astype(BF16)
        net.start(a_sem[i][0], fin[i].at[s], fin[i].at[s], (s1, f))
        net.start(a_sem[i][1], fin[i].at[s], fin[i].at[s], (s2, f))

    def spread(i):
        net.arrived(a_sem[i][0], fin[i].at[s1], (s1, f))
        net.start(a_sem[i][2], fin[i].at[s1, :, cols(i, 0)], fin[i].at[s1, :, cols(i, 0)], (s2, f))
        net.arrived(a_sem[i][1], fin[i].at[s2], (s2, f))
        net.start(a_sem[i][3], fin[i].at[s2, :, cols(i, 1)], fin[i].at[s2, :, cols(i, 1)], (s1, f))

    final_out = (go_out, ge_out, gs_out)

    def spread_end(i):
        net.arrived(a_sem[i][2], fin[i].at[s3, :, cols(i, 0)], (s2, f))
        net.arrived(a_sem[i][3], fin[i].at[s3, :, cols(i, 1)], (s1, f))
        copy = pltpu.make_async_copy(fin[i], final_out[i], local.at[5 + i])
        copy.start()
        return copy

    gm[...] = jnp.zeros_like(gm)
    plane_start(2)
    for copy in loads[:5]:
        copy.wait()

    @pl.loop(0, HL)
    def _(h):
        k_t[h] = ka[h].astype(F32).T[0:HEAD_DIM].astype(BF16)

    @pl.loop(0, SEQ)
    def _(t):
        at = pl.multiple_of(t * rows, rows)
        tok_t[:, pl.ds(at, rows)] = tok[t].astype(F32).T.astype(BF16)

    plane_start(1)
    plane_start(0)

    net.arrived(v_core, svcore, sib)
    svec[c] = svec[c] + svcore[...]
    for j, (zt, _) in enumerate(zpeers):
        net.start(v_z[j], svec.at[c, zt], svz.at[j], (s, zt * 2 + c))

    for j, (_, zf) in enumerate(zpeers):
        net.arrived(w_z[j], wland.at[zf, c], (s, zf * 2 + c))
        net.start(w_sib[j + 1], wland.at[zf, c], wland.at[zf, c], sib)

    g_sem = [[net.slot() for _ in range(3)] for _ in range(HL)]
    tc_sem = [net.slot() for _ in range(HL)]
    tz_sem = [[net.slot() for _ in zpeers] for _ in range(HL)]
    ts_sem = [[net.slot() for _ in range(3)] for _ in range(HL)]

    def prepare(h):
        for k, peer in enumerate((s3, s1, s2)):
            net.arrived(d_sem[h][k], drecv.at[peer, h], (peer, f))

        @pl.loop(0, SEQ)
        def _(t):
            grad = drecv[t, h].astype(F32)
            prod = grad * own[t, h].astype(F32)
            left = lane < HEAD_DIM
            for k in range(2):
                inner = -jnp.sum(jnp.where(left if k == 0 else jnp.logical_not(left), prod, 0.0), axis=-1, keepdims=True)
                hi = inner.astype(BF16).astype(F32)
                here = grad if k == 0 else pltpu.roll(grad, HEAD_DIM, 1)
                here = jnp.where(left, here, jnp.where(lane == HEAD_DIM, hi, jnp.where(lane == HEAD_DIM + 1, inner - hi, 0.0)))
                at = pl.multiple_of(t * rows + k * half, half)
                da[pl.ds(at, half), :] = here.astype(BF16)

        dq_t[...] = jnp.zeros_like(dq_t)

    def key_block(h, r):
        acc_k[...] = jnp.zeros_like(acc_k)
        acc_v[...] = jnp.zeros_like(acc_v)
        keys = pl.multiple_of(r * rows, rows)
        nt = (((1,), (1,)), ((), ()))

        @pl.loop(0, length // QB)
        def _(i):
            at = pl.multiple_of(i * QB, QB)
            q = qa[h, pl.ds(at, QB), :]
            grad = da[pl.ds(at, QB), :]
            probs = jnp.exp(lax.dot_general(ka[h, pl.ds(keys, rows), :], q, nt, preferred_element_type=F32))
            inner = lax.dot_general(vv[h, pl.ds(keys, rows), :], grad, nt, preferred_element_type=F32)
            ds = (probs * inner).astype(BF16)
            acc_v[...] += jnp.dot(probs.astype(BF16), grad, preferred_element_type=F32)
            acc_k[...] += jnp.dot(ds, q, preferred_element_type=F32)
            dq_t[:, pl.ds(at, QB)] += jnp.dot(k_t[h, :, pl.ds(keys, rows)], ds, preferred_element_type=F32)

        gm[pl.ds(keys, rows), HEAD_DIM:LANES] = acc_k[:, 0:HEAD_DIM].astype(BF16)
        gm[pl.ds(keys, rows), LANES : LANES + HEAD_DIM] = acc_v[:, 0:HEAD_DIM].astype(BF16)

    rt = tsend.shape[3]
    vrow = n + n // 2
    brow = rt - 16

    def head_done(h):
        @pl.loop(0, SEQ)
        def _(t):
            at = pl.multiple_of(t * rows, rows)
            dq = (dq_t[:, pl.ds(at, rows)].T * (HEAD_DIM**-0.5)).astype(BF16)
            gm[pl.ds(at, rows), 0:HEAD_DIM] = dq
            for k in range(3):
                for p in range(2):
                    piece = gm[pl.ds(at + p * half, half), k * HEAD_DIM : (k + 1) * HEAD_DIM]
                    gsend[h, t, k, :, p * HEAD_DIM : (p + 1) * HEAD_DIM] = piece

        for k, peer in enumerate((s3, s1, s2)):
            net.start(g_sem[h][k], gsend.at[h, peer], grecv.at[h, s], (peer, f))
        grecv[h, s] = gsend[h, s]
        sums = jnp.sum(gm[...].astype(F32), axis=0, keepdims=True).astype(BF16)
        for zi in range(zs):
            for ci in range(2):
                fi = zi * 2 + ci
                grad = jnp.dot(tok_t[fi * n : (fi + 1) * n, :], gm[...], preferred_element_type=F32).astype(BF16)
                tsend[h, ci, zi, 0:n, :] = grad[:, 0:LANES]
                tsend[h, ci, zi, n:vrow, 0:HEAD_DIM] = grad[0 : n // 2, LANES : LANES + HEAD_DIM]
                tsend[h, ci, zi, n:vrow, HEAD_DIM:LANES] = grad[n // 2 : n, LANES : LANES + HEAD_DIM]
                tsend[h, ci, zi, brow:rt, :] = jnp.broadcast_to(sums[:, 0:LANES], (16, LANES))
                tsend[h, ci, zi, brow + 8 : rt, :] = jnp.broadcast_to(sums[:, LANES : 2 * LANES], (8, LANES))
        net.start(tc_sem[h], tsend.at[h, 1 - c], tcore.at[h], sib)

    def triple_z(h):
        net.arrived(tc_sem[h], tcore.at[h], sib)
        tsend[h, c] = (tsend[h, c].astype(F32) + tcore[h].astype(F32)).astype(BF16)
        for j, (zt, _) in enumerate(zpeers):
            net.start(tz_sem[h][j], tsend.at[h, c, zt], tz.at[h, j], (s, zt * 2 + c))

    def triple_own(h):
        total = tsend[h, c, z].astype(F32)
        for j, (_, zf) in enumerate(zpeers):
            net.arrived(tz_sem[h][j], tz.at[h, j], (s, zf * 2 + c))
            total = total + tz[h, j].astype(F32)
        tfin[h, s] = total.astype(BF16)
        for k, peer in enumerate((s3, s1, s2)):
            net.start(ts_sem[h][k], tfin.at[h, s], tfin.at[h, s], (peer, f))

    def rows_in(h):
        for k, peer in enumerate((s3, s1, s2)):
            net.arrived(g_sem[h][k], grecv.at[h, peer], (peer, f))
        for t in range(SEQ):
            for k in range(3):
                at = k * width + t * hw + h * HEAD_DIM
                gmr[0:half, at : at + HEAD_DIM] = grecv[h, t, k, :, 0:HEAD_DIM]
                gmr[half:rows, at : at + HEAD_DIM] = grecv[h, t, k, :, HEAD_DIM:LANES]

    def attend_back(h):
        @pl.loop(0, SEQ)
        def _(r):
            key_block(h, r)

    prepare(0)
    attend_back(0)
    head_done(0)
    plane_second(2)
    plane_second(1)
    prepare(1)
    attend_back(1)
    head_done(1)
    along_z(2)
    plane_second(0)
    triple_z(0)
    total = svec[c, z]
    for j, (_, zf) in enumerate(zpeers):
        net.arrived(v_z[j], svz.at[j], (s, zf * 2 + c))
        total = total + svz[j]
    svseq[s] = total
    for k, peer in enumerate((s3, s1, s2)):
        net.start(v_seq[k], svseq.at[s], svseq.at[s], (peer, f))
    along_z(1)
    prepare(2)
    attend_back(2)
    head_done(2)
    own_rows(2)
    along_z(0)
    triple_z(1)
    triple_own(0)
    rows_in(0)
    net.arrived(w_sib[0], wland.at[z, 1 - c], sib)
    for j, (_, zf) in enumerate(zpeers):
        net.arrived(w_sib[j + 1], wland.at[zf, 1 - c], sib)
    for zi in range(zs):
        for ci in range(2):
            fi = zi * 2 + ci
            wfull[fi * n : (fi + 1) * n, :] = wland[zi, ci]
    own_rows(1)
    triple_z(2)
    triple_own(1)
    spread(2)
    own_rows(0)
    rows_in(1)
    spread(1)
    triple_own(2)
    spread(0)
    rows_in(2)
    tile = min(128, rows)

    @pl.loop(0, rows // tile)
    def _(i):
        at = pl.multiple_of(i * tile, tile)
        back = lax.dot_general(
            gmr[pl.ds(at, tile), :], wfull[...], (((1,), (1,)), ((), ())), preferred_element_type=F32
        )
        tg_out[pl.ds(at, tile), :] = (gfirst[pl.ds(at, tile), :] + back).astype(BF16)

    copies = [spread_end(2), spread_end(1)]
    for k, peer in enumerate((s3, s1, s2)):
        net.arrived(v_seq[k], svseq.at[peer], (peer, f))
    small_out[...] = svseq[0] + svseq[1] + svseq[2] + svseq[3]
    for h in range(HL):
        for k, peer in enumerate((s3, s1, s2)):
            net.arrived(ts_sem[h][k], tfin.at[h, peer], (peer, f))
    q_row, v_row = [], []
    for t in range(SEQ):
        for h in range(HL):
            at = t * hw + h * HEAD_DIM
            block = tfin[h, t].astype(F32)
            trip_out[:, at : at + HEAD_DIM] = block[0:n, 0:HEAD_DIM]
            trip_out[:, width + at : width + at + HEAD_DIM] = block[0:n, HEAD_DIM:LANES]
            trip_out[0 : n // 2, 2 * width + at : 2 * width + at + HEAD_DIM] = block[n:vrow, 0:HEAD_DIM]
            trip_out[n // 2 : n, 2 * width + at : 2 * width + at + HEAD_DIM] = block[n:vrow, HEAD_DIM:LANES]
            q_row.append(block[brow : brow + 1, 0:HEAD_DIM])
            v_row.append(block[brow + 8 : brow + 9, 0:HEAD_DIM])
    q_row, v_row = jnp.concatenate(q_row, axis=1), jnp.concatenate(v_row, axis=1)
    bias_out[...] = jnp.zeros_like(bias_out)
    for fi in range(2 * zs):

        @pl.when(f == fi)
        def _(fi=fi):
            bias_out[0:1, 0:n] = q_row[:, fi * n : (fi + 1) * n]
            bias_out[1:2, 0:n] = v_row[:, fi * n : (fi + 1) * n]

    copies.append(spread_end(0))
    for copy in copies:
        copy.wait()
    net.drain()


QB = 512


def collect_call(qa, ka, vv, own, tok, triple, dctx, gfirst, vecs, ebg, go, ge, gs):
    rows, width = dctx.shape
    length = rows * SEQ
    n = triple.shape[0]
    zs = width // n // 2
    p = zs - 1
    ff = ge.shape[1]
    q, qs = n // SEQ, ff // (2 * zs) // SEQ
    rt = (n + n // 2 + 15) // 16 * 16 + 16
    half = rows // 2
    slots = 3 * HL + 3 + 1 + p + 3 + p + zs + 3 * (4 + 2 + p + 4) + HL * (3 + 1 + p + 3)
    vm = pl.BlockSpec(memory_space=pltpu.VMEM)
    hbm = pl.BlockSpec(memory_space=pl.ANY)

    def block(a, b):
        return (a, b) if a % 8 == 0 else (a * b // 256, 256)

    shapes = (block(q, width), block(q, ff), block(qs, width))

    def per_weight(make):
        return [pltpu.VMEM(make(a, b), BF16) for a, b in shapes]

    return pl.pallas_call(
        functools.partial(collect_kernel, zs),
        out_shape=(
            jax.ShapeDtypeStruct((rows, width), BF16),
            jax.ShapeDtypeStruct((n, 3 * width), F32),
            jax.ShapeDtypeStruct((8, LANES), F32),
            jax.ShapeDtypeStruct((16, LANES), F32),
        )
        + tuple(jax.ShapeDtypeStruct((SEQ, a, b), BF16) for a, b in shapes),
        in_specs=[hbm] * 5 + [vm] * 5 + [hbm] * 3,
        out_specs=(vm, vm, vm, vm, hbm, hbm, hbm),
        scratch_shapes=[
            pltpu.VMEM((HL, length, LANES), BF16),
            pltpu.VMEM((HL, length, LANES), BF16),
            pltpu.VMEM((HL, length, LANES), BF16),
            pltpu.VMEM((SEQ, HL, half, LANES), BF16),
            pltpu.VMEM((SEQ, rows, width), BF16),
            pltpu.VMEM((width, length), BF16),
            pltpu.VMEM((HL, HEAD_DIM, length), BF16),
            pltpu.VMEM((SEQ, HL, half, LANES), BF16),
            pltpu.VMEM((SEQ, HL, half, LANES), BF16),
            pltpu.VMEM((length, LANES), BF16),
            pltpu.VMEM((HEAD_DIM, length), F32),
            pltpu.VMEM((rows, LANES), F32),
            pltpu.VMEM((rows, LANES), F32),
            pltpu.VMEM((length, 2 * LANES), BF16),
            pltpu.VMEM((HL, SEQ, 3, half, LANES), BF16),
            pltpu.VMEM((HL, SEQ, 3, half, LANES), BF16),
            pltpu.VMEM((rows, 3 * width), BF16),
            pltpu.VMEM((zs, 2, n, 3 * width), BF16),
            pltpu.VMEM((width, 3 * width), BF16),
            pltpu.VMEM((HL, 2, zs, rt, LANES), BF16),
            pltpu.VMEM((HL, zs, rt, LANES), BF16),
            pltpu.VMEM((HL, p, rt, LANES), BF16),
            pltpu.VMEM((HL, SEQ, rt, LANES), BF16),
            pltpu.VMEM((2, zs, 16, LANES), F32),
            pltpu.VMEM((zs, 16, LANES), F32),
            pltpu.VMEM((p, 16, LANES), F32),
            pltpu.VMEM((SEQ, 16, LANES), F32),
        ]
        + per_weight(lambda a, b: (zs, SEQ, a, b))
        + per_weight(lambda a, b: (zs, SEQ, a, b))
        + per_weight(lambda a, b: (zs, 2, a, b // 2))
        + per_weight(lambda a, b: (zs, 2, a, b // 2))
        + per_weight(lambda a, b: (zs, a, b // 2))
        + per_weight(lambda a, b: (zs, a, b // 2))
        + per_weight(lambda a, b: (p, a, b))
        + per_weight(lambda a, b: (SEQ, a, b))
        + [
            pltpu.SemaphoreType.DMA((slots,)),
            pltpu.SemaphoreType.DMA((slots,)),
            pltpu.SemaphoreType.DMA((8,)),
        ],
        compiler_params=pltpu.CompilerParams(
            collective_id=1, has_side_effects=True, vmem_limit_bytes=60 << 20
        ),
        name="collect",
    )(
        qa,
        ka,
        vv,
        own,
        tok,
        triple,
        dctx,
        gfirst,
        vecs,
        ebg,
        go.reshape(zs, 2, SEQ, *shapes[0]),
        ge.reshape(zs, 2, SEQ, *shapes[1]),
        gs.reshape(zs, 2, SEQ, *shapes[2]),
    )


def layer_norm(hidden, gain, shift):
    center = hidden - jnp.mean(hidden, axis=-1, keepdims=True)
    spread = jnp.mean(center * center, axis=-1, keepdims=True)
    return center * lax.rsqrt(spread + EPS) * gain + shift


def exact_gelu(values):
    return jax.nn.gelu(values, approximate=False)


def middle(flat, context, par, eb, wo, we, ws, cotangent):
    out_bias, gain_one, shift_one, shr_bias, gain_two, shift_two = [par[r] for r in range(2, 8)]
    attended = jnp.dot(context, wo, preferred_element_type=F32) + out_bias
    first = flat.astype(F32) + attended
    normed, first_pull = jax.vjp(layer_norm, first, gain_one, shift_one)
    normed_low = normed.astype(BF16)
    expand = jnp.dot(normed_low, we, preferred_element_type=F32) + eb[0]
    active_full, gelu_pull = jax.vjp(exact_gelu, expand)
    active = active_full.astype(BF16)
    shrink = jnp.dot(active, ws, preferred_element_type=F32) + shr_bias
    second = normed + shrink
    result, second_pull = jax.vjp(layer_norm, second, gain_two, shift_two)
    layer_out = result.astype(BF16)
    grad_second, g_gain_two, g_shift_two = second_pull(cotangent.astype(F32))
    shrink_low = grad_second.astype(BF16)
    gs = jnp.dot(active.T, shrink_low, preferred_element_type=F32).astype(BF16)
    g_shr_bias = jnp.sum(shrink_low, axis=0, dtype=F32)
    (grad_expand,) = gelu_pull(jnp.dot(shrink_low, ws.T, preferred_element_type=F32))
    expand_low = grad_expand.astype(BF16)
    ge = jnp.dot(normed_low.T, expand_low, preferred_element_type=F32).astype(BF16)
    g_exp_bias = jnp.sum(expand_low, axis=0, dtype=F32)
    grad_normed = grad_second + jnp.dot(expand_low, we.T, preferred_element_type=F32)
    grad_first, g_gain_one, g_shift_one = first_pull(grad_normed)
    attended_low = grad_first.astype(BF16)
    go = jnp.dot(context.T, attended_low, preferred_element_type=F32).astype(BF16)
    g_out_bias = jnp.sum(attended_low, axis=0, dtype=F32)
    dctx = jnp.dot(attended_low, wo.T, preferred_element_type=F32).astype(BF16)
    zero = jnp.zeros_like(g_out_bias)
    vecs = jnp.stack([zero, zero, g_out_bias, g_gain_one, g_shift_one, g_shr_bias, g_gain_two, g_shift_two])
    return layer_out, grad_first, dctx, vecs, g_exp_bias[None], go, ge, gs


def body(
    tokens,
    segment,
    padding,
    triple_weight,
    query_bias,
    value_bias,
    output_weight,
    output_bias,
    first_gain,
    first_shift,
    expand_weight,
    expand_bias,
    shrink_weight,
    shrink_bias,
    second_gain,
    second_shift,
    cotangent,
):
    n, width = output_weight.shape
    ff = expand_weight.shape[1]
    small = pack_small(
        query_bias,
        value_bias,
        output_bias,
        first_gain,
        first_shift,
        shrink_bias,
        second_gain,
        second_shift,
        expand_bias,
    )
    qa, ka, vv, own, tok, context, par, eb, wo, we, ws = gather_call(
        tokens[0], segment, padding, triple_weight, small, output_weight, expand_weight, shrink_weight
    )
    layer_out, grad_first, dctx, vecs, ebg, go, ge, gs = middle(
        tokens[0], context, par, eb, wo, we, ws, cotangent[0]
    )
    tokens_grad, triple_grad, bias_grad, small_grad, go, ge, gs = collect_call(
        qa, ka, vv, own, tok, triple_weight, dctx, grad_first, vecs, ebg, go, ge, gs
    )
    return (
        layer_out[None],
        tokens_grad[None],
        triple_grad,
        bias_grad[0, :n],
        bias_grad[1, :n],
        go.reshape(n, width).astype(F32),
        small_grad[2, :n],
        small_grad[3, :n],
        small_grad[4, :n],
        ge.reshape(n, ff).astype(F32),
        small_grad[8:12, :n].reshape(4 * n),
        gs.reshape(4 * n, width).astype(F32),
        small_grad[5, :n],
        small_grad[6, :n],
        small_grad[7, :n],
    )


def solution(mesh):
    return jax.shard_map(
        body,
        mesh=mesh,
        in_specs=(
            P("fsdp", "seq", None),
            P("fsdp", None),
            P("fsdp", None),
            P("fsdp", None),
            P("fsdp"),
            P("fsdp"),
            P("fsdp", None),
            P("fsdp"),
            P("fsdp"),
            P("fsdp"),
            P("fsdp", None),
            P("fsdp"),
            P("fsdp", None),
            P("fsdp"),
            P("fsdp"),
            P("fsdp"),
            P("fsdp", "seq", None),
        ),
        out_specs=(
            P("fsdp", "seq", None),
            P("fsdp", "seq", None),
            P("fsdp", None),
            P("fsdp"),
            P("fsdp"),
            P("fsdp", None),
            P("fsdp"),
            P("fsdp"),
            P("fsdp"),
            P("fsdp", None),
            P("fsdp"),
            P("fsdp", None),
            P("fsdp"),
            P("fsdp"),
            P("fsdp"),
        ),
        check_vma=False,
    )
```

```python
import functools

import jax
import jax.numpy as jnp
from jax import lax
from jax.experimental import pallas as pl
from jax.experimental.pallas import tpu as pltpu
from jax.sharding import PartitionSpec as P

HEADS = 12
HEAD_DIM = 64
EPS = 1e-06
MASKED = -1e30
MESH = pl.DeviceIdType.MESH
F32 = jnp.float32
BF16 = jnp.bfloat16
SEQ = 4
HL = HEADS // SEQ
LANES = 128


def ring(s):
    return (s + 1 - 2 * (s % 2), (s + 2) % 4, 3 - s)


class Net:
    def __init__(self, send, recv):
        self.send, self.recv, self.next = send, recv, 0
        self.pending = {}

    def slot(self):
        self.next += 1
        return self.next - 1

    def copy(self, i, src, dst, device):
        return pltpu.make_async_remote_copy(
            src_ref=src,
            dst_ref=dst,
            send_sem=self.send.at[i],
            recv_sem=self.recv.at[i],
            device_id=device,
            device_id_type=MESH,
        )

    def start(self, i, src, dst, device):
        copy = self.copy(i, src, dst, device)
        copy.start()
        self.pending[i] = copy.wait_send

    def begin(self, i, make):
        self.copy(i, *make()).start()
        self.pending[i] = lambda: self.copy(i, *make()).wait_send()

    def arrived(self, i, dst, device):
        self.copy(i, dst, dst, device).wait_recv()

    def drain(self):
        for wait in self.pending.values():
            wait()
        self.pending = {}


def gather_kernel(
    zs,
    tok,
    seg,
    pad,
    trip,
    small,
    wo,
    we,
    ws,
    qa_out,
    ka_out,
    v_out,
    own_out,
    kt_out,
    tt_out,
    ctx_out,
    par_out,
    eb_out,
    wo_all,
    we_all,
    ws_all,
    tokbuf,
    wsend,
    wbuf,
    wpad,
    smallbuf,
    qa,
    ka,
    vv,
    kt,
    tt,
    qmask,
    kmask,
    ctxsend,
    ctxrecv,
    send,
    recv,
    local,
):
    s = lax.axis_index("seq")
    f = lax.axis_index("fsdp")
    z, c = f // 2, f % 2
    rows, width = tok.shape
    length = rows * SEQ
    part = wsend.shape[1]
    n = trip.shape[0]
    hw = HL * HEAD_DIM
    s1, s2, s3 = ring(s)
    zpeers = [((z + j) % zs, (z - j + zs) % zs) for j in range(1, zs)]
    sib = (s, z * 2 + 1 - c)

    for t in range(SEQ):

        @pl.when(s == t)
        def _(t=t):
            for j in range(3):
                wsend[:, j * hw : (j + 1) * hw] = trip[:, j * width + t * hw : j * width + (t + 1) * hw]

    barrier = pltpu.get_barrier_semaphore()
    partners = [(s1, f), (s2, f), (s3, f), sib] + [(s, zt * 2 + c) for zt, _ in zpeers]
    for partner in partners:
        pl.semaphore_signal(barrier, inc=1, device_id=partner, device_id_type=MESH)
    pl.semaphore_wait(barrier, len(partners))

    net = Net(send, recv)
    half = rows // 2
    lo, hi = pl.ds(0, half), pl.ds(half, half)

    t_1lo, t_1hi, t_2lo, t_2hi, t_3lo, t_3hi = [net.slot() for _ in range(6)]
    net.start(t_1lo, tok.at[lo], tokbuf.at[s, lo], (s1, f))
    net.start(t_2hi, tok.at[hi], tokbuf.at[s, hi], (s2, f))
    w_z = [net.slot() for _ in zpeers]
    p_z = [net.slot() for _ in zpeers]
    w_sib = [net.slot() for _ in range(zs)]
    p_sib = [net.slot() for _ in range(zs)]

    for j, (zt, _) in enumerate(zpeers):
        net.start(w_z[j], wsend, wbuf.at[z, c], (s, zt * 2 + c))
        net.start(p_z[j], small, smallbuf.at[z, c], (s, zt * 2 + c))
    net.start(w_sib[0], wsend, wbuf.at[z, c], sib)
    net.start(p_sib[0], small, smallbuf.at[z, c], sib)
    net.start(t_1hi, tok.at[hi], tokbuf.at[s, hi], (s1, f))
    net.start(t_2lo, tok.at[lo], tokbuf.at[s, lo], (s2, f))
    weights = ((wo, wo_all), (we, we_all), (ws, ws_all))
    f_z = [[net.slot() for _ in weights] for _ in zpeers]
    for i, (mine, full) in enumerate(weights):
        for j, (zt, _) in enumerate(zpeers):
            net.start(f_z[j][i], mine.at[s], full.at[z, c, s], (s, zt * 2 + c))
    f_sib = [[net.slot() for _ in weights] for _ in range(zs)]
    own = []
    for i, (mine, full) in enumerate(weights):
        net.start(f_sib[0][i], mine, full.at[z, c], sib)
        copy = pltpu.make_async_copy(mine, full.at[z, c], local.at[i])
        copy.start()
        own.append(copy)

    wbuf[z, c] = wsend[...]
    smallbuf[z, c] = small[...]
    tokbuf[s] = tok[...]

    row_id = lax.broadcasted_iota(jnp.int32, (LANES, length), 0) - HEAD_DIM
    seg_row = jnp.broadcast_to(seg[...], (LANES, length))
    pad_row = jnp.broadcast_to(pad[...], (LANES, length))
    here = (row_id == seg_row) & (row_id >= 0)
    live_row = row_id == 32
    q_t = jnp.where(live_row, pad_row.astype(F32), jnp.where(here, 1.0, 0.0))
    qmask[...] = q_t.T
    inside = (row_id >= 0) & (row_id < 16)
    k_t = jnp.where(inside & jnp.logical_not(here & (pad_row == 1)), MASKED, 0.0)
    k_t = jnp.where((row_id >= 16) & (row_id < 19), 1.0, k_t)
    kmask[...] = k_t.T.astype(BF16)

    net.arrived(t_1lo, tokbuf.at[s1, lo], (s1, f))
    net.start(t_3lo, tokbuf.at[s1, lo], tokbuf.at[s1, lo], (s2, f))
    net.arrived(t_2hi, tokbuf.at[s2, hi], (s2, f))
    net.start(t_3hi, tokbuf.at[s2, hi], tokbuf.at[s2, hi], (s1, f))

    for j, (_, zf) in enumerate(zpeers):
        net.arrived(w_z[j], wbuf.at[zf, c], (s, zf * 2 + c))
        net.start(w_sib[j + 1], wbuf.at[zf, c], wbuf.at[zf, c], sib)
        net.arrived(p_z[j], smallbuf.at[zf, c], (s, zf * 2 + c))
        net.start(p_sib[j + 1], smallbuf.at[zf, c], smallbuf.at[zf, c], sib)

    net.arrived(w_sib[0], wbuf.at[z, 1 - c], sib)
    net.arrived(p_sib[0], smallbuf.at[z, 1 - c], sib)
    for j, (_, zf) in enumerate(zpeers):
        net.arrived(w_sib[j + 1], wbuf.at[zf, 1 - c], sib)
        net.arrived(p_sib[j + 1], smallbuf.at[zf, 1 - c], sib)

    for zi in range(zs):
        for ci in range(2):
            fi = zi * 2 + ci
            block = smallbuf[zi, ci].astype(F32)
            par_out[:, fi * n : (fi + 1) * n] = block[:, :n]
            for r in range(4):
                at = fi * 4 * n + r * n
                eb_out[:, at : at + n] = block[8 + r : 9 + r, :n]

    wpad[...] = jnp.zeros_like(wpad)
    for zi in range(zs):
        for ci in range(2):
            fi = zi * 2 + ci
            for k in range(3 * HL):
                wpad[fi * n : (fi + 1) * n, k * LANES : k * LANES + HEAD_DIM] = wbuf[
                    zi, ci, :, k * HEAD_DIM : (k + 1) * HEAD_DIM
                ]
    bias = jnp.zeros((2, HL * LANES), F32)
    zero = jnp.zeros((2, HEAD_DIM), F32)
    for t in range(SEQ):
        pieces = []
        for h in range(HL):
            pieces += [par_out[0:2, t * hw + h * HEAD_DIM : t * hw + (h + 1) * HEAD_DIM], zero]
        bias = jnp.where(s == t, jnp.concatenate(pieces, axis=1), bias)
    lane = lax.broadcasted_iota(jnp.int32, (1, LANES), 1)
    ones_lane = jnp.where((lane == HEAD_DIM) | (lane == HEAD_DIM + 1), 1.0, 0.0)

    def project(block):
        x = tokbuf[block]
        at = pl.ds(pl.multiple_of(block * rows, rows), rows)
        group = HL * LANES

        def part(k):
            return jnp.dot(x, wpad[:, k * group : (k + 1) * group], preferred_element_type=F32)

        qm = jnp.where(lane < HEAD_DIM + 16, qmask[at, :], 0.0).astype(BF16)
        q = ((part(0) + bias[0:1, :]).astype(BF16) * BF16(HEAD_DIM**-0.5))
        k = part(1).astype(BF16)
        v = part(2) + bias[1:2, :]
        for h in range(HL):
            cut = slice(h * LANES, (h + 1) * LANES)
            qa[h, at, :] = q[:, cut] + qm
            ka[h, at, :] = k[:, cut] + kmask[at, :]
            vv[h, at, :] = (v[:, cut] + ones_lane).astype(BF16)

    project(s)
    net.arrived(t_1hi, tokbuf.at[s1, hi], (s1, f))
    project(s1)
    net.arrived(t_2lo, tokbuf.at[s2, lo], (s2, f))
    project(s2)
    net.arrived(t_3lo, tokbuf.at[s3, lo], (s2, f))
    net.arrived(t_3hi, tokbuf.at[s3, hi], (s1, f))
    project(s3)

    f_1 = [[net.slot() for _ in weights] for _ in zpeers]
    f_2 = [[net.slot() for _ in weights] for _ in zpeers]
    f_3lo = [[net.slot() for _ in weights] for _ in zpeers]
    f_3hi = [[net.slot() for _ in weights] for _ in zpeers]

    def spread(i):
        full = weights[i][1]
        for j, (_, zf) in enumerate(zpeers):
            net.arrived(f_z[j][i], full.at[zf, c, s], (s, zf * 2 + c))
            net.start(f_1[j][i], full.at[zf, c, s], full.at[zf, c, s], (s1, f))
            net.start(f_2[j][i], full.at[zf, c, s], full.at[zf, c, s], (s2, f))

    def halves(full, zf, src, which):
        w = full.shape[-1] // 2
        return full.at[zf, c, src, :, pl.ds(which * w, w)]

    def pass_on(i):
        full = weights[i][1]
        for j, (_, zf) in enumerate(zpeers):
            net.arrived(f_1[j][i], full.at[zf, c, s1], (s1, f))
            net.start(f_3lo[j][i], halves(full, zf, s1, 0), halves(full, zf, s1, 0), (s2, f))
            net.arrived(f_2[j][i], full.at[zf, c, s2], (s2, f))
            net.start(f_3hi[j][i], halves(full, zf, s2, 1), halves(full, zf, s2, 1), (s1, f))

    def finish(i):
        full = weights[i][1]
        for j, (_, zf) in enumerate(zpeers):
            net.arrived(f_3lo[j][i], halves(full, zf, s3, 0), (s2, f))
            net.arrived(f_3hi[j][i], halves(full, zf, s3, 1), (s1, f))
            net.start(f_sib[j + 1][i], full.at[zf, c], full.at[zf, c], sib)

    c_1, c_2, c_3 = [net.slot() for _ in range(3)]
    qt = min(256, rows)

    def attend(block):
        @pl.loop(0, HL)
        def _(h):
            @pl.loop(0, rows // qt)
            def _(i):
                at = pl.multiple_of(block * rows + i * qt, qt)
                scores = lax.dot_general(
                    qa[h, pl.ds(at, qt), :],
                    ka[h],
                    (((1,), (1,)), ((), ())),
                    preferred_element_type=F32,
                )
                top = jnp.max(scores, axis=-1, keepdims=True)
                probs = jnp.exp(scores - top).astype(BF16)
                out = jnp.dot(probs, vv[h], preferred_element_type=F32)
                total = out[:, HEAD_DIM : HEAD_DIM + 1]
                live = qmask[pl.ds(at, qt), HEAD_DIM + 32 : HEAD_DIM + 33]
                ctx = (out * (live / total)).astype(BF16)[:, :HEAD_DIM]
                lse = jnp.where(live > 0.0, top + jnp.log(total), -MASKED)
                lse = -lse
                hi = lse.astype(BF16).astype(F32)
                mid = (lse - hi).astype(BF16).astype(F32)
                rest = lse - hi - mid
                base = HEAD_DIM + 16
                extra = jnp.where(lane == base, hi, jnp.where(lane == base + 1, mid, jnp.where(lane == base + 2, rest, 0.0)))
                qa[h, pl.ds(at, qt), :] = qa[h, pl.ds(at, qt), :] + extra.astype(BF16)
                per = half // qt
                down = pl.multiple_of((i % per) * qt, qt)

                @pl.when(i < per)
                def _():
                    ctxsend[block, h, pl.ds(down, qt), 0:HEAD_DIM] = ctx

                @pl.when(i >= per)
                def _():
                    ctxsend[block, h, pl.ds(down, qt), HEAD_DIM:LANES] = ctx

    spread(0)
    spread(1)
    attend(s3)
    net.start(c_3, ctxsend.at[s3], ctxrecv.at[s], (s3, f))
    spread(2)
    attend(s1)
    net.start(c_1, ctxsend.at[s1], ctxrecv.at[s], (s1, f))
    pass_on(0)
    pass_on(1)
    attend(s2)
    net.start(c_2, ctxsend.at[s2], ctxrecv.at[s], (s2, f))
    pass_on(2)
    attend(s)
    ctxrecv[s] = ctxsend[s]
    outs = []

    def save(i, src, dst):
        copy = pltpu.make_async_copy(src, dst, local.at[3 + i])
        copy.start()
        outs.append(copy)

    for i, (src, dst) in enumerate(((qa, qa_out), (ka, ka_out), (vv, v_out), (ctxsend, own_out))):
        save(i, src, dst)

    @pl.loop(0, HL)
    def _(h):
        kt[h] = ka[h].T[0:HEAD_DIM]

    @pl.loop(0, SEQ)
    def _(t):
        at = pl.multiple_of(t * rows, rows)
        tt[:, pl.ds(at, rows)] = tokbuf[t].T

    save(4, kt, kt_out)
    save(5, tt, tt_out)
    net.arrived(c_3, ctxrecv.at[s3], (s3, f))
    net.arrived(c_1, ctxrecv.at[s1], (s1, f))
    net.arrived(c_2, ctxrecv.at[s2], (s2, f))
    for t in range(SEQ):
        for h in range(HL):
            at = t * hw + h * HEAD_DIM
            ctx_out[0:half, at : at + HEAD_DIM] = ctxrecv[t, h, :, 0:HEAD_DIM]
            ctx_out[half:rows, at : at + HEAD_DIM] = ctxrecv[t, h, :, HEAD_DIM:LANES]
    for i in range(3):
        finish(i)
    for i, (_, full) in enumerate(weights):
        net.arrived(f_sib[0][i], full.at[z, 1 - c], sib)
        for j, (_, zf) in enumerate(zpeers):
            net.arrived(f_sib[j + 1][i], full.at[zf, 1 - c], sib)
    for copy in own + outs:
        copy.wait()
    net.drain()


def gather_slots(zs):
    p = zs - 1
    return 6 + 2 * p + 2 * zs + 3 * p + 3 * zs + 12 * p + 3


def gather_call(tokens, segment, padding, triple, small, wo, we, ws):
    rows, width = tokens.shape
    length = rows * SEQ
    n = triple.shape[0]
    shards = width // n
    zs = shards // 2
    hw = HL * HEAD_DIM
    ff = we.shape[1]
    slots = gather_slots(zs)
    vm = pl.BlockSpec(memory_space=pltpu.VMEM)
    hbm = pl.BlockSpec(memory_space=pl.ANY)
    q, qs = n // SEQ, ws.shape[0] // SEQ
    out_shape = (
        jax.ShapeDtypeStruct((HL, length, LANES), BF16),
        jax.ShapeDtypeStruct((HL, length, LANES), BF16),
        jax.ShapeDtypeStruct((HL, length, LANES), BF16),
        jax.ShapeDtypeStruct((SEQ, HL, rows // 2, LANES), BF16),
        jax.ShapeDtypeStruct((HL, HEAD_DIM, length), BF16),
        jax.ShapeDtypeStruct((width, length), BF16),
        jax.ShapeDtypeStruct((rows, width), BF16),
        jax.ShapeDtypeStruct((16, width), F32),
        jax.ShapeDtypeStruct((1, ff), F32),
        jax.ShapeDtypeStruct((zs, 2, SEQ, q, width), BF16),
        jax.ShapeDtypeStruct((zs, 2, SEQ, q, ff), BF16),
        jax.ShapeDtypeStruct((zs, 2, SEQ, qs, width), BF16),
    )
    outs = pl.pallas_call(
        functools.partial(gather_kernel, zs),
        out_shape=out_shape,
        in_specs=[vm, vm, vm, vm, vm, hbm, hbm, hbm],
        out_specs=(hbm, hbm, hbm, hbm, hbm, hbm, vm, vm, vm, hbm, hbm, hbm),
        scratch_shapes=[
            pltpu.VMEM((SEQ, rows, width), BF16),
            pltpu.VMEM((n, 3 * hw), BF16),
            pltpu.VMEM((zs, 2, n, 3 * hw), BF16),
            pltpu.VMEM((width, 3 * HL * LANES), BF16),
            pltpu.VMEM((zs, 2, 16, LANES), BF16),
            pltpu.VMEM((HL, length, LANES), BF16),
            pltpu.VMEM((HL, length, LANES), BF16),
            pltpu.VMEM((HL, length, LANES), BF16),
            pltpu.VMEM((HL, HEAD_DIM, length), BF16),
            pltpu.VMEM((width, length), BF16),
            pltpu.VMEM((length, LANES), F32),
            pltpu.VMEM((length, LANES), BF16),
            pltpu.VMEM((SEQ, HL, rows // 2, LANES), BF16),
            pltpu.VMEM((SEQ, HL, rows // 2, LANES), BF16),
            pltpu.SemaphoreType.DMA((slots,)),
            pltpu.SemaphoreType.DMA((slots,)),
            pltpu.SemaphoreType.DMA((9,)),
        ],
        compiler_params=pltpu.CompilerParams(
            collective_id=0, has_side_effects=True, vmem_limit_bytes=60 << 20
        ),
        name="gather_attend",
    )(
        tokens,
        segment,
        padding,
        triple,
        small,
        wo.reshape(SEQ, q, width),
        we.reshape(SEQ, q, ff),
        ws.reshape(SEQ, qs, width),
    )
    qa, ka, vv, own, kt, tt, ctx, par, eb, wof, wef, wsf = outs
    return (
        qa,
        ka,
        vv,
        own,
        kt,
        tt,
        ctx,
        par,
        eb,
        wof.reshape(width, width),
        wef.reshape(width, ff),
        wsf.reshape(ff, width),
    )


def pack_small(query_bias, value_bias, output_bias, first_gain, first_shift, shrink_bias, second_gain, second_shift, expand_bias):
    n = query_bias.shape[0]
    rows = [query_bias, value_bias, output_bias, first_gain, first_shift, shrink_bias, second_gain, second_shift]
    table = jnp.concatenate([jnp.stack(rows), expand_bias.reshape(4, n)], axis=0)
    return jnp.pad(table, ((0, 4), (0, LANES - n)))


def norm_parts(hidden):
    center = hidden - jnp.mean(hidden, axis=-1, keepdims=True)
    factor = lax.rsqrt(jnp.mean(center * center, axis=-1, keepdims=True) + EPS)
    return center * factor, factor


def norm_back(grad, normal, factor, gain):
    c = grad * gain
    mean = jnp.mean(c, axis=-1, keepdims=True)
    inner = jnp.mean(c * normal, axis=-1, keepdims=True)
    return factor * (c - mean - normal * inner)


NT = (((1,), (1,)), ((), ()))
TN = (((0,), (0,)), ((), ()))


def middle(
    refs,
    grads,
    shrink_ready,
    shrink_go,
    context_ready,
    loads,
    out_sem,
    wo,
    we,
    ws,
    nl,
    nlt,
    n1,
    r1,
    act,
    slope,
    sl,
):
    tok, ctx, par, eb, cot, lout, gfirst, vecs, ebg = refs
    g_out, g_exp, g_shr = grads
    rows, width = tok.shape
    ff = eb.shape[1]
    zs = g_out.shape[1]
    n = width // (2 * zs)
    tile = min(128, rows)
    wide = 256
    vecs[...] = jnp.zeros_like(vecs)

    def add_row(r, value):
        vecs[r : r + 1, :] = vecs[r : r + 1, :] + jnp.sum(value, axis=0, keepdims=True)

    loads[0].wait()

    @pl.loop(0, width // wide)
    def _(j):
        at = pl.ds(pl.multiple_of(j * wide, wide), wide)
        gfirst[:, at] = jnp.dot(ctx[...], wo[:, at], preferred_element_type=F32)

    @pl.loop(0, rows // tile)
    def _(i):
        at = pl.ds(pl.multiple_of(i * tile, tile), tile)
        normal, factor = norm_parts(tok[at, :].astype(F32) + gfirst[at, :] + par[2:3, :])
        n1[at, :] = normal
        r1[at, :] = factor
        nl[at, :] = (normal * par[3:4, :] + par[4:5, :]).astype(BF16)

    loads[1].wait()

    @pl.loop(0, ff // wide)
    def _(j):
        at = pl.ds(pl.multiple_of(j * wide, wide), wide)
        u = jnp.dot(nl[...], we[:, at], preferred_element_type=F32) + eb[:, at]
        phi = 0.5 + 0.5 * lax.erf(u * 0.5**0.5)
        act[:, at] = (u * phi).astype(BF16)
        slope[:, at] = (phi + u * (jnp.exp(-0.5 * u * u) * (2.0 * 3.141592653589793) ** -0.5)).astype(BF16)

    nlt[...] = nl[...].T
    loads[2].wait()

    @pl.loop(0, width // wide)
    def _(j):
        at = pl.ds(pl.multiple_of(j * wide, wide), wide)
        gfirst[:, at] = jnp.dot(act[...], ws[:, at], preferred_element_type=F32)

    @pl.loop(0, rows // tile)
    def _(i):
        at = pl.ds(pl.multiple_of(i * tile, tile), tile)
        second = n1[at, :] * par[3:4, :] + par[4:5, :] + par[5:6, :] + gfirst[at, :]
        normal, factor = norm_parts(second)
        nl[at, :] = (normal * par[6:7, :] + par[7:8, :]).astype(BF16)
        e = cot[at, :].astype(F32)
        add_row(6, e * normal)
        add_row(7, e)
        back = norm_back(e, normal, factor, par[6:7, :])
        gfirst[at, :] = back
        low = back.astype(BF16)
        sl[at, :] = low
        add_row(5, low.astype(F32))

    result = pltpu.make_async_copy(nl, lout, out_sem)
    result.start()
    per = max(1, 384 // (4 * n))

    @pl.loop(0, ff // (per * 4 * n))
    def _(j):
        at = pl.ds(pl.multiple_of(j * per * 4 * n, LANES), per * 4 * n)
        g = lax.dot_general(act[:, at], sl[...], TN, preferred_element_type=F32)
        for k in range(per):
            fi = j * per + k
            for qi in range(SEQ):
                lo = (k * SEQ + qi) * n
                g_shr[fi % 2, fi // 2, qi] = g[lo : lo + n].astype(BF16)

    shrink_ready()

    @pl.loop(0, ff // wide)
    def _(j):
        at = pl.ds(pl.multiple_of(j * wide, wide), wide)
        back = lax.dot_general(sl[...], ws[at, :], NT, preferred_element_type=F32)
        low = (back * slope[:, at].astype(F32)).astype(BF16)
        act[:, at] = low
        ebg[:, at] = jnp.sum(low.astype(F32), axis=0, keepdims=True)

    shrink_go()

    @pl.loop(0, width // wide)
    def _(j):
        at = pl.ds(pl.multiple_of(j * wide, wide), wide)
        gfirst[:, at] += lax.dot_general(act[...], we[at, :], NT, preferred_element_type=F32)

    @pl.loop(0, rows // tile)
    def _(i):
        at = pl.ds(pl.multiple_of(i * tile, tile), tile)
        e = gfirst[at, :]
        normal = n1[at, :]
        add_row(3, e * normal)
        add_row(4, e)
        back = norm_back(e, normal, r1[at, :], par[3:4, :])
        gfirst[at, :] = back
        low = back.astype(BF16)
        sl[at, :] = low
        add_row(2, low.astype(F32))

    context_ready()
    q = n // SEQ

    def keep(grad, g, j, at):
        if q % 8 == 0:
            for fi in range(2 * zs):
                for qi in range(SEQ):
                    lo = fi * n + qi * q
                    grad[fi % 2, fi // 2, qi, :, at] = g[lo : lo + q].astype(BF16)
        else:
            blocks = ff // SEQ // wide
            for fi in range(2 * zs):
                grad[fi % 2, fi // 2, j // blocks, :, pl.ds(pl.multiple_of(j % blocks * wide, wide), wide)] = g[
                    fi * n : (fi + 1) * n
                ].astype(BF16)

    @pl.loop(0, ff // wide)
    def _(j):
        at = pl.ds(pl.multiple_of(j * wide, wide), wide)
        keep(g_exp, jnp.dot(nlt[...], act[:, at], preferred_element_type=F32), j, at)

    if q % 8 == 0:

        @pl.loop(0, width // wide)
        def _(j):
            at = pl.ds(pl.multiple_of(j * wide, wide), wide)
            keep(g_out, lax.dot_general(ctx[...], sl[:, at], TN, preferred_element_type=F32), j, at)

    else:
        w = width // SEQ
        for qi in range(SEQ):
            g = lax.dot_general(ctx[...], sl[:, qi * w : (qi + 1) * w], TN, preferred_element_type=F32)
            for fi in range(2 * zs):
                g_out[fi % 2, fi // 2, qi, :, 0:w] = g[fi * n : (fi + 1) * n].astype(BF16)

    result.wait()


def collect_kernel(
    zs,
    qa_hbm,
    ka_hbm,
    v_hbm,
    own_hbm,
    kt_hbm,
    tt_hbm,
    trip,
    tokens,
    ctx,
    par,
    eb,
    cot,
    wo_hbm,
    we_hbm,
    ws_hbm,
    lout,
    tg_out,
    trip_out,
    bias_out,
    small_out,
    go_out,
    ge_out,
    gs_out,
    wland,
    dsend,
    drecv,
    grecv,
    gfirst,
    vecs,
    ebg,
    tsend,
    tcore,
    tz,
    tfin,
    svec,
    svcore,
    svz,
    svseq,
    ao,
    ae,
    a_s,
    co,
    ce,
    cs,
    xo,
    xe,
    xs,
    yo,
    ye,
    ys,
    x2o,
    x2e,
    x2s,
    y2o,
    y2e,
    y2s,
    zo,
    ze,
    zsm,
    fo,
    fe,
    fs,
    send,
    recv,
    local,
):
    s = lax.axis_index("seq")
    f = lax.axis_index("fsdp")
    z, c = f // 2, f % 2
    rows, width = tokens.shape
    half = rows // 2
    length = rows * SEQ
    n = trip.shape[0]
    hw = HL * HEAD_DIM
    s1, s2, s3 = ring(s)
    zpeers = [((z + j) % zs, (z - j + zs) % zs) for j in range(1, zs)]
    sib = (s, z * 2 + 1 - c)
    net = Net(send, recv)
    lane = lax.broadcasted_iota(jnp.int32, (1, LANES), 1)

    barrier = pltpu.get_barrier_semaphore()
    partners = [(s1, f), (s2, f), (s3, f), sib] + [(s, zt * 2 + c) for zt, _ in zpeers]
    for partner in partners:
        pl.semaphore_signal(barrier, inc=1, device_id=partner, device_id_type=MESH)
    pl.semaphore_wait(barrier, len(partners))

    w_z = [net.slot() for _ in zpeers]
    w_sib = [net.slot() for _ in range(zs)]
    for j, (zt, _) in enumerate(zpeers):
        net.start(w_z[j], trip, wland.at[z, c], (s, zt * 2 + c))
    net.start(w_sib[0], trip, wland.at[z, c], sib)
    own_copy = pltpu.make_async_copy(trip, wland.at[z, c], local.at[0])
    own_copy.start()

    d_sem = [[net.slot() for _ in range(3)] for _ in range(HL)]
    grads, core = (ao, ae, a_s), (co, ce, cs)
    c_sem = [net.slot() for _ in range(3)]

    def core_start(i):
        net.begin(c_sem[i], lambda: (grads[i].at[1 - c], core[i], sib))

    v_core = net.slot()
    v_z = [net.slot() for _ in zpeers]
    v_seq = [net.slot() for _ in range(3)]

    def small_start():
        for zi in range(zs):
            for ci in range(2):
                fi = zi * 2 + ci
                svec[ci, zi] = jnp.zeros((16, LANES), F32)
                svec[ci, zi, 0:8, 0:n] = vecs[:, fi * n : (fi + 1) * n]
                for r in range(4):
                    at = fi * 4 * n + r * n
                    svec[ci, zi, 8 + r : 9 + r, 0:n] = ebg[:, at : at + n]
        net.start(v_core, svec.at[1 - c], svcore, sib)

    xr, yr, x2r, y2r, zr, fin = (xo, xe, xs), (yo, ye, ys), (x2o, x2e, x2s), (y2o, y2e, y2s), (zo, ze, zsm), (fo, fe, fs)
    x_sem = [[net.slot() for _ in range(4)] for _ in range(3)]
    x2_sem = [[net.slot() for _ in range(2)] for _ in range(3)]
    z_sem = [[net.slot() for _ in zpeers] for _ in range(3)]
    a_sem = [[net.slot() for _ in range(4)] for _ in range(3)]

    def cols(i, which):
        w = grads[i].shape[-1] // 2
        return pl.ds(which * w, w)

    def plane_start(i):
        net.arrived(c_sem[i], core[i], sib)

        @pl.loop(0, zs * SEQ)
        def _(k):
            zi, qi = k // SEQ, k % SEQ
            total = grads[i][c, zi, qi].astype(F32) + core[i][zi, qi].astype(F32)
            grads[i][c, zi, qi] = total.astype(BF16)

        x, y = cols(i, 0), cols(i, 1)
        net.begin(x_sem[i][0], lambda: (grads[i].at[c, :, s3, :, x], xr[i].at[:, 1], (s1, f)))
        net.begin(x_sem[i][2], lambda: (grads[i].at[c, :, s3, :, y], yr[i].at[:, 1], (s2, f)))
        net.begin(x_sem[i][1], lambda: (grads[i].at[c, :, s1, :, x], xr[i].at[:, 0], (s1, f)))
        net.begin(x_sem[i][3], lambda: (grads[i].at[c, :, s2, :, y], yr[i].at[:, 0], (s2, f)))

    def add_into(i, part, qi, which, from_ref):
        w = grads[i].shape[-1] // 2

        @pl.loop(0, zs)
        def _(zi):
            a = grads[i][c, zi, qi, :, which * w : (which + 1) * w].astype(F32)
            b = (from_ref[zi] if part is None else from_ref[zi, part]).astype(F32)
            grads[i][c, zi, qi, :, which * w : (which + 1) * w] = (a + b).astype(BF16)

    def plane_second(i):
        net.arrived(x_sem[i][0], xr[i].at[:, 1], (s1, f))
        add_into(i, 1, s2, 0, xr[i])
        net.begin(x2_sem[i][0], lambda: (grads[i].at[c, :, s2, :, cols(i, 0)], x2r[i], (s2, f)))
        net.arrived(x_sem[i][2], yr[i].at[:, 1], (s2, f))
        add_into(i, 1, s1, 1, yr[i])
        net.begin(x2_sem[i][1], lambda: (grads[i].at[c, :, s1, :, cols(i, 1)], y2r[i], (s1, f)))
        net.arrived(x_sem[i][1], xr[i].at[:, 0], (s1, f))
        add_into(i, 0, s, 0, xr[i])
        net.arrived(x_sem[i][3], yr[i].at[:, 0], (s2, f))
        add_into(i, 0, s, 1, yr[i])

    def along_z(i):
        net.arrived(x2_sem[i][0], x2r[i], (s2, f))
        add_into(i, None, s, 0, x2r[i])
        net.arrived(x2_sem[i][1], y2r[i], (s1, f))
        add_into(i, None, s, 1, y2r[i])
        for j, (zt, _) in enumerate(zpeers):
            net.begin(z_sem[i][j], lambda zt=zt, j=j: (grads[i].at[c, zt, s], zr[i].at[j], (s, zt * 2 + c)))

    def own_rows(i):
        total = grads[i][c, z, s].astype(F32)
        for j, (_, zf) in enumerate(zpeers):
            net.arrived(z_sem[i][j], zr[i].at[j], (s, zf * 2 + c))
            total = total + zr[i][j].astype(F32)
        fin[i][s] = total.astype(BF16)
        net.begin(a_sem[i][0], lambda: (fin[i].at[s], fin[i].at[s], (s1, f)))
        net.begin(a_sem[i][1], lambda: (fin[i].at[s], fin[i].at[s], (s2, f)))

    def spread(i):
        net.arrived(a_sem[i][0], fin[i].at[s1], (s1, f))
        net.begin(a_sem[i][2], lambda: (fin[i].at[s1, :, cols(i, 0)], fin[i].at[s1, :, cols(i, 0)], (s2, f)))
        net.arrived(a_sem[i][1], fin[i].at[s2], (s2, f))
        net.begin(a_sem[i][3], lambda: (fin[i].at[s2, :, cols(i, 1)], fin[i].at[s2, :, cols(i, 1)], (s1, f)))

    final_out = (go_out, ge_out, gs_out)

    def spread_end(i):
        net.arrived(a_sem[i][2], fin[i].at[s3, :, cols(i, 0)], (s2, f))
        net.arrived(a_sem[i][3], fin[i].at[s3, :, cols(i, 1)], (s1, f))
        copy = pltpu.make_async_copy(fin[i], final_out[i], local.at[1 + i])
        copy.start()
        return copy

    def context_ready(wo, al):
        for t in range(SEQ):
            at = t * hw
            back = lax.dot_general(al[...], wo[at : at + hw, :], NT, preferred_element_type=F32).astype(BF16)
            for h in range(HL):
                dsend[t, h, :, 0:HEAD_DIM] = back[0:half, h * HEAD_DIM : (h + 1) * HEAD_DIM]
                dsend[t, h, :, HEAD_DIM:LANES] = back[half:rows, h * HEAD_DIM : (h + 1) * HEAD_DIM]
        for h in range(HL):
            for k, peer in enumerate((s3, s1, s2)):
                net.begin(d_sem[h][k], lambda peer=peer, h=h: (dsend.at[peer, h], drecv.at[s, h], (peer, f)))
        drecv[s] = dsend[s]

    def tokens_part(wo, we, ws, nl, nlt, n1, r1, act, slope, sl):
        loads = []
        for i, (src, dst) in enumerate(((wo_hbm, wo), (we_hbm, we), (ws_hbm, ws))):
            copy = pltpu.make_async_copy(src, dst, local.at[1 + i])
            copy.start()
            loads.append(copy)
        middle(
            (tokens, ctx, par, eb, cot, lout, gfirst, vecs, ebg),
            grads,
            lambda: core_start(2),
            lambda: plane_start(2),
            lambda: context_ready(wo, sl),
            loads,
            local.at[4],
            wo,
            we,
            ws,
            nl,
            nlt,
            n1,
            r1,
            act,
            slope,
            sl,
        )

    ff = eb.shape[1]
    pl.run_scoped(
        tokens_part,
        pltpu.VMEM((width, width), BF16),
        pltpu.VMEM((width, ff), BF16),
        pltpu.VMEM((ff, width), BF16),
        pltpu.VMEM((rows, width), BF16),
        pltpu.VMEM((width, rows), BF16),
        pltpu.VMEM((rows, width), F32),
        pltpu.VMEM((rows, 1), F32),
        pltpu.VMEM((rows, ff), BF16),
        pltpu.VMEM((rows, ff), BF16),
        pltpu.VMEM((rows, width), BF16),
    )
    core_start(1)
    core_start(0)
    small_start()
    own_copy.wait()

    def attention_part(qa, ka, vv, own, k_t, tok_t, da, dq_t, acc_k, acc_v, gm, gsend, gmr, wtmp, wfull):
        loads = []
        pairs = ((qa_hbm, qa), (ka_hbm, ka), (v_hbm, vv), (own_hbm, own), (kt_hbm, k_t), (tt_hbm, tok_t))
        for i, (src, dst) in enumerate(pairs):
            copy = pltpu.make_async_copy(src, dst, local.at[1 + i])
            copy.start()
            loads.append(copy)
        gm[...] = jnp.zeros_like(gm)
        plane_start(1)
        plane_start(0)
        for copy in loads:
            copy.wait()

        net.arrived(v_core, svcore, sib)
        svec[c] = svec[c] + svcore[...]
        for j, (zt, _) in enumerate(zpeers):
            net.start(v_z[j], svec.at[c, zt], svz.at[j], (s, zt * 2 + c))

        for j, (_, zf) in enumerate(zpeers):
            net.arrived(w_z[j], wland.at[zf, c], (s, zf * 2 + c))
            net.start(w_sib[j + 1], wland.at[zf, c], wland.at[zf, c], sib)

        g_sem = [[net.slot() for _ in range(3)] for _ in range(HL)]
        tc_sem = [net.slot() for _ in range(HL)]
        tz_sem = [[net.slot() for _ in zpeers] for _ in range(HL)]
        ts_sem = [[net.slot() for _ in range(3)] for _ in range(HL)]

        def prepare(h):
            for k, peer in enumerate((s3, s1, s2)):
                net.arrived(d_sem[h][k], drecv.at[peer, h], (peer, f))

            @pl.loop(0, SEQ)
            def _(t):
                grad = drecv[t, h].astype(F32)
                prod = grad * own[t, h].astype(F32)
                left = lane < HEAD_DIM
                for k in range(2):
                    inner = -jnp.sum(jnp.where(left if k == 0 else jnp.logical_not(left), prod, 0.0), axis=-1, keepdims=True)
                    hi = inner.astype(BF16).astype(F32)
                    here = grad if k == 0 else pltpu.roll(grad, HEAD_DIM, 1)
                    here = jnp.where(left, here, jnp.where(lane == HEAD_DIM, hi, jnp.where(lane == HEAD_DIM + 1, inner - hi, 0.0)))
                    at = pl.multiple_of(t * rows + k * half, half)
                    da[pl.ds(at, half), :] = here.astype(BF16)

            dq_t[...] = jnp.zeros_like(dq_t)

        def key_block(h, r):
            acc_k[...] = jnp.zeros_like(acc_k)
            acc_v[...] = jnp.zeros_like(acc_v)
            keys = pl.multiple_of(r * rows, rows)
            nt = (((1,), (1,)), ((), ()))

            @pl.loop(0, length // QB)
            def _(i):
                at = pl.multiple_of(i * QB, QB)
                q = qa[h, pl.ds(at, QB), :]
                grad = da[pl.ds(at, QB), :]
                probs = jnp.exp(lax.dot_general(ka[h, pl.ds(keys, rows), :], q, nt, preferred_element_type=F32))
                inner = lax.dot_general(vv[h, pl.ds(keys, rows), :], grad, nt, preferred_element_type=F32)
                ds = (probs * inner).astype(BF16)
                acc_v[...] += jnp.dot(probs.astype(BF16), grad, preferred_element_type=F32)
                acc_k[...] += jnp.dot(ds, q, preferred_element_type=F32)
                dq_t[:, pl.ds(at, QB)] += jnp.dot(k_t[h, :, pl.ds(keys, rows)], ds, preferred_element_type=F32)

            gm[pl.ds(keys, rows), HEAD_DIM:LANES] = acc_k[:, 0:HEAD_DIM].astype(BF16)
            gm[pl.ds(keys, rows), LANES : LANES + HEAD_DIM] = acc_v[:, 0:HEAD_DIM].astype(BF16)

        rt = tsend.shape[3]
        vrow = n + n // 2
        brow = rt - 16

        def head_done(h):
            @pl.loop(0, SEQ)
            def _(t):
                at = pl.multiple_of(t * rows, rows)
                dq = (dq_t[:, pl.ds(at, rows)].T * (HEAD_DIM**-0.5)).astype(BF16)
                gm[pl.ds(at, rows), 0:HEAD_DIM] = dq
                for k in range(3):
                    for p in range(2):
                        piece = gm[pl.ds(at + p * half, half), k * HEAD_DIM : (k + 1) * HEAD_DIM]
                        gsend[h, t, k, :, p * HEAD_DIM : (p + 1) * HEAD_DIM] = piece

            for k, peer in enumerate((s3, s1, s2)):
                net.start(g_sem[h][k], gsend.at[h, peer], grecv.at[h, s], (peer, f))
            grecv[h, s] = gsend[h, s]
            sums = jnp.sum(gm[...].astype(F32), axis=0, keepdims=True).astype(BF16)
            whole = jnp.dot(tok_t[...], gm[...], preferred_element_type=F32)
            for zi in range(zs):
                for ci in range(2):
                    fi = zi * 2 + ci
                    grad = whole[fi * n : (fi + 1) * n].astype(BF16)
                    tsend[h, ci, zi, 0:n, :] = grad[:, 0:LANES]
                    tsend[h, ci, zi, n:vrow, 0:HEAD_DIM] = grad[0 : n // 2, LANES : LANES + HEAD_DIM]
                    tsend[h, ci, zi, n:vrow, HEAD_DIM:LANES] = grad[n // 2 : n, LANES : LANES + HEAD_DIM]
                    tsend[h, ci, zi, brow:rt, :] = jnp.broadcast_to(sums[:, 0:LANES], (16, LANES))
                    tsend[h, ci, zi, brow + 8 : rt, :] = jnp.broadcast_to(sums[:, LANES : 2 * LANES], (8, LANES))
            net.start(tc_sem[h], tsend.at[h, 1 - c], tcore.at[h], sib)

        def triple_z(h):
            net.arrived(tc_sem[h], tcore.at[h], sib)
            tsend[h, c] = (tsend[h, c].astype(F32) + tcore[h].astype(F32)).astype(BF16)
            for j, (zt, _) in enumerate(zpeers):
                net.begin(tz_sem[h][j], lambda zt=zt, j=j: (tsend.at[h, c, zt], tz.at[h, j], (s, zt * 2 + c)))

        def triple_own(h):
            total = tsend[h, c, z].astype(F32)
            for j, (_, zf) in enumerate(zpeers):
                net.arrived(tz_sem[h][j], tz.at[h, j], (s, zf * 2 + c))
                total = total + tz[h, j].astype(F32)
            tfin[h, s] = total.astype(BF16)
            for k, peer in enumerate((s3, s1, s2)):
                net.begin(ts_sem[h][k], lambda peer=peer: (tfin.at[h, s], tfin.at[h, s], (peer, f)))

        def rows_in(h):
            for k, peer in enumerate((s3, s1, s2)):
                net.arrived(g_sem[h][k], grecv.at[h, peer], (peer, f))
            for t in range(SEQ):
                for k in range(3):
                    at = k * width + t * hw + h * HEAD_DIM
                    gmr[0:half, at : at + HEAD_DIM] = grecv[h, t, k, :, 0:HEAD_DIM]
                    gmr[half:rows, at : at + HEAD_DIM] = grecv[h, t, k, :, HEAD_DIM:LANES]

        def attend_back(h, *steps):
            @pl.loop(0, SEQ)
            def _(r):
                key_block(h, r)
                for k, step in enumerate(steps):

                    @pl.when(r == k)
                    def _(step=step):
                        for call, arg in step:
                            call(arg)

        plane_second(2)
        prepare(0)
        attend_back(0)
        head_done(0)
        prepare(1)
        attend_back(
            1,
            [(plane_second, 1), (triple_z, 0)],
            [(along_z, 2), (plane_second, 0)],
        )
        head_done(1)
        total = svec[c, z]
        for j, (_, zf) in enumerate(zpeers):
            net.arrived(v_z[j], svz.at[j], (s, zf * 2 + c))
            total = total + svz[j]
        svseq[s] = total
        for k, peer in enumerate((s3, s1, s2)):
            net.start(v_seq[k], svseq.at[s], svseq.at[s], (peer, f))
        prepare(2)
        attend_back(
            2,
            [(triple_own, 0)],
            [(own_rows, 2), (along_z, 1)],
            [(along_z, 0), (triple_z, 1)],
        )
        head_done(2)
        spread(2)
        rows_in(0)
        net.arrived(w_sib[0], wland.at[z, 1 - c], sib)
        for j, (_, zf) in enumerate(zpeers):
            net.arrived(w_sib[j + 1], wland.at[zf, 1 - c], sib)
        depth = wtmp.shape[0]
        for base in range(0, zs, depth):
            copy = pltpu.make_async_copy(wland.at[pl.ds(base, depth)], wtmp, local.at[0])
            copy.start()
            copy.wait()
            for zi in range(depth):
                for ci in range(2):
                    fi = (base + zi) * 2 + ci
                    wfull[fi * n : (fi + 1) * n, :] = wtmp[zi, ci]
        triple_own(1)
        triple_z(2)
        own_rows(1)
        own_rows(0)
        rows_in(1)
        triple_own(2)
        spread(1)
        spread(0)
        rows_in(2)
        wide = 256

        @pl.loop(0, width // wide)
        def _(j):
            at = pl.ds(pl.multiple_of(j * wide, wide), wide)
            back = lax.dot_general(gmr[...], wfull[at, :], NT, preferred_element_type=F32)
            tg_out[:, at] = (gfirst[:, at] + back).astype(BF16)

        copies = [spread_end(2), spread_end(1)]
        for k, peer in enumerate((s3, s1, s2)):
            net.arrived(v_seq[k], svseq.at[peer], (peer, f))
        small_out[...] = svseq[0] + svseq[1] + svseq[2] + svseq[3]
        for h in range(HL):
            for k, peer in enumerate((s3, s1, s2)):
                net.arrived(ts_sem[h][k], tfin.at[h, peer], (peer, f))
        q_row, v_row = [], []
        for t in range(SEQ):
            for h in range(HL):
                at = t * hw + h * HEAD_DIM
                block = tfin[h, t].astype(F32)
                trip_out[:, at : at + HEAD_DIM] = block[0:n, 0:HEAD_DIM]
                trip_out[:, width + at : width + at + HEAD_DIM] = block[0:n, HEAD_DIM:LANES]
                trip_out[0 : n // 2, 2 * width + at : 2 * width + at + HEAD_DIM] = block[n:vrow, 0:HEAD_DIM]
                trip_out[n // 2 : n, 2 * width + at : 2 * width + at + HEAD_DIM] = block[n:vrow, HEAD_DIM:LANES]
                q_row.append(block[brow : brow + 1, 0:HEAD_DIM])
                v_row.append(block[brow + 8 : brow + 9, 0:HEAD_DIM])
        q_row, v_row = jnp.concatenate(q_row, axis=1), jnp.concatenate(v_row, axis=1)
        bias_out[...] = jnp.zeros_like(bias_out)
        for fi in range(2 * zs):

            @pl.when(f == fi)
            def _(fi=fi):
                bias_out[0:1, 0:n] = q_row[:, fi * n : (fi + 1) * n]
                bias_out[1:2, 0:n] = v_row[:, fi * n : (fi + 1) * n]

        copies.append(spread_end(0))
        for copy in copies:
            copy.wait()
        net.drain()

    pl.run_scoped(
        attention_part,
        pltpu.VMEM((HL, length, LANES), BF16),
        pltpu.VMEM((HL, length, LANES), BF16),
        pltpu.VMEM((HL, length, LANES), BF16),
        pltpu.VMEM((SEQ, HL, half, LANES), BF16),
        pltpu.VMEM((HL, HEAD_DIM, length), BF16),
        pltpu.VMEM((width, length), BF16),
        pltpu.VMEM((length, LANES), BF16),
        pltpu.VMEM((HEAD_DIM, length), F32),
        pltpu.VMEM((rows, LANES), F32),
        pltpu.VMEM((rows, LANES), F32),
        pltpu.VMEM((length, 2 * LANES), BF16),
        pltpu.VMEM((HL, SEQ, 3, half, LANES), BF16),
        pltpu.VMEM((rows, 3 * width), BF16),
        pltpu.VMEM((zs if zs <= 4 else 1, 2, n, 3 * width), BF16),
        pltpu.VMEM((width, 3 * width), BF16),
    )


QB = 512
VMEM_BYTES = 127 << 19


def collect_call(qa, ka, vv, own, kt, tt, triple, tokens, ctx, par, eb, cot, wo, we, ws):
    rows, width = tokens.shape
    length = rows * SEQ
    n = triple.shape[0]
    zs = width // n // 2
    p = zs - 1
    ff = eb.shape[1]
    q = n // SEQ
    rt = (n + n // 2 + 7) // 8 * 8 + 16
    half = rows // 2
    slots = 3 * HL + 3 + 1 + p + 3 + p + zs + 3 * (4 + 2 + p + 4) + HL * (3 + 1 + p + 3)
    vm = pl.BlockSpec(memory_space=pltpu.VMEM)
    hbm = pl.BlockSpec(memory_space=pl.ANY)
    if q % 8 == 0:
        shapes = ((q, width), (q, ff), (n, width))
    else:
        shapes = ((n, 256), (n, ff // SEQ), (n, width))

    def per_weight(make):
        return [pltpu.VMEM(make(a, b), BF16) for a, b in shapes]

    outs = pl.pallas_call(
        functools.partial(collect_kernel, zs),
        out_shape=(
            jax.ShapeDtypeStruct((rows, width), BF16),
            jax.ShapeDtypeStruct((rows, width), BF16),
            jax.ShapeDtypeStruct((n, 3 * width), F32),
            jax.ShapeDtypeStruct((8, LANES), F32),
            jax.ShapeDtypeStruct((16, LANES), F32),
        )
        + tuple(jax.ShapeDtypeStruct((SEQ, a, b), BF16) for a, b in shapes)
        + (jax.ShapeDtypeStruct((zs, 2, n, 3 * width), BF16),),
        in_specs=[hbm] * 7 + [vm] * 5 + [hbm] * 3,
        out_specs=(hbm, vm, vm, vm, vm, hbm, hbm, hbm, hbm),
        scratch_shapes=[
            pltpu.VMEM((SEQ, HL, half, LANES), BF16),
            pltpu.VMEM((SEQ, HL, half, LANES), BF16),
            pltpu.VMEM((HL, SEQ, 3, half, LANES), BF16),
            pltpu.VMEM((rows, width), F32),
            pltpu.VMEM((8, width), F32),
            pltpu.VMEM((1, ff), F32),
            pltpu.VMEM((HL, 2, zs, rt, LANES), BF16),
            pltpu.VMEM((HL, zs, rt, LANES), BF16),
            pltpu.VMEM((HL, p, rt, LANES), BF16),
            pltpu.VMEM((HL, SEQ, rt, LANES), BF16),
            pltpu.VMEM((2, zs, 16, LANES), F32),
            pltpu.VMEM((zs, 16, LANES), F32),
            pltpu.VMEM((p, 16, LANES), F32),
            pltpu.VMEM((SEQ, 16, LANES), F32),
        ]
        + per_weight(lambda a, b: (2, zs, SEQ, a, b))
        + per_weight(lambda a, b: (zs, SEQ, a, b))
        + per_weight(lambda a, b: (zs, 2, a, b // 2))
        + per_weight(lambda a, b: (zs, 2, a, b // 2))
        + per_weight(lambda a, b: (zs, a, b // 2))
        + per_weight(lambda a, b: (zs, a, b // 2))
        + per_weight(lambda a, b: (p, a, b))
        + per_weight(lambda a, b: (SEQ, a, b))
        + [
            pltpu.SemaphoreType.DMA((slots,)),
            pltpu.SemaphoreType.DMA((slots,)),
            pltpu.SemaphoreType.DMA((8,)),
        ],
        compiler_params=pltpu.CompilerParams(
            collective_id=1, has_side_effects=True, vmem_limit_bytes=VMEM_BYTES
        ),
        name="collect",
    )(qa, ka, vv, own, kt, tt, triple, tokens, ctx, par, eb, cot, wo, we, ws)
    lout, tg, trip, bias, small, go, ge, gs, _ = outs
    if q % 8 == 0:
        go, ge = go.reshape(n, width), ge.reshape(n, ff)
    else:
        go = go[:, :, : width // SEQ].transpose(1, 0, 2).reshape(n, width)
        ge = ge.transpose(1, 0, 2).reshape(n, ff)
    return lout, tg, trip, bias, small, go, ge, gs.reshape(4 * n, width)


def body(
    tokens,
    segment,
    padding,
    triple_weight,
    query_bias,
    value_bias,
    output_weight,
    output_bias,
    first_gain,
    first_shift,
    expand_weight,
    expand_bias,
    shrink_weight,
    shrink_bias,
    second_gain,
    second_shift,
    cotangent,
):
    n = output_weight.shape[0]
    small = pack_small(
        query_bias,
        value_bias,
        output_bias,
        first_gain,
        first_shift,
        shrink_bias,
        second_gain,
        second_shift,
        expand_bias,
    )
    qa, ka, vv, own, kt, tt, context, par, eb, wo, we, ws = gather_call(
        tokens[0], segment, padding, triple_weight, small, output_weight, expand_weight, shrink_weight
    )
    layer_out, tokens_grad, triple_grad, bias_grad, small_grad, go, ge, gs = collect_call(
        qa, ka, vv, own, kt, tt, triple_weight, tokens[0], context, par, eb, cotangent[0], wo, we, ws
    )
    return (
        layer_out[None],
        tokens_grad[None],
        triple_grad,
        bias_grad[0, :n],
        bias_grad[1, :n],
        go.astype(F32),
        small_grad[2, :n],
        small_grad[3, :n],
        small_grad[4, :n],
        ge.astype(F32),
        small_grad[8:12, :n].reshape(4 * n),
        gs.astype(F32),
        small_grad[5, :n],
        small_grad[6, :n],
        small_grad[7, :n],
    )


def solution(mesh):
    return jax.shard_map(
        body,
        mesh=mesh,
        in_specs=(
            P("fsdp", "seq", None),
            P("fsdp", None),
            P("fsdp", None),
            P("fsdp", None),
            P("fsdp"),
            P("fsdp"),
            P("fsdp", None),
            P("fsdp"),
            P("fsdp"),
            P("fsdp"),
            P("fsdp", None),
            P("fsdp"),
            P("fsdp", None),
            P("fsdp"),
            P("fsdp"),
            P("fsdp"),
            P("fsdp", "seq", None),
        ),
        out_specs=(
            P("fsdp", "seq", None),
            P("fsdp", "seq", None),
            P("fsdp", None),
            P("fsdp"),
            P("fsdp"),
            P("fsdp", None),
            P("fsdp"),
            P("fsdp"),
            P("fsdp"),
            P("fsdp", None),
            P("fsdp"),
            P("fsdp", None),
            P("fsdp"),
            P("fsdp"),
            P("fsdp"),
        ),
        check_vma=False,
    )
```

```python
import functools

import jax
import jax.numpy as jnp
from jax import lax
from jax.experimental import pallas as pl
from jax.experimental.pallas import tpu as pltpu
from jax.sharding import PartitionSpec as P

HEADS = 12
HEAD_DIM = 64
EPS = 1e-06
MASKED = -1e30
MESH = pl.DeviceIdType.MESH
F32 = jnp.float32
BF16 = jnp.bfloat16
SEQ = 4
HL = HEADS // SEQ
LANES = 128


def ring(s):
    return (s + 1 - 2 * (s % 2), (s + 2) % 4, 3 - s)


class Net:
    def __init__(self, send, recv):
        self.send, self.recv, self.next = send, recv, 0
        self.pending = {}

    def slot(self):
        self.next += 1
        return self.next - 1

    def copy(self, i, src, dst, device):
        return pltpu.make_async_remote_copy(
            src_ref=src,
            dst_ref=dst,
            send_sem=self.send.at[i],
            recv_sem=self.recv.at[i],
            device_id=device,
            device_id_type=MESH,
        )

    def start(self, i, src, dst, device):
        copy = self.copy(i, src, dst, device)
        copy.start()
        self.pending[i] = copy.wait_send

    def begin(self, i, make):
        self.copy(i, *make()).start()
        self.pending[i] = lambda: self.copy(i, *make()).wait_send()

    def arrived(self, i, dst, device):
        self.copy(i, dst, dst, device).wait_recv()

    def drain(self):
        for wait in self.pending.values():
            wait()
        self.pending = {}


def gather_kernel(
    zs,
    tok,
    seg,
    pad,
    trip,
    small,
    wo,
    we,
    ws,
    qa_out,
    ka_out,
    v_out,
    own_out,
    kt_out,
    tt_out,
    ctx_out,
    par_out,
    eb_out,
    wo_out,
    we_out,
    ws_out,
    wo_all,
    we_all,
    ws_all,
    tokbuf,
    wsend,
    wbuf,
    wpad,
    smallbuf,
    qa,
    ka,
    vv,
    kt,
    tt,
    qmask,
    kmask,
    ctxsend,
    ctxrecv,
    send,
    recv,
    local,
):
    s = lax.axis_index("seq")
    f = lax.axis_index("fsdp")
    z, c = f // 2, f % 2
    rows, width = tok.shape
    length = rows * SEQ
    part = wsend.shape[1]
    n = trip.shape[0]
    hw = HL * HEAD_DIM
    s1, s2, s3 = ring(s)
    zpeers = [((z + j) % zs, (z - j + zs) % zs) for j in range(1, zs)]
    sib = (s, z * 2 + 1 - c)

    for t in range(SEQ):

        @pl.when(s == t)
        def _(t=t):
            for j in range(3):
                wsend[:, j * hw : (j + 1) * hw] = trip[:, j * width + t * hw : j * width + (t + 1) * hw]

    barrier = pltpu.get_barrier_semaphore()
    partners = [(s1, f), (s2, f), (s3, f), sib] + [(s, zt * 2 + c) for zt, _ in zpeers]
    for partner in partners:
        pl.semaphore_signal(barrier, inc=1, device_id=partner, device_id_type=MESH)
    pl.semaphore_wait(barrier, len(partners))

    net = Net(send, recv)
    half = rows // 2
    lo, hi = pl.ds(0, half), pl.ds(half, half)

    t_1lo, t_1hi, t_2lo, t_2hi, t_3lo, t_3hi = [net.slot() for _ in range(6)]
    net.start(t_1lo, tok.at[lo], tokbuf.at[s, lo], (s1, f))
    net.start(t_2hi, tok.at[hi], tokbuf.at[s, hi], (s2, f))
    w_z = [net.slot() for _ in zpeers]
    p_z = [net.slot() for _ in zpeers]
    w_sib = [net.slot() for _ in range(zs)]
    p_sib = [net.slot() for _ in range(zs)]

    for j, (zt, _) in enumerate(zpeers):
        net.start(w_z[j], wsend, wbuf.at[z, c], (s, zt * 2 + c))
        net.start(p_z[j], small, smallbuf.at[z, c], (s, zt * 2 + c))
    net.start(w_sib[0], wsend, wbuf.at[z, c], sib)
    net.start(p_sib[0], small, smallbuf.at[z, c], sib)
    net.start(t_1hi, tok.at[hi], tokbuf.at[s, hi], (s1, f))
    net.start(t_2lo, tok.at[lo], tokbuf.at[s, lo], (s2, f))
    weights = ((wo, wo_all), (we, we_all), (ws, ws_all))
    f_z = [[net.slot() for _ in weights] for _ in zpeers]
    for i, (mine, full) in enumerate(weights):
        for j, (zt, _) in enumerate(zpeers):
            net.start(f_z[j][i], mine.at[s], full.at[z, c, s], (s, zt * 2 + c))
    f_sib = [[net.slot() for _ in weights] for _ in range(zs)]
    for i, (mine, full) in enumerate(weights):
        net.start(f_sib[0][i], mine, full.at[z, c], sib)
    for mine, full in weights:
        full[z, c] = mine[...]
    wbuf[z, c] = wsend[...]
    smallbuf[z, c] = small[...]
    tokbuf[s] = tok[...]

    row_id = lax.broadcasted_iota(jnp.int32, (LANES, length), 0) - HEAD_DIM
    seg_row = jnp.broadcast_to(seg[...], (LANES, length))
    pad_row = jnp.broadcast_to(pad[...], (LANES, length))
    here = (row_id == seg_row) & (row_id >= 0)
    live_row = row_id == 32
    q_t = jnp.where(live_row, pad_row.astype(F32), jnp.where(here, 1.0, 0.0))
    qmask[...] = q_t.T
    inside = (row_id >= 0) & (row_id < 16)
    k_t = jnp.where(inside & jnp.logical_not(here & (pad_row == 1)), MASKED, 0.0)
    k_t = jnp.where((row_id >= 16) & (row_id < 19), 1.0, k_t)
    kmask[...] = k_t.T.astype(BF16)

    net.arrived(t_1lo, tokbuf.at[s1, lo], (s1, f))
    net.start(t_3lo, tokbuf.at[s1, lo], tokbuf.at[s1, lo], (s2, f))
    net.arrived(t_2hi, tokbuf.at[s2, hi], (s2, f))
    net.start(t_3hi, tokbuf.at[s2, hi], tokbuf.at[s2, hi], (s1, f))

    for j, (_, zf) in enumerate(zpeers):
        net.arrived(w_z[j], wbuf.at[zf, c], (s, zf * 2 + c))
        net.start(w_sib[j + 1], wbuf.at[zf, c], wbuf.at[zf, c], sib)
        net.arrived(p_z[j], smallbuf.at[zf, c], (s, zf * 2 + c))
        net.start(p_sib[j + 1], smallbuf.at[zf, c], smallbuf.at[zf, c], sib)

    net.arrived(w_sib[0], wbuf.at[z, 1 - c], sib)
    net.arrived(p_sib[0], smallbuf.at[z, 1 - c], sib)
    for j, (_, zf) in enumerate(zpeers):
        net.arrived(w_sib[j + 1], wbuf.at[zf, 1 - c], sib)
        net.arrived(p_sib[j + 1], smallbuf.at[zf, 1 - c], sib)

    for zi in range(zs):
        for ci in range(2):
            fi = zi * 2 + ci
            block = smallbuf[zi, ci].astype(F32)
            par_out[:, fi * n : (fi + 1) * n] = block[:, :n]
            for r in range(4):
                at = fi * 4 * n + r * n
                eb_out[:, at : at + n] = block[8 + r : 9 + r, :n]

    wpad[...] = jnp.zeros_like(wpad)
    for zi in range(zs):
        for ci in range(2):
            fi = zi * 2 + ci
            for k in range(3 * HL):
                wpad[fi * n : (fi + 1) * n, k * LANES : k * LANES + HEAD_DIM] = wbuf[
                    zi, ci, :, k * HEAD_DIM : (k + 1) * HEAD_DIM
                ]
    bias = jnp.zeros((2, HL * LANES), F32)
    zero = jnp.zeros((2, HEAD_DIM), F32)
    for t in range(SEQ):
        pieces = []
        for h in range(HL):
            pieces += [par_out[0:2, t * hw + h * HEAD_DIM : t * hw + (h + 1) * HEAD_DIM], zero]
        bias = jnp.where(s == t, jnp.concatenate(pieces, axis=1), bias)
    lane = lax.broadcasted_iota(jnp.int32, (1, LANES), 1)
    ones_lane = jnp.where((lane == HEAD_DIM) | (lane == HEAD_DIM + 1), 1.0, 0.0)

    def project(block):
        x = tokbuf[block]
        at = pl.ds(pl.multiple_of(block * rows, rows), rows)
        group = HL * LANES

        def part(k):
            return jnp.dot(x, wpad[:, k * group : (k + 1) * group], preferred_element_type=F32)

        qm = jnp.where(lane < HEAD_DIM + 16, qmask[at, :], 0.0).astype(BF16)
        q = ((part(0) + bias[0:1, :]).astype(BF16) * BF16(HEAD_DIM**-0.5))
        k = part(1).astype(BF16)
        v = part(2) + bias[1:2, :]
        for h in range(HL):
            cut = slice(h * LANES, (h + 1) * LANES)
            qa[h, at, :] = q[:, cut] + qm
            ka[h, at, :] = k[:, cut] + kmask[at, :]
            vv[h, at, :] = (v[:, cut] + ones_lane).astype(BF16)

    project(s)
    net.arrived(t_1hi, tokbuf.at[s1, hi], (s1, f))
    project(s1)
    net.arrived(t_2lo, tokbuf.at[s2, lo], (s2, f))
    project(s2)
    net.arrived(t_3lo, tokbuf.at[s3, lo], (s2, f))
    net.arrived(t_3hi, tokbuf.at[s3, hi], (s1, f))
    project(s3)

    f_1 = [[net.slot() for _ in weights] for _ in zpeers]
    f_2 = [[net.slot() for _ in weights] for _ in zpeers]
    f_3lo = [[net.slot() for _ in weights] for _ in zpeers]
    f_3hi = [[net.slot() for _ in weights] for _ in zpeers]

    def spread(i):
        full = weights[i][1]
        for j, (_, zf) in enumerate(zpeers):
            net.arrived(f_z[j][i], full.at[zf, c, s], (s, zf * 2 + c))
            net.start(f_1[j][i], full.at[zf, c, s], full.at[zf, c, s], (s1, f))
            net.start(f_2[j][i], full.at[zf, c, s], full.at[zf, c, s], (s2, f))

    def halves(full, zf, src, which):
        w = full.shape[-1] // 2
        return full.at[zf, c, src, :, pl.ds(which * w, w)]

    def pass_on(i):
        full = weights[i][1]
        for j, (_, zf) in enumerate(zpeers):
            net.arrived(f_1[j][i], full.at[zf, c, s1], (s1, f))
            net.start(f_3lo[j][i], halves(full, zf, s1, 0), halves(full, zf, s1, 0), (s2, f))
            net.arrived(f_2[j][i], full.at[zf, c, s2], (s2, f))
            net.start(f_3hi[j][i], halves(full, zf, s2, 1), halves(full, zf, s2, 1), (s1, f))

    def finish(i):
        full = weights[i][1]
        for j, (_, zf) in enumerate(zpeers):
            net.arrived(f_3lo[j][i], halves(full, zf, s3, 0), (s2, f))
            net.arrived(f_3hi[j][i], halves(full, zf, s3, 1), (s1, f))
            net.start(f_sib[j + 1][i], full.at[zf, c], full.at[zf, c], sib)

    c_1, c_2, c_3 = [net.slot() for _ in range(3)]
    qt = min(256, rows)

    def attend(block):
        @pl.loop(0, HL)
        def _(h):
            @pl.loop(0, rows // qt)
            def _(i):
                at = pl.multiple_of(block * rows + i * qt, qt)
                scores = lax.dot_general(
                    qa[h, pl.ds(at, qt), :],
                    ka[h],
                    (((1,), (1,)), ((), ())),
                    preferred_element_type=F32,
                )
                top = jnp.max(scores, axis=-1, keepdims=True)
                probs = jnp.exp(scores - top).astype(BF16)
                out = jnp.dot(probs, vv[h], preferred_element_type=F32)
                total = out[:, HEAD_DIM : HEAD_DIM + 1]
                live = qmask[pl.ds(at, qt), HEAD_DIM + 32 : HEAD_DIM + 33]
                ctx = (out * (live / total)).astype(BF16)[:, :HEAD_DIM]
                lse = jnp.where(live > 0.0, top + jnp.log(total), -MASKED)
                lse = -lse
                hi = lse.astype(BF16).astype(F32)
                mid = (lse - hi).astype(BF16).astype(F32)
                rest = lse - hi - mid
                base = HEAD_DIM + 16
                extra = jnp.where(lane == base, hi, jnp.where(lane == base + 1, mid, jnp.where(lane == base + 2, rest, 0.0)))
                qa[h, pl.ds(at, qt), :] = qa[h, pl.ds(at, qt), :] + extra.astype(BF16)
                per = half // qt
                down = pl.multiple_of((i % per) * qt, qt)

                @pl.when(i < per)
                def _():
                    ctxsend[block, h, pl.ds(down, qt), 0:HEAD_DIM] = ctx

                @pl.when(i >= per)
                def _():
                    ctxsend[block, h, pl.ds(down, qt), HEAD_DIM:LANES] = ctx

    spread(0)
    spread(1)
    attend(s3)
    net.start(c_3, ctxsend.at[s3], ctxrecv.at[s], (s3, f))
    spread(2)
    attend(s1)
    net.start(c_1, ctxsend.at[s1], ctxrecv.at[s], (s1, f))
    pass_on(0)
    pass_on(1)
    attend(s2)
    net.start(c_2, ctxsend.at[s2], ctxrecv.at[s], (s2, f))
    pass_on(2)
    attend(s)
    ctxrecv[s] = ctxsend[s]
    outs = []

    def save(i, src, dst):
        copy = pltpu.make_async_copy(src, dst, local.at[3 + i])
        copy.start()
        outs.append(copy)

    for i, (src, dst) in enumerate(((qa, qa_out), (ka, ka_out), (vv, v_out), (ctxsend, own_out))):
        save(i, src, dst)

    @pl.loop(0, HL)
    def _(h):
        kt[h] = ka[h].T[0:HEAD_DIM]

    @pl.loop(0, SEQ)
    def _(t):
        at = pl.multiple_of(t * rows, rows)
        tt[:, pl.ds(at, rows)] = tokbuf[t].T

    save(4, kt, kt_out)
    save(5, tt, tt_out)
    net.arrived(c_3, ctxrecv.at[s3], (s3, f))
    net.arrived(c_1, ctxrecv.at[s1], (s1, f))
    net.arrived(c_2, ctxrecv.at[s2], (s2, f))
    for t in range(SEQ):
        for h in range(HL):
            at = t * hw + h * HEAD_DIM
            ctx_out[0:half, at : at + HEAD_DIM] = ctxrecv[t, h, :, 0:HEAD_DIM]
            ctx_out[half:rows, at : at + HEAD_DIM] = ctxrecv[t, h, :, HEAD_DIM:LANES]
    for i in range(3):
        finish(i)
    for i, (dst, (_, full)) in enumerate(zip((wo_out, we_out, ws_out), weights)):
        net.arrived(f_sib[0][i], full.at[z, 1 - c], sib)
        for j, (_, zf) in enumerate(zpeers):
            net.arrived(f_sib[j + 1][i], full.at[zf, 1 - c], sib)
        copy = pltpu.make_async_copy(full, dst, local.at[i])
        copy.start()
        outs.append(copy)
    for copy in outs:
        copy.wait()
    net.drain()


def gather_slots(zs):
    p = zs - 1
    return 6 + 2 * p + 2 * zs + 3 * p + 3 * zs + 12 * p + 3


def gather_call(tokens, segment, padding, triple, small, wo, we, ws):
    rows, width = tokens.shape
    length = rows * SEQ
    n = triple.shape[0]
    shards = width // n
    zs = shards // 2
    hw = HL * HEAD_DIM
    ff = we.shape[1]
    slots = gather_slots(zs)
    vm = pl.BlockSpec(memory_space=pltpu.VMEM)
    hbm = pl.BlockSpec(memory_space=pl.ANY)
    q, qs = n // SEQ, ws.shape[0] // SEQ
    out_shape = (
        jax.ShapeDtypeStruct((HL, length, LANES), BF16),
        jax.ShapeDtypeStruct((HL, length, LANES), BF16),
        jax.ShapeDtypeStruct((HL, length, LANES), BF16),
        jax.ShapeDtypeStruct((SEQ, HL, rows // 2, LANES), BF16),
        jax.ShapeDtypeStruct((HL, HEAD_DIM, length), BF16),
        jax.ShapeDtypeStruct((width, length), BF16),
        jax.ShapeDtypeStruct((rows, width), BF16),
        jax.ShapeDtypeStruct((16, width), F32),
        jax.ShapeDtypeStruct((1, ff), F32),
        jax.ShapeDtypeStruct((zs, 2, SEQ, q, width), BF16),
        jax.ShapeDtypeStruct((zs, 2, SEQ, q, ff), BF16),
        jax.ShapeDtypeStruct((zs, 2, SEQ, qs, width), BF16),
    )
    outs = pl.pallas_call(
        functools.partial(gather_kernel, zs),
        out_shape=out_shape,
        in_specs=[vm] * 8,
        out_specs=(hbm, hbm, hbm, hbm, hbm, hbm, vm, vm, vm, hbm, hbm, hbm),
        scratch_shapes=[
            pltpu.VMEM((zs, 2, SEQ, q, width), BF16),
            pltpu.VMEM((zs, 2, SEQ, q, ff), BF16),
            pltpu.VMEM((zs, 2, SEQ, qs, width), BF16),
            pltpu.VMEM((SEQ, rows, width), BF16),
            pltpu.VMEM((n, 3 * hw), BF16),
            pltpu.VMEM((zs, 2, n, 3 * hw), BF16),
            pltpu.VMEM((width, 3 * HL * LANES), BF16),
            pltpu.VMEM((zs, 2, 16, LANES), BF16),
            pltpu.VMEM((HL, length, LANES), BF16),
            pltpu.VMEM((HL, length, LANES), BF16),
            pltpu.VMEM((HL, length, LANES), BF16),
            pltpu.VMEM((HL, HEAD_DIM, length), BF16),
            pltpu.VMEM((width, length), BF16),
            pltpu.VMEM((length, LANES), F32),
            pltpu.VMEM((length, LANES), BF16),
            pltpu.VMEM((SEQ, HL, rows // 2, LANES), BF16),
            pltpu.VMEM((SEQ, HL, rows // 2, LANES), BF16),
            pltpu.SemaphoreType.DMA((slots,)),
            pltpu.SemaphoreType.DMA((slots,)),
            pltpu.SemaphoreType.DMA((9,)),
        ],
        compiler_params=pltpu.CompilerParams(
            collective_id=0, has_side_effects=True, vmem_limit_bytes=60 << 20
        ),
        name="gather_attend",
    )(
        tokens,
        segment,
        padding,
        triple,
        small,
        wo.reshape(SEQ, q, width),
        we.reshape(SEQ, q, ff),
        ws.reshape(SEQ, qs, width),
    )
    qa, ka, vv, own, kt, tt, ctx, par, eb, wof, wef, wsf = outs
    return (
        qa,
        ka,
        vv,
        own,
        kt,
        tt,
        ctx,
        par,
        eb,
        wof.reshape(width, width),
        wef.reshape(width, ff),
        wsf.reshape(ff, width),
    )


def finish_kernel(
    lout,
    tg,
    trip,
    go,
    ge,
    gs,
    bias,
    small,
    o_lout,
    o_tg,
    o_trip,
    o_qb,
    o_vb,
    o_go,
    o_ob,
    o_g1,
    o_s1,
    o_ge,
    o_eb,
    o_gs,
    o_sb,
    o_g2,
    o_s2,
    b_lout,
    b_tg,
    b_trip,
    b_go,
    b_ge,
    b_gs,
    f_go,
    f_ge,
    f_gs,
    sem_in,
    sem_out,
):
    ins = ((ge, b_ge), (gs, b_gs), (trip, b_trip), (lout, b_lout), (tg, b_tg), (go, b_go))
    loads = [pltpu.make_async_copy(src, dst, sem_in.at[i]) for i, (src, dst) in enumerate(ins)]
    for copy in loads:
        copy.start()
    n = o_qb.shape[0]
    o_qb[...] = bias[0, :n]
    o_vb[...] = bias[1, :n]
    for r, ref in ((2, o_ob), (3, o_g1), (4, o_s1), (5, o_sb), (6, o_g2), (7, o_s2)):
        ref[...] = small[r, :n]
    for r in range(4):
        o_eb[pl.ds(r * n, n)] = small[8 + r, :n]
    outs = ((f_ge, o_ge), (f_gs, o_gs), (b_trip, o_trip), (b_lout, o_lout), (b_tg, o_tg), (f_go, o_go))
    wide = {0: (b_ge, f_ge), 1: (b_gs, f_gs), 5: (b_go, f_go)}
    stores = []
    for i, (src, dst) in enumerate(outs):
        loads[i].wait()
        if i in wide:
            wide[i][1][...] = wide[i][0][...].astype(F32)
        copy = pltpu.make_async_copy(src, dst, sem_out.at[i])
        copy.start()
        stores.append(copy)
    for copy in stores:
        copy.wait()


def finish_call(lout, tg, trip, go, ge, gs, bias, small, n):
    vm = pl.BlockSpec(memory_space=pltpu.VMEM)
    hbm = pl.BlockSpec(memory_space=pl.ANY)

    def like(x, dtype=None):
        return jax.ShapeDtypeStruct(x.shape, dtype or x.dtype)

    vec = jax.ShapeDtypeStruct((n,), F32)
    big = (lout, tg, trip, go, ge, gs)
    return pl.pallas_call(
        finish_kernel,
        out_shape=(
            like(lout),
            like(tg),
            like(trip),
            vec,
            vec,
            like(go, F32),
            vec,
            vec,
            vec,
            like(ge, F32),
            jax.ShapeDtypeStruct((4 * n,), F32),
            like(gs, F32),
            vec,
            vec,
            vec,
        ),
        in_specs=[hbm] * 6 + [vm] * 2,
        out_specs=(hbm, hbm, hbm, vm, vm, hbm, vm, vm, vm, hbm, vm, hbm, vm, vm, vm),
        scratch_shapes=[pltpu.VMEM(x.shape, x.dtype) for x in big]
        + [pltpu.VMEM(x.shape, F32) for x in (go, ge, gs)]
        + [pltpu.SemaphoreType.DMA((6,)), pltpu.SemaphoreType.DMA((6,))],
        compiler_params=pltpu.CompilerParams(vmem_limit_bytes=VMEM_BYTES),
        name="finish",
    )(*big, bias, small)


def pack_small(query_bias, value_bias, output_bias, first_gain, first_shift, shrink_bias, second_gain, second_shift, expand_bias):
    n = query_bias.shape[0]
    rows = [query_bias, value_bias, output_bias, first_gain, first_shift, shrink_bias, second_gain, second_shift]
    table = jnp.concatenate([jnp.stack(rows), expand_bias.reshape(4, n)], axis=0)
    return jnp.pad(table, ((0, 4), (0, LANES - n)))


def norm_parts(hidden):
    center = hidden - jnp.mean(hidden, axis=-1, keepdims=True)
    factor = lax.rsqrt(jnp.mean(center * center, axis=-1, keepdims=True) + EPS)
    return center * factor, factor


def norm_back(grad, normal, factor, gain):
    c = grad * gain
    mean = jnp.mean(c, axis=-1, keepdims=True)
    inner = jnp.mean(c * normal, axis=-1, keepdims=True)
    return factor * (c - mean - normal * inner)


NT = (((1,), (1,)), ((), ()))
TN = (((0,), (0,)), ((), ()))


def middle(
    refs,
    grads,
    shrink_ready,
    shrink_go,
    context_ready,
    loads,
    out_sem,
    wo,
    we,
    ws,
    nl,
    nlt,
    n1,
    r1,
    act,
    slope,
    sl,
):
    tok, ctx, par, eb, cot, lout, gfirst, vecs, ebg = refs
    g_out, g_exp, g_shr = grads
    rows, width = tok.shape
    ff = eb.shape[1]
    zs = g_out.shape[1]
    n = width // (2 * zs)
    tile = min(128, rows)
    wide = 256
    vecs[...] = jnp.zeros_like(vecs)

    def add_row(r, value):
        vecs[r : r + 1, :] = vecs[r : r + 1, :] + jnp.sum(value, axis=0, keepdims=True)

    loads[0].wait()

    @pl.loop(0, width // wide)
    def _(j):
        at = pl.ds(pl.multiple_of(j * wide, wide), wide)
        gfirst[:, at] = jnp.dot(ctx[...], wo[:, at], preferred_element_type=F32)

    @pl.loop(0, rows // tile)
    def _(i):
        at = pl.ds(pl.multiple_of(i * tile, tile), tile)
        normal, factor = norm_parts(tok[at, :].astype(F32) + gfirst[at, :] + par[2:3, :])
        n1[at, :] = normal
        r1[at, :] = factor
        nl[at, :] = (normal * par[3:4, :] + par[4:5, :]).astype(BF16)

    loads[1].wait()

    @pl.loop(0, ff // wide)
    def _(j):
        at = pl.ds(pl.multiple_of(j * wide, wide), wide)
        u = jnp.dot(nl[...], we[:, at], preferred_element_type=F32) + eb[:, at]
        phi = 0.5 + 0.5 * lax.erf(u * 0.5**0.5)
        act[:, at] = (u * phi).astype(BF16)
        slope[:, at] = (phi + u * (jnp.exp(-0.5 * u * u) * (2.0 * 3.141592653589793) ** -0.5)).astype(BF16)

    nlt[...] = nl[...].T
    loads[2].wait()

    @pl.loop(0, width // wide)
    def _(j):
        at = pl.ds(pl.multiple_of(j * wide, wide), wide)
        gfirst[:, at] = jnp.dot(act[...], ws[:, at], preferred_element_type=F32)

    @pl.loop(0, rows // tile)
    def _(i):
        at = pl.ds(pl.multiple_of(i * tile, tile), tile)
        second = n1[at, :] * par[3:4, :] + par[4:5, :] + par[5:6, :] + gfirst[at, :]
        normal, factor = norm_parts(second)
        nl[at, :] = (normal * par[6:7, :] + par[7:8, :]).astype(BF16)
        e = cot[at, :].astype(F32)
        add_row(6, e * normal)
        add_row(7, e)
        back = norm_back(e, normal, factor, par[6:7, :])
        gfirst[at, :] = back
        low = back.astype(BF16)
        sl[at, :] = low
        add_row(5, low.astype(F32))

    result = pltpu.make_async_copy(nl, lout, out_sem)
    result.start()
    per = max(1, 384 // (4 * n))

    @pl.loop(0, ff // (per * 4 * n))
    def _(j):
        at = pl.ds(pl.multiple_of(j * per * 4 * n, LANES), per * 4 * n)
        g = lax.dot_general(act[:, at], sl[...], TN, preferred_element_type=F32)
        for k in range(per):
            fi = j * per + k
            for qi in range(SEQ):
                lo = (k * SEQ + qi) * n
                g_shr[fi % 2, fi // 2, qi] = g[lo : lo + n].astype(BF16)

    shrink_ready()

    @pl.loop(0, ff // wide)
    def _(j):
        at = pl.ds(pl.multiple_of(j * wide, wide), wide)
        back = lax.dot_general(sl[...], ws[at, :], NT, preferred_element_type=F32)
        low = (back * slope[:, at].astype(F32)).astype(BF16)
        act[:, at] = low
        ebg[:, at] = jnp.sum(low.astype(F32), axis=0, keepdims=True)

    shrink_go()

    @pl.loop(0, width // wide)
    def _(j):
        at = pl.ds(pl.multiple_of(j * wide, wide), wide)
        gfirst[:, at] += lax.dot_general(act[...], we[at, :], NT, preferred_element_type=F32)

    @pl.loop(0, rows // tile)
    def _(i):
        at = pl.ds(pl.multiple_of(i * tile, tile), tile)
        e = gfirst[at, :]
        normal = n1[at, :]
        add_row(3, e * normal)
        add_row(4, e)
        back = norm_back(e, normal, r1[at, :], par[3:4, :])
        gfirst[at, :] = back
        low = back.astype(BF16)
        sl[at, :] = low
        add_row(2, low.astype(F32))

    context_ready()
    q = n // SEQ

    def keep(grad, g, j, at):
        if q % 8 == 0:
            for fi in range(2 * zs):
                for qi in range(SEQ):
                    lo = fi * n + qi * q
                    grad[fi % 2, fi // 2, qi, :, at] = g[lo : lo + q].astype(BF16)
        else:
            blocks = ff // SEQ // wide
            for fi in range(2 * zs):
                grad[fi % 2, fi // 2, j // blocks, :, pl.ds(pl.multiple_of(j % blocks * wide, wide), wide)] = g[
                    fi * n : (fi + 1) * n
                ].astype(BF16)

    @pl.loop(0, ff // wide)
    def _(j):
        at = pl.ds(pl.multiple_of(j * wide, wide), wide)
        keep(g_exp, jnp.dot(nlt[...], act[:, at], preferred_element_type=F32), j, at)

    if q % 8 == 0:

        @pl.loop(0, width // wide)
        def _(j):
            at = pl.ds(pl.multiple_of(j * wide, wide), wide)
            keep(g_out, lax.dot_general(ctx[...], sl[:, at], TN, preferred_element_type=F32), j, at)

    else:
        w = width // SEQ
        for qi in range(SEQ):
            g = lax.dot_general(ctx[...], sl[:, qi * w : (qi + 1) * w], TN, preferred_element_type=F32)
            for fi in range(2 * zs):
                g_out[fi % 2, fi // 2, qi, :, 0:w] = g[fi * n : (fi + 1) * n].astype(BF16)

    result.wait()


def collect_kernel(
    zs,
    qa_hbm,
    ka_hbm,
    v_hbm,
    own_hbm,
    kt_hbm,
    tt_hbm,
    trip,
    tokens,
    ctx,
    par,
    eb,
    cot,
    wo_hbm,
    we_hbm,
    ws_hbm,
    lout,
    tg_out,
    trip_out,
    bias_out,
    small_out,
    go_out,
    ge_out,
    gs_out,
    wland,
    dsend,
    drecv,
    grecv,
    gfirst,
    vecs,
    ebg,
    tsend,
    tcore,
    tz,
    tfin,
    svec,
    svcore,
    svz,
    svseq,
    ao,
    ae,
    a_s,
    co,
    ce,
    cs,
    xo,
    xe,
    xs,
    yo,
    ye,
    ys,
    x2o,
    x2e,
    x2s,
    y2o,
    y2e,
    y2s,
    zo,
    ze,
    zsm,
    fo,
    fe,
    fs,
    send,
    recv,
    local,
):
    s = lax.axis_index("seq")
    f = lax.axis_index("fsdp")
    z, c = f // 2, f % 2
    rows, width = tokens.shape
    half = rows // 2
    length = rows * SEQ
    n = trip.shape[0]
    hw = HL * HEAD_DIM
    s1, s2, s3 = ring(s)
    zpeers = [((z + j) % zs, (z - j + zs) % zs) for j in range(1, zs)]
    sib = (s, z * 2 + 1 - c)
    net = Net(send, recv)
    lane = lax.broadcasted_iota(jnp.int32, (1, LANES), 1)

    barrier = pltpu.get_barrier_semaphore()
    partners = [(s1, f), (s2, f), (s3, f), sib] + [(s, zt * 2 + c) for zt, _ in zpeers]
    for partner in partners:
        pl.semaphore_signal(barrier, inc=1, device_id=partner, device_id_type=MESH)
    pl.semaphore_wait(barrier, len(partners))

    w_z = [net.slot() for _ in zpeers]
    w_sib = [net.slot() for _ in range(zs)]
    for j, (zt, _) in enumerate(zpeers):
        net.start(w_z[j], trip, wland.at[z, c], (s, zt * 2 + c))
    net.start(w_sib[0], trip, wland.at[z, c], sib)
    own_copy = pltpu.make_async_copy(trip, wland.at[z, c], local.at[0])
    own_copy.start()

    d_sem = [[net.slot() for _ in range(3)] for _ in range(HL)]
    grads, core = (ao, ae, a_s), (co, ce, cs)
    c_sem = [net.slot() for _ in range(3)]

    def core_start(i):
        net.begin(c_sem[i], lambda: (grads[i].at[1 - c], core[i], sib))

    v_core = net.slot()
    v_z = [net.slot() for _ in zpeers]
    v_seq = [net.slot() for _ in range(3)]

    def small_start():
        for zi in range(zs):
            for ci in range(2):
                fi = zi * 2 + ci
                svec[ci, zi] = jnp.zeros((16, LANES), F32)
                svec[ci, zi, 0:8, 0:n] = vecs[:, fi * n : (fi + 1) * n]
                for r in range(4):
                    at = fi * 4 * n + r * n
                    svec[ci, zi, 8 + r : 9 + r, 0:n] = ebg[:, at : at + n]
        net.start(v_core, svec.at[1 - c], svcore, sib)

    xr, yr, x2r, y2r, zr, fin = (xo, xe, xs), (yo, ye, ys), (x2o, x2e, x2s), (y2o, y2e, y2s), (zo, ze, zsm), (fo, fe, fs)
    x_sem = [[net.slot() for _ in range(4)] for _ in range(3)]
    x2_sem = [[net.slot() for _ in range(2)] for _ in range(3)]
    z_sem = [[net.slot() for _ in zpeers] for _ in range(3)]
    a_sem = [[net.slot() for _ in range(4)] for _ in range(3)]

    def cols(i, which):
        w = grads[i].shape[-1] // 2
        return pl.ds(which * w, w)

    def plane_start(i):
        net.arrived(c_sem[i], core[i], sib)

        @pl.loop(0, zs * SEQ)
        def _(k):
            zi, qi = k // SEQ, k % SEQ
            total = grads[i][c, zi, qi].astype(F32) + core[i][zi, qi].astype(F32)
            grads[i][c, zi, qi] = total.astype(BF16)

        x, y = cols(i, 0), cols(i, 1)
        net.begin(x_sem[i][0], lambda: (grads[i].at[c, :, s3, :, x], xr[i].at[:, 1], (s1, f)))
        net.begin(x_sem[i][2], lambda: (grads[i].at[c, :, s3, :, y], yr[i].at[:, 1], (s2, f)))
        net.begin(x_sem[i][1], lambda: (grads[i].at[c, :, s1, :, x], xr[i].at[:, 0], (s1, f)))
        net.begin(x_sem[i][3], lambda: (grads[i].at[c, :, s2, :, y], yr[i].at[:, 0], (s2, f)))

    def add_into(i, part, qi, which, from_ref):
        w = grads[i].shape[-1] // 2

        @pl.loop(0, zs)
        def _(zi):
            a = grads[i][c, zi, qi, :, which * w : (which + 1) * w].astype(F32)
            b = (from_ref[zi] if part is None else from_ref[zi, part]).astype(F32)
            grads[i][c, zi, qi, :, which * w : (which + 1) * w] = (a + b).astype(BF16)

    def plane_second(i):
        net.arrived(x_sem[i][0], xr[i].at[:, 1], (s1, f))
        add_into(i, 1, s2, 0, xr[i])
        net.begin(x2_sem[i][0], lambda: (grads[i].at[c, :, s2, :, cols(i, 0)], x2r[i], (s2, f)))
        net.arrived(x_sem[i][2], yr[i].at[:, 1], (s2, f))
        add_into(i, 1, s1, 1, yr[i])
        net.begin(x2_sem[i][1], lambda: (grads[i].at[c, :, s1, :, cols(i, 1)], y2r[i], (s1, f)))
        net.arrived(x_sem[i][1], xr[i].at[:, 0], (s1, f))
        add_into(i, 0, s, 0, xr[i])
        net.arrived(x_sem[i][3], yr[i].at[:, 0], (s2, f))
        add_into(i, 0, s, 1, yr[i])

    def along_z(i):
        net.arrived(x2_sem[i][0], x2r[i], (s2, f))
        add_into(i, None, s, 0, x2r[i])
        net.arrived(x2_sem[i][1], y2r[i], (s1, f))
        add_into(i, None, s, 1, y2r[i])
        for j, (zt, _) in enumerate(zpeers):
            net.begin(z_sem[i][j], lambda zt=zt, j=j: (grads[i].at[c, zt, s], zr[i].at[j], (s, zt * 2 + c)))

    def own_rows(i):
        total = grads[i][c, z, s].astype(F32)
        for j, (_, zf) in enumerate(zpeers):
            net.arrived(z_sem[i][j], zr[i].at[j], (s, zf * 2 + c))
            total = total + zr[i][j].astype(F32)
        fin[i][s] = total.astype(BF16)
        net.begin(a_sem[i][0], lambda: (fin[i].at[s], fin[i].at[s], (s1, f)))
        net.begin(a_sem[i][1], lambda: (fin[i].at[s], fin[i].at[s], (s2, f)))

    def spread(i):
        net.arrived(a_sem[i][0], fin[i].at[s1], (s1, f))
        net.begin(a_sem[i][2], lambda: (fin[i].at[s1, :, cols(i, 0)], fin[i].at[s1, :, cols(i, 0)], (s2, f)))
        net.arrived(a_sem[i][1], fin[i].at[s2], (s2, f))
        net.begin(a_sem[i][3], lambda: (fin[i].at[s2, :, cols(i, 1)], fin[i].at[s2, :, cols(i, 1)], (s1, f)))

    final_out = (go_out, ge_out, gs_out)

    def spread_end(i):
        net.arrived(a_sem[i][2], fin[i].at[s3, :, cols(i, 0)], (s2, f))
        net.arrived(a_sem[i][3], fin[i].at[s3, :, cols(i, 1)], (s1, f))
        copy = pltpu.make_async_copy(fin[i], final_out[i], local.at[1 + i])
        copy.start()
        return copy

    def context_ready(wo, al):
        for t in range(SEQ):
            at = t * hw
            back = lax.dot_general(al[...], wo[at : at + hw, :], NT, preferred_element_type=F32).astype(BF16)
            for h in range(HL):
                dsend[t, h, :, 0:HEAD_DIM] = back[0:half, h * HEAD_DIM : (h + 1) * HEAD_DIM]
                dsend[t, h, :, HEAD_DIM:LANES] = back[half:rows, h * HEAD_DIM : (h + 1) * HEAD_DIM]
        for h in range(HL):
            for k, peer in enumerate((s3, s1, s2)):
                net.begin(d_sem[h][k], lambda peer=peer, h=h: (dsend.at[peer, h], drecv.at[s, h], (peer, f)))
        drecv[s] = dsend[s]

    def tokens_part(wo, we, ws, nl, nlt, n1, r1, act, slope, sl):
        loads = []
        for i, (src, dst) in enumerate(((wo_hbm, wo), (we_hbm, we), (ws_hbm, ws))):
            copy = pltpu.make_async_copy(src, dst, local.at[1 + i])
            copy.start()
            loads.append(copy)
        middle(
            (tokens, ctx, par, eb, cot, lout, gfirst, vecs, ebg),
            grads,
            lambda: core_start(2),
            lambda: plane_start(2),
            lambda: context_ready(wo, sl),
            loads,
            local.at[4],
            wo,
            we,
            ws,
            nl,
            nlt,
            n1,
            r1,
            act,
            slope,
            sl,
        )

    ff = eb.shape[1]
    pl.run_scoped(
        tokens_part,
        pltpu.VMEM((width, width), BF16),
        pltpu.VMEM((width, ff), BF16),
        pltpu.VMEM((ff, width), BF16),
        pltpu.VMEM((rows, width), BF16),
        pltpu.VMEM((width, rows), BF16),
        pltpu.VMEM((rows, width), F32),
        pltpu.VMEM((rows, 1), F32),
        pltpu.VMEM((rows, ff), BF16),
        pltpu.VMEM((rows, ff), BF16),
        pltpu.VMEM((rows, width), BF16),
    )
    core_start(1)
    core_start(0)
    small_start()
    own_copy.wait()

    def attention_part(qa, ka, vv, own, k_t, tok_t, da, dq_t, acc_k, acc_v, gm, gsend, gmr, wfull, wtmp=None):
        loads = []
        pairs = ((qa_hbm, qa), (ka_hbm, ka), (v_hbm, vv), (own_hbm, own), (kt_hbm, k_t), (tt_hbm, tok_t))
        for i, (src, dst) in enumerate(pairs):
            copy = pltpu.make_async_copy(src, dst, local.at[1 + i])
            copy.start()
            loads.append(copy)
        gm[...] = jnp.zeros_like(gm)
        plane_start(1)
        plane_start(0)
        for copy in loads:
            copy.wait()

        net.arrived(v_core, svcore, sib)
        svec[c] = svec[c] + svcore[...]
        for j, (zt, _) in enumerate(zpeers):
            net.start(v_z[j], svec.at[c, zt], svz.at[j], (s, zt * 2 + c))

        for j, (_, zf) in enumerate(zpeers):
            net.arrived(w_z[j], wland.at[zf, c], (s, zf * 2 + c))
            net.start(w_sib[j + 1], wland.at[zf, c], wland.at[zf, c], sib)

        g_sem = [[net.slot() for _ in range(3)] for _ in range(HL)]
        tc_sem = [net.slot() for _ in range(HL)]
        tz_sem = [[net.slot() for _ in zpeers] for _ in range(HL)]
        ts_sem = [[net.slot() for _ in range(3)] for _ in range(HL)]

        def prepare(h):
            for k, peer in enumerate((s3, s1, s2)):
                net.arrived(d_sem[h][k], drecv.at[peer, h], (peer, f))

            @pl.loop(0, SEQ)
            def _(t):
                grad = drecv[t, h].astype(F32)
                prod = grad * own[t, h].astype(F32)
                left = lane < HEAD_DIM
                for k in range(2):
                    inner = -jnp.sum(jnp.where(left if k == 0 else jnp.logical_not(left), prod, 0.0), axis=-1, keepdims=True)
                    hi = inner.astype(BF16).astype(F32)
                    here = grad if k == 0 else pltpu.roll(grad, HEAD_DIM, 1)
                    here = jnp.where(left, here, jnp.where(lane == HEAD_DIM, hi, jnp.where(lane == HEAD_DIM + 1, inner - hi, 0.0)))
                    at = pl.multiple_of(t * rows + k * half, half)
                    da[pl.ds(at, half), :] = here.astype(BF16)

            dq_t[...] = jnp.zeros_like(dq_t)

        def key_block(h, r):
            acc_k[...] = jnp.zeros_like(acc_k)
            acc_v[...] = jnp.zeros_like(acc_v)
            keys = pl.multiple_of(r * rows, rows)
            nt = (((1,), (1,)), ((), ()))

            @pl.loop(0, length // QB)
            def _(i):
                at = pl.multiple_of(i * QB, QB)
                q = qa[h, pl.ds(at, QB), :]
                grad = da[pl.ds(at, QB), :]
                probs = jnp.exp(lax.dot_general(ka[h, pl.ds(keys, rows), :], q, nt, preferred_element_type=F32))
                inner = lax.dot_general(vv[h, pl.ds(keys, rows), :], grad, nt, preferred_element_type=F32)
                ds = (probs * inner).astype(BF16)
                acc_v[...] += jnp.dot(probs.astype(BF16), grad, preferred_element_type=F32)
                acc_k[...] += jnp.dot(ds, q, preferred_element_type=F32)
                dq_t[:, pl.ds(at, QB)] += jnp.dot(k_t[h, :, pl.ds(keys, rows)], ds, preferred_element_type=F32)

            gm[pl.ds(keys, rows), HEAD_DIM:LANES] = acc_k[:, 0:HEAD_DIM].astype(BF16)
            gm[pl.ds(keys, rows), LANES : LANES + HEAD_DIM] = acc_v[:, 0:HEAD_DIM].astype(BF16)

        rt = tsend.shape[3]
        vrow = n + n // 2
        brow = rt - 16

        def head_done(h):
            @pl.loop(0, SEQ)
            def _(t):
                at = pl.multiple_of(t * rows, rows)
                dq = (dq_t[:, pl.ds(at, rows)].T * (HEAD_DIM**-0.5)).astype(BF16)
                gm[pl.ds(at, rows), 0:HEAD_DIM] = dq
                for k in range(3):
                    for p in range(2):
                        piece = gm[pl.ds(at + p * half, half), k * HEAD_DIM : (k + 1) * HEAD_DIM]
                        gsend[h, t, k, :, p * HEAD_DIM : (p + 1) * HEAD_DIM] = piece

            for k, peer in enumerate((s3, s1, s2)):
                net.start(g_sem[h][k], gsend.at[h, peer], grecv.at[h, s], (peer, f))
            grecv[h, s] = gsend[h, s]
            sums = jnp.sum(gm[...].astype(F32), axis=0, keepdims=True).astype(BF16)
            whole = jnp.dot(tok_t[...], gm[...], preferred_element_type=F32)
            for zi in range(zs):
                for ci in range(2):
                    fi = zi * 2 + ci
                    grad = whole[fi * n : (fi + 1) * n].astype(BF16)
                    tsend[h, ci, zi, 0:n, :] = grad[:, 0:LANES]
                    tsend[h, ci, zi, n:vrow, 0:HEAD_DIM] = grad[0 : n // 2, LANES : LANES + HEAD_DIM]
                    tsend[h, ci, zi, n:vrow, HEAD_DIM:LANES] = grad[n // 2 : n, LANES : LANES + HEAD_DIM]
                    tsend[h, ci, zi, brow:rt, :] = jnp.broadcast_to(sums[:, 0:LANES], (16, LANES))
                    tsend[h, ci, zi, brow + 8 : rt, :] = jnp.broadcast_to(sums[:, LANES : 2 * LANES], (8, LANES))
            net.start(tc_sem[h], tsend.at[h, 1 - c], tcore.at[h], sib)

        def triple_z(h):
            net.arrived(tc_sem[h], tcore.at[h], sib)
            tsend[h, c] = (tsend[h, c].astype(F32) + tcore[h].astype(F32)).astype(BF16)
            for j, (zt, _) in enumerate(zpeers):
                net.begin(tz_sem[h][j], lambda zt=zt, j=j: (tsend.at[h, c, zt], tz.at[h, j], (s, zt * 2 + c)))

        def triple_own(h):
            total = tsend[h, c, z].astype(F32)
            for j, (_, zf) in enumerate(zpeers):
                net.arrived(tz_sem[h][j], tz.at[h, j], (s, zf * 2 + c))
                total = total + tz[h, j].astype(F32)
            tfin[h, s] = total.astype(BF16)
            for k, peer in enumerate((s3, s1, s2)):
                net.begin(ts_sem[h][k], lambda peer=peer: (tfin.at[h, s], tfin.at[h, s], (peer, f)))

        def rows_in(h):
            for k, peer in enumerate((s3, s1, s2)):
                net.arrived(g_sem[h][k], grecv.at[h, peer], (peer, f))
            for t in range(SEQ):
                for k in range(3):
                    at = k * width + t * hw + h * HEAD_DIM
                    gmr[0:half, at : at + HEAD_DIM] = grecv[h, t, k, :, 0:HEAD_DIM]
                    gmr[half:rows, at : at + HEAD_DIM] = grecv[h, t, k, :, HEAD_DIM:LANES]

        def attend_back(h, *steps):
            @pl.loop(0, SEQ)
            def _(r):
                key_block(h, r)
                for k, step in enumerate(steps):

                    @pl.when(r == k)
                    def _(step=step):
                        for call, arg in step:
                            call(arg)

        plane_second(2)
        prepare(0)
        attend_back(0)
        head_done(0)
        prepare(1)
        attend_back(
            1,
            [(plane_second, 1), (triple_z, 0)],
            [(along_z, 2), (plane_second, 0)],
        )
        head_done(1)
        total = svec[c, z]
        for j, (_, zf) in enumerate(zpeers):
            net.arrived(v_z[j], svz.at[j], (s, zf * 2 + c))
            total = total + svz[j]
        svseq[s] = total
        for k, peer in enumerate((s3, s1, s2)):
            net.start(v_seq[k], svseq.at[s], svseq.at[s], (peer, f))
        prepare(2)
        attend_back(
            2,
            [(triple_own, 0)],
            [(own_rows, 2), (along_z, 1)],
            [(along_z, 0), (triple_z, 1)],
        )
        head_done(2)
        spread(2)
        rows_in(0)
        net.arrived(w_sib[0], wland.at[z, 1 - c], sib)
        for j, (_, zf) in enumerate(zpeers):
            net.arrived(w_sib[j + 1], wland.at[zf, 1 - c], sib)
        depth = zs if zs <= 4 else 1
        for base in range(0, zs, depth):
            if zs > 4:
                copy = pltpu.make_async_copy(wland.at[pl.ds(base, depth)], wtmp, local.at[0])
                copy.start()
                copy.wait()
            for zi in range(depth):
                for ci in range(2):
                    fi = (base + zi) * 2 + ci
                    wfull[fi * n : (fi + 1) * n, :] = (wtmp if zs > 4 else wland)[zi, ci]
        triple_own(1)
        triple_z(2)
        own_rows(1)
        own_rows(0)
        rows_in(1)
        triple_own(2)
        spread(1)
        spread(0)
        rows_in(2)
        wide = 256

        @pl.loop(0, width // wide)
        def _(j):
            at = pl.ds(pl.multiple_of(j * wide, wide), wide)
            back = lax.dot_general(gmr[...], wfull[at, :], NT, preferred_element_type=F32)
            tg_out[:, at] = (gfirst[:, at] + back).astype(BF16)

        copies = [spread_end(2), spread_end(1)]
        for k, peer in enumerate((s3, s1, s2)):
            net.arrived(v_seq[k], svseq.at[peer], (peer, f))
        small_out[...] = svseq[0] + svseq[1] + svseq[2] + svseq[3]
        for h in range(HL):
            for k, peer in enumerate((s3, s1, s2)):
                net.arrived(ts_sem[h][k], tfin.at[h, peer], (peer, f))
        q_row, v_row = [], []
        for t in range(SEQ):
            for h in range(HL):
                at = t * hw + h * HEAD_DIM
                block = tfin[h, t].astype(F32)
                trip_out[:, at : at + HEAD_DIM] = block[0:n, 0:HEAD_DIM]
                trip_out[:, width + at : width + at + HEAD_DIM] = block[0:n, HEAD_DIM:LANES]
                trip_out[0 : n // 2, 2 * width + at : 2 * width + at + HEAD_DIM] = block[n:vrow, 0:HEAD_DIM]
                trip_out[n // 2 : n, 2 * width + at : 2 * width + at + HEAD_DIM] = block[n:vrow, HEAD_DIM:LANES]
                q_row.append(block[brow : brow + 1, 0:HEAD_DIM])
                v_row.append(block[brow + 8 : brow + 9, 0:HEAD_DIM])
        q_row, v_row = jnp.concatenate(q_row, axis=1), jnp.concatenate(v_row, axis=1)
        bias_out[...] = jnp.zeros_like(bias_out)
        for fi in range(2 * zs):

            @pl.when(f == fi)
            def _(fi=fi):
                bias_out[0:1, 0:n] = q_row[:, fi * n : (fi + 1) * n]
                bias_out[1:2, 0:n] = v_row[:, fi * n : (fi + 1) * n]

        copies.append(spread_end(0))
        for copy in copies:
            copy.wait()
        net.drain()

    pl.run_scoped(
        attention_part,
        pltpu.VMEM((HL, length, LANES), BF16),
        pltpu.VMEM((HL, length, LANES), BF16),
        pltpu.VMEM((HL, length, LANES), BF16),
        pltpu.VMEM((SEQ, HL, half, LANES), BF16),
        pltpu.VMEM((HL, HEAD_DIM, length), BF16),
        pltpu.VMEM((width, length), BF16),
        pltpu.VMEM((length, LANES), BF16),
        pltpu.VMEM((HEAD_DIM, length), F32),
        pltpu.VMEM((rows, LANES), F32),
        pltpu.VMEM((rows, LANES), F32),
        pltpu.VMEM((length, 2 * LANES), BF16),
        pltpu.VMEM((HL, SEQ, 3, half, LANES), BF16),
        pltpu.VMEM((rows, 3 * width), BF16),
        pltpu.VMEM((width, 3 * width), BF16),
        *([pltpu.VMEM((1, 2, n, 3 * width), BF16)] if zs > 4 else []),
    )


QB = 512
VMEM_BYTES = 127 << 19


def collect_call(qa, ka, vv, own, kt, tt, triple, tokens, ctx, par, eb, cot, wo, we, ws):
    rows, width = tokens.shape
    length = rows * SEQ
    n = triple.shape[0]
    zs = width // n // 2
    p = zs - 1
    ff = eb.shape[1]
    q = n // SEQ
    rt = (n + n // 2 + 7) // 8 * 8 + 16
    half = rows // 2
    slots = 3 * HL + 3 + 1 + p + 3 + p + zs + 3 * (4 + 2 + p + 4) + HL * (3 + 1 + p + 3)
    vm = pl.BlockSpec(memory_space=pltpu.VMEM)
    hbm = pl.BlockSpec(memory_space=pl.ANY)
    if q % 8 == 0:
        shapes = ((q, width), (q, ff), (n, width))
    else:
        shapes = ((n, 256), (n, ff // SEQ), (n, width))

    def per_weight(make):
        return [pltpu.VMEM(make(a, b), BF16) for a, b in shapes]

    outs = pl.pallas_call(
        functools.partial(collect_kernel, zs),
        out_shape=(
            jax.ShapeDtypeStruct((rows, width), BF16),
            jax.ShapeDtypeStruct((rows, width), BF16),
            jax.ShapeDtypeStruct((n, 3 * width), F32),
            jax.ShapeDtypeStruct((8, LANES), F32),
            jax.ShapeDtypeStruct((16, LANES), F32),
        )
        + tuple(jax.ShapeDtypeStruct((SEQ, a, b), BF16) for a, b in shapes)
        + ((jax.ShapeDtypeStruct((zs, 2, n, 3 * width), BF16),) if zs > 4 else ()),
        in_specs=[hbm] * 6 + [vm] * 6 + [hbm] * 3,
        out_specs=(hbm, vm, vm, vm, vm, hbm, hbm, hbm) + ((hbm,) if zs > 4 else ()),
        scratch_shapes=([] if zs > 4 else [pltpu.VMEM((zs, 2, n, 3 * width), BF16)])
        + [
            pltpu.VMEM((SEQ, HL, half, LANES), BF16),
            pltpu.VMEM((SEQ, HL, half, LANES), BF16),
            pltpu.VMEM((HL, SEQ, 3, half, LANES), BF16),
            pltpu.VMEM((rows, width), F32),
            pltpu.VMEM((8, width), F32),
            pltpu.VMEM((1, ff), F32),
            pltpu.VMEM((HL, 2, zs, rt, LANES), BF16),
            pltpu.VMEM((HL, zs, rt, LANES), BF16),
            pltpu.VMEM((HL, p, rt, LANES), BF16),
            pltpu.VMEM((HL, SEQ, rt, LANES), BF16),
            pltpu.VMEM((2, zs, 16, LANES), F32),
            pltpu.VMEM((zs, 16, LANES), F32),
            pltpu.VMEM((p, 16, LANES), F32),
            pltpu.VMEM((SEQ, 16, LANES), F32),
        ]
        + per_weight(lambda a, b: (2, zs, SEQ, a, b))
        + per_weight(lambda a, b: (zs, SEQ, a, b))
        + per_weight(lambda a, b: (zs, 2, a, b // 2))
        + per_weight(lambda a, b: (zs, 2, a, b // 2))
        + per_weight(lambda a, b: (zs, a, b // 2))
        + per_weight(lambda a, b: (zs, a, b // 2))
        + per_weight(lambda a, b: (p, a, b))
        + per_weight(lambda a, b: (SEQ, a, b))
        + [
            pltpu.SemaphoreType.DMA((slots,)),
            pltpu.SemaphoreType.DMA((slots,)),
            pltpu.SemaphoreType.DMA((8,)),
        ],
        compiler_params=pltpu.CompilerParams(
            collective_id=1, has_side_effects=True, vmem_limit_bytes=VMEM_BYTES
        ),
        name="collect",
    )(qa, ka, vv, own, kt, tt, triple, tokens, ctx, par, eb, cot, wo, we, ws)
    lout, tg, trip, bias, small, go, ge, gs = outs[:8]
    if q % 8 == 0:
        go, ge = go.reshape(n, width), ge.reshape(n, ff)
    else:
        go = go[:, :, : width // SEQ].transpose(1, 0, 2).reshape(n, width)
        ge = ge.transpose(1, 0, 2).reshape(n, ff)
    return lout, tg, trip, bias, small, go, ge, gs.reshape(4 * n, width)


def body(
    tokens,
    segment,
    padding,
    triple_weight,
    query_bias,
    value_bias,
    output_weight,
    output_bias,
    first_gain,
    first_shift,
    expand_weight,
    expand_bias,
    shrink_weight,
    shrink_bias,
    second_gain,
    second_shift,
    cotangent,
):
    n = output_weight.shape[0]
    small = pack_small(
        query_bias,
        value_bias,
        output_bias,
        first_gain,
        first_shift,
        shrink_bias,
        second_gain,
        second_shift,
        expand_bias,
    )
    qa, ka, vv, own, kt, tt, context, par, eb, wo, we, ws = gather_call(
        tokens[0], segment, padding, triple_weight, small, output_weight, expand_weight, shrink_weight
    )
    layer_out, tokens_grad, triple_grad, bias_grad, small_grad, go, ge, gs = collect_call(
        qa, ka, vv, own, kt, tt, triple_weight, tokens[0], context, par, eb, cotangent[0], wo, we, ws
    )
    outs = finish_call(layer_out, tokens_grad, triple_grad, go, ge, gs, bias_grad, small_grad, n)
    return (outs[0][None], outs[1][None]) + tuple(outs[2:])


def solution(mesh):
    return jax.shard_map(
        body,
        mesh=mesh,
        in_specs=(
            P("fsdp", "seq", None),
            P("fsdp", None),
            P("fsdp", None),
            P("fsdp", None),
            P("fsdp"),
            P("fsdp"),
            P("fsdp", None),
            P("fsdp"),
            P("fsdp"),
            P("fsdp"),
            P("fsdp", None),
            P("fsdp"),
            P("fsdp", None),
            P("fsdp"),
            P("fsdp"),
            P("fsdp"),
            P("fsdp", "seq", None),
        ),
        out_specs=(
            P("fsdp", "seq", None),
            P("fsdp", "seq", None),
            P("fsdp", None),
            P("fsdp"),
            P("fsdp"),
            P("fsdp", None),
            P("fsdp"),
            P("fsdp"),
            P("fsdp"),
            P("fsdp", None),
            P("fsdp"),
            P("fsdp", None),
            P("fsdp"),
            P("fsdp"),
            P("fsdp"),
        ),
        check_vma=False,
    )
```

```python
import functools

import jax
import jax.numpy as jnp
from jax import lax
from jax.experimental import pallas as pl
from jax.experimental.pallas import tpu as pltpu
from jax.sharding import PartitionSpec as P

HEADS = 12
HEAD_DIM = 64
EPS = 1e-06
MASKED = -1e30
MESH = pl.DeviceIdType.MESH
F32 = jnp.float32
BF16 = jnp.bfloat16
SEQ = 4
HL = HEADS // SEQ
LANES = 128
NEAR = 512


def ring(s):
    return (s + 1 - 2 * (s % 2), (s + 2) % 4, 3 - s)


class Net:
    def __init__(self, send, recv):
        self.send, self.recv, self.next = send, recv, 0
        self.pending = {}

    def slot(self):
        self.next += 1
        return self.next - 1

    def copy(self, i, src, dst, device):
        return pltpu.make_async_remote_copy(
            src_ref=src,
            dst_ref=dst,
            send_sem=self.send.at[i],
            recv_sem=self.recv.at[i],
            device_id=device,
            device_id_type=MESH,
        )

    def start(self, i, src, dst, device):
        copy = self.copy(i, src, dst, device)
        copy.start()
        self.pending[i] = copy.wait_send

    def begin(self, i, make):
        self.copy(i, *make()).start()
        self.pending[i] = lambda: self.copy(i, *make()).wait_send()

    def arrived(self, i, dst, device):
        self.copy(i, dst, dst, device).wait_recv()

    def drain(self):
        for wait in self.pending.values():
            wait()
        self.pending = {}


def gather_kernel(
    zs,
    tok,
    seg,
    pad,
    trip,
    v0,
    v1,
    v2,
    v3,
    v4,
    v5,
    v6,
    v7,
    v8,
    wo,
    we,
    ws,
    qa_out,
    ka_out,
    v_out,
    own_out,
    kt_out,
    tt_out,
    ctx_out,
    par_out,
    eb_out,
    wo_out,
    we_out,
    ws_out,
    wo_all,
    we_all,
    ws_all,
    tokbuf,
    small,
    wsend,
    wbuf,
    wpad,
    smallbuf,
    qa,
    ka,
    vv,
    kt,
    tt,
    qmask,
    kmask,
    ctxsend,
    ctxrecv,
    send,
    recv,
    local,
):
    s = lax.axis_index("seq")
    f = lax.axis_index("fsdp")
    z, c = f // 2, f % 2
    rows, width = tok.shape
    length = rows * SEQ
    part = wsend.shape[1]
    n = trip.shape[0]
    hw = HL * HEAD_DIM
    s1, s2, s3 = ring(s)
    zpeers = [((z + j) % zs, (z - j + zs) % zs) for j in range(1, zs)]
    sib = (s, z * 2 + 1 - c)

    barrier = pltpu.get_barrier_semaphore()
    partners = [(s1, f), (s2, f), (s3, f), sib] + [(s, zt * 2 + c) for zt, _ in zpeers]
    for partner in partners:
        pl.semaphore_signal(barrier, inc=1, device_id=partner, device_id_type=MESH)
    small[...] = jnp.zeros_like(small)
    for r, ref in enumerate((v0, v1, v2, v3, v4, v5, v6, v7)):
        small[r : r + 1, 0:n] = ref[...].astype(F32).reshape(1, n)
    for r in range(4):
        small[8 + r : 9 + r, 0:n] = v8[pl.ds(r * n, n)].astype(F32).reshape(1, n)

    for t in range(SEQ):

        @pl.when(s == t)
        def _(t=t):
            for j in range(3):
                wsend[:, j * hw : (j + 1) * hw] = trip[:, j * width + t * hw : j * width + (t + 1) * hw]

    pl.semaphore_wait(barrier, len(partners))

    net = Net(send, recv)
    half = rows // 2
    lo, hi = pl.ds(0, half), pl.ds(half, half)

    t_1lo, t_1hi, t_2lo, t_2hi, t_3lo, t_3hi = [net.slot() for _ in range(6)]
    net.start(t_1lo, tok.at[lo], tokbuf.at[s, lo], (s1, f))
    net.start(t_2hi, tok.at[hi], tokbuf.at[s, hi], (s2, f))
    w_z = [net.slot() for _ in zpeers]
    p_z = [net.slot() for _ in zpeers]
    w_sib = [net.slot() for _ in range(zs)]
    p_sib = [net.slot() for _ in range(zs)]

    for j, (zt, _) in enumerate(zpeers):
        net.start(w_z[j], wsend, wbuf.at[z, c], (s, zt * 2 + c))
        net.start(p_z[j], small, smallbuf.at[z, c], (s, zt * 2 + c))
    net.start(w_sib[0], wsend, wbuf.at[z, c], sib)
    net.start(p_sib[0], small, smallbuf.at[z, c], sib)
    net.start(t_1hi, tok.at[hi], tokbuf.at[s, hi], (s1, f))
    net.start(t_2lo, tok.at[lo], tokbuf.at[s, lo], (s2, f))
    weights = ((wo, wo_all), (we, we_all), (ws, ws_all))
    f_z = [[net.slot() for _ in weights] for _ in zpeers]

    near = pl.ds(0, NEAR)
    far = pl.ds(NEAR, width - NEAR)
    f_far = [net.slot() for _ in zpeers]

    def quarter(i, zi, src):
        ref = weights[i][1].at[zi, c, src]
        return ref.at[:, near] if i == 2 else ref

    def along(i):
        mine = weights[i][0].at[s]
        mine = mine.at[:, near] if i == 2 else mine
        for j, (zt, _) in enumerate(zpeers):
            net.start(f_z[j][i], mine, quarter(i, z, s), (s, zt * 2 + c))

    def along_whole():
        for j, (zt, _) in enumerate(zpeers):
            net.start(f_z[j][0], wo, wo_all.at[z, c], (s, zt * 2 + c))
        for j, (zt, _) in enumerate(zpeers):
            net.start(f_far[j], ws.at[:, :, far], ws_all.at[z, c, :, :, far], (s, zt * 2 + c))

    f_sib = [[net.slot() for _ in weights] for _ in range(zs)]
    for i, (mine, full) in enumerate(weights):
        net.start(f_sib[0][i], mine, full.at[z, c], sib)
    for mine, full in weights:
        full[z, c] = mine[...]
    wbuf[z, c] = wsend[...]
    smallbuf[z, c] = small[...]
    tokbuf[s] = tok[...]

    row_id = lax.broadcasted_iota(jnp.int32, (LANES, length), 0) - HEAD_DIM
    seg_row = jnp.broadcast_to(seg[...], (LANES, length))
    pad_row = jnp.broadcast_to(pad[...], (LANES, length))
    here = (row_id == seg_row) & (row_id >= 0)
    live_row = row_id == 32
    q_t = jnp.where(live_row, pad_row.astype(F32), jnp.where(here, 1.0, 0.0))
    qmask[...] = q_t.T
    inside = (row_id >= 0) & (row_id < 16)
    k_t = jnp.where(inside & jnp.logical_not(here & (pad_row == 1)), MASKED, 0.0)
    k_t = jnp.where((row_id >= 16) & (row_id < 19), 1.0, k_t)
    kmask[...] = k_t.T.astype(BF16)

    net.arrived(t_1lo, tokbuf.at[s1, lo], (s1, f))
    net.start(t_3lo, tokbuf.at[s1, lo], tokbuf.at[s1, lo], (s2, f))
    net.arrived(t_2hi, tokbuf.at[s2, hi], (s2, f))
    net.start(t_3hi, tokbuf.at[s2, hi], tokbuf.at[s2, hi], (s1, f))

    for j, (_, zf) in enumerate(zpeers):
        net.arrived(w_z[j], wbuf.at[zf, c], (s, zf * 2 + c))
        net.start(w_sib[j + 1], wbuf.at[zf, c], wbuf.at[zf, c], sib)
        net.arrived(p_z[j], smallbuf.at[zf, c], (s, zf * 2 + c))
        net.start(p_sib[j + 1], smallbuf.at[zf, c], smallbuf.at[zf, c], sib)
    along(1)

    net.arrived(w_sib[0], wbuf.at[z, 1 - c], sib)
    net.arrived(p_sib[0], smallbuf.at[z, 1 - c], sib)
    for j, (_, zf) in enumerate(zpeers):
        net.arrived(w_sib[j + 1], wbuf.at[zf, 1 - c], sib)
        net.arrived(p_sib[j + 1], smallbuf.at[zf, 1 - c], sib)

    for zi in range(zs):
        for ci in range(2):
            fi = zi * 2 + ci
            block = smallbuf[zi, ci]
            par_out[:, fi * n : (fi + 1) * n] = block[:, :n]
            for r in range(4):
                at = fi * 4 * n + r * n
                eb_out[:, at : at + n] = block[8 + r : 9 + r, :n]

    wpad[...] = jnp.zeros_like(wpad)
    for zi in range(zs):
        for ci in range(2):
            fi = zi * 2 + ci
            for k in range(3 * HL):
                wpad[fi * n : (fi + 1) * n, k * LANES : k * LANES + HEAD_DIM] = wbuf[
                    zi, ci, :, k * HEAD_DIM : (k + 1) * HEAD_DIM
                ]
    bias = jnp.zeros((2, HL * LANES), F32)
    zero = jnp.zeros((2, HEAD_DIM), F32)
    for t in range(SEQ):
        pieces = []
        for h in range(HL):
            pieces += [par_out[0:2, t * hw + h * HEAD_DIM : t * hw + (h + 1) * HEAD_DIM], zero]
        bias = jnp.where(s == t, jnp.concatenate(pieces, axis=1), bias)
    lane = lax.broadcasted_iota(jnp.int32, (1, LANES), 1)
    ones_lane = jnp.where((lane == HEAD_DIM) | (lane == HEAD_DIM + 1), 1.0, 0.0)

    def project(block):
        x = tokbuf[block]
        at = pl.ds(pl.multiple_of(block * rows, rows), rows)
        group = HL * LANES

        def part(k):
            return jnp.dot(x, wpad[:, k * group : (k + 1) * group], preferred_element_type=F32)

        qm = jnp.where(lane < HEAD_DIM + 16, qmask[at, :], 0.0).astype(BF16)
        q = ((part(0) + bias[0:1, :]).astype(BF16) * BF16(HEAD_DIM**-0.5))
        k = part(1).astype(BF16)
        v = part(2) + bias[1:2, :]
        for h in range(HL):
            cut = slice(h * LANES, (h + 1) * LANES)
            qa[h, at, :] = q[:, cut] + qm
            ka[h, at, :] = k[:, cut] + kmask[at, :]
            vv[h, at, :] = (v[:, cut] + ones_lane).astype(BF16)

    project(s)
    net.arrived(t_1hi, tokbuf.at[s1, hi], (s1, f))
    project(s1)
    net.arrived(t_2lo, tokbuf.at[s2, lo], (s2, f))
    project(s2)
    along(2)
    net.arrived(t_3lo, tokbuf.at[s3, lo], (s2, f))
    net.arrived(t_3hi, tokbuf.at[s3, hi], (s1, f))
    project(s3)

    f_1 = [[net.slot() for _ in weights] for _ in zpeers]
    f_2 = [[net.slot() for _ in weights] for _ in zpeers]
    f_3lo = [[net.slot() for _ in weights] for _ in zpeers]
    f_3hi = [[net.slot() for _ in weights] for _ in zpeers]

    def halves(i, zf, src, which):
        w = (NEAR if i == 2 else weights[i][1].shape[-1]) // 2
        return weights[i][1].at[zf, c, src, :, pl.ds(which * w, w)]

    def spread(i):
        for j, (_, zf) in enumerate(zpeers):
            net.arrived(f_z[j][i], quarter(i, zf, s), (s, zf * 2 + c))
            net.start(f_1[j][i], quarter(i, zf, s), quarter(i, zf, s), (s1, f))
            net.start(f_2[j][i], quarter(i, zf, s), quarter(i, zf, s), (s2, f))

    def pass_on(i):
        for j, (_, zf) in enumerate(zpeers):
            net.arrived(f_1[j][i], quarter(i, zf, s1), (s1, f))
            net.start(f_3lo[j][i], halves(i, zf, s1, 0), halves(i, zf, s1, 0), (s2, f))
            net.arrived(f_2[j][i], quarter(i, zf, s2), (s2, f))
            net.start(f_3hi[j][i], halves(i, zf, s2, 1), halves(i, zf, s2, 1), (s1, f))

    def finish(i):
        for j, (_, zf) in enumerate(zpeers):
            if i == 0:
                net.arrived(f_z[j][0], wo_all.at[zf, c], (s, zf * 2 + c))
            else:
                net.arrived(f_3lo[j][i], halves(i, zf, s3, 0), (s2, f))
                net.arrived(f_3hi[j][i], halves(i, zf, s3, 1), (s1, f))
            if i == 2:
                net.arrived(f_far[j], ws_all.at[zf, c, :, :, far], (s, zf * 2 + c))
            full = weights[i][1]
            net.start(f_sib[j + 1][i], full.at[zf, c], full.at[zf, c], sib)

    c_1, c_2, c_3 = [net.slot() for _ in range(3)]
    qt = min(256, rows)

    def attend(block, first=0, last=HL):
        @pl.loop(first, last)
        def _(h):
            @pl.loop(0, rows // qt)
            def _(i):
                at = pl.multiple_of(block * rows + i * qt, qt)
                scores = lax.dot_general(
                    qa[h, pl.ds(at, qt), :],
                    ka[h],
                    (((1,), (1,)), ((), ())),
                    preferred_element_type=F32,
                )
                top = jnp.max(scores, axis=-1, keepdims=True)
                probs = jnp.exp(scores - top).astype(BF16)
                out = jnp.dot(probs, vv[h], preferred_element_type=F32)
                total = out[:, HEAD_DIM : HEAD_DIM + 1]
                live = qmask[pl.ds(at, qt), HEAD_DIM + 32 : HEAD_DIM + 33]
                ctx = (out * (live / total)).astype(BF16)[:, :HEAD_DIM]
                lse = jnp.where(live > 0.0, top + jnp.log(total), -MASKED)
                lse = -lse
                hi = lse.astype(BF16).astype(F32)
                mid = (lse - hi).astype(BF16).astype(F32)
                rest = lse - hi - mid
                base = HEAD_DIM + 16
                extra = jnp.where(lane == base, hi, jnp.where(lane == base + 1, mid, jnp.where(lane == base + 2, rest, 0.0)))
                qa[h, pl.ds(at, qt), :] = qa[h, pl.ds(at, qt), :] + extra.astype(BF16)
                per = half // qt
                down = pl.multiple_of((i % per) * qt, qt)

                @pl.when(i < per)
                def _():
                    ctxsend[block, h, pl.ds(down, qt), 0:HEAD_DIM] = ctx

                @pl.when(i >= per)
                def _():
                    ctxsend[block, h, pl.ds(down, qt), HEAD_DIM:LANES] = ctx

    spread(1)
    attend(s3)
    net.start(c_3, ctxsend.at[s3], ctxrecv.at[s], (s3, f))
    along_whole()
    spread(2)
    attend(s1)
    net.start(c_1, ctxsend.at[s1], ctxrecv.at[s], (s1, f))
    pass_on(1)
    attend(s2)
    net.start(c_2, ctxsend.at[s2], ctxrecv.at[s], (s2, f))
    pass_on(2)
    attend(s)
    ctxrecv[s] = ctxsend[s]
    outs = []

    def save(i, src, dst):
        copy = pltpu.make_async_copy(src, dst, local.at[3 + i])
        copy.start()
        outs.append(copy)

    for i, (src, dst) in enumerate(((qa, qa_out), (ka, ka_out), (vv, v_out), (ctxsend, own_out))):
        save(i, src, dst)

    @pl.loop(0, HL)
    def _(h):
        kt[h] = ka[h].T[0:HEAD_DIM]

    @pl.loop(0, SEQ)
    def _(t):
        at = pl.multiple_of(t * rows, rows)
        tt[:, pl.ds(at, rows)] = tokbuf[t].T

    save(4, kt, kt_out)
    save(5, tt, tt_out)
    net.arrived(c_3, ctxrecv.at[s3], (s3, f))
    net.arrived(c_1, ctxrecv.at[s1], (s1, f))
    net.arrived(c_2, ctxrecv.at[s2], (s2, f))
    for t in range(SEQ):
        for h in range(HL):
            at = t * hw + h * HEAD_DIM
            ctx_out[0:half, at : at + HEAD_DIM] = ctxrecv[t, h, :, 0:HEAD_DIM]
            ctx_out[half:rows, at : at + HEAD_DIM] = ctxrecv[t, h, :, HEAD_DIM:LANES]
    for i in range(3):
        finish(i)
    for i, (dst, (_, full)) in enumerate(zip((wo_out, we_out, ws_out), weights)):
        save(6 + 2 * i, full.at[:, c], dst.at[:, c])
    for i, (dst, (_, full)) in enumerate(zip((wo_out, we_out, ws_out), weights)):
        net.arrived(f_sib[0][i], full.at[z, 1 - c], sib)
        for j, (_, zf) in enumerate(zpeers):
            net.arrived(f_sib[j + 1][i], full.at[zf, 1 - c], sib)
        save(7 + 2 * i, full.at[:, 1 - c], dst.at[:, 1 - c])
    for copy in outs:
        copy.wait()
    net.drain()


def gather_slots(zs):
    p = zs - 1
    return 6 + 2 * p + 2 * zs + 3 * p + 3 * zs + 13 * p + 3


def gather_call(tokens, segment, padding, triple, small, wo, we, ws):
    rows, width = tokens.shape
    length = rows * SEQ
    n = triple.shape[0]
    shards = width // n
    zs = shards // 2
    hw = HL * HEAD_DIM
    ff = we.shape[1]
    slots = gather_slots(zs)
    vm = pl.BlockSpec(memory_space=pltpu.VMEM)
    hbm = pl.BlockSpec(memory_space=pl.ANY)
    q, qs = n // SEQ, ws.shape[0] // SEQ
    out_shape = (
        jax.ShapeDtypeStruct((HL, length, LANES), BF16),
        jax.ShapeDtypeStruct((HL, length, LANES), BF16),
        jax.ShapeDtypeStruct((HL, length, LANES), BF16),
        jax.ShapeDtypeStruct((SEQ, HL, rows // 2, LANES), BF16),
        jax.ShapeDtypeStruct((HL, HEAD_DIM, length), BF16),
        jax.ShapeDtypeStruct((width, length), BF16),
        jax.ShapeDtypeStruct((rows, width), BF16),
        jax.ShapeDtypeStruct((16, width), F32),
        jax.ShapeDtypeStruct((1, ff), F32),
        jax.ShapeDtypeStruct((zs, 2, SEQ, q, width), BF16),
        jax.ShapeDtypeStruct((zs, 2, SEQ, q, ff), BF16),
        jax.ShapeDtypeStruct((zs, 2, SEQ, qs, width), BF16),
    )
    outs = pl.pallas_call(
        functools.partial(gather_kernel, zs),
        out_shape=out_shape,
        in_specs=[vm] * 16,
        out_specs=(hbm, hbm, hbm, hbm, hbm, hbm, vm, vm, vm, hbm, hbm, hbm),
        scratch_shapes=[
            pltpu.VMEM((zs, 2, SEQ, q, width), BF16),
            pltpu.VMEM((zs, 2, SEQ, q, ff), BF16),
            pltpu.VMEM((zs, 2, SEQ, qs, width), BF16),
            pltpu.VMEM((SEQ, rows, width), BF16),
            pltpu.VMEM((16, LANES), F32),
            pltpu.VMEM((n, 3 * hw), BF16),
            pltpu.VMEM((zs, 2, n, 3 * hw), BF16),
            pltpu.VMEM((width, 3 * HL * LANES), BF16),
            pltpu.VMEM((zs, 2, 16, LANES), F32),
            pltpu.VMEM((HL, length, LANES), BF16),
            pltpu.VMEM((HL, length, LANES), BF16),
            pltpu.VMEM((HL, length, LANES), BF16),
            pltpu.VMEM((HL, HEAD_DIM, length), BF16),
            pltpu.VMEM((width, length), BF16),
            pltpu.VMEM((length, LANES), F32),
            pltpu.VMEM((length, LANES), BF16),
            pltpu.VMEM((SEQ, HL, rows // 2, LANES), BF16),
            pltpu.VMEM((SEQ, HL, rows // 2, LANES), BF16),
            pltpu.SemaphoreType.DMA((slots,)),
            pltpu.SemaphoreType.DMA((slots,)),
            pltpu.SemaphoreType.DMA((16,)),
        ],
        compiler_params=pltpu.CompilerParams(
            collective_id=0, has_side_effects=True, vmem_limit_bytes=60 << 20
        ),
        name="gather_attend",
    )(
        tokens,
        segment,
        padding,
        triple,
        *small,
        wo.reshape(SEQ, q, width),
        we.reshape(SEQ, q, ff),
        ws.reshape(SEQ, qs, width),
    )
    qa, ka, vv, own, kt, tt, ctx, par, eb, wof, wef, wsf = outs
    return (
        qa,
        ka,
        vv,
        own,
        kt,
        tt,
        ctx,
        par,
        eb,
        wof.reshape(width, width),
        wef.reshape(width, ff),
        wsf.reshape(ff, width),
    )


def finish_kernel(
    lout,
    tg,
    trip,
    go,
    ge,
    gs,
    bias,
    small,
    o_lout,
    o_tg,
    o_trip,
    o_qb,
    o_vb,
    o_go,
    o_ob,
    o_g1,
    o_s1,
    o_ge,
    o_eb,
    o_gs,
    o_sb,
    o_g2,
    o_s2,
    b_lout,
    b_tg,
    b_trip,
    b_go,
    b_ge,
    b_gs,
    f_go,
    f_ge,
    f_gs,
    sem_in,
    sem_out,
):
    ins = ((ge, b_ge), (gs, b_gs), (trip, b_trip), (lout, b_lout), (tg, b_tg), (go, b_go))
    loads = [pltpu.make_async_copy(src, dst, sem_in.at[i]) for i, (src, dst) in enumerate(ins)]
    for copy in loads:
        copy.start()
    n = o_qb.shape[0]
    o_qb[...] = bias[0, :n]
    o_vb[...] = bias[1, :n]
    for r, ref in ((2, o_ob), (3, o_g1), (4, o_s1), (5, o_sb), (6, o_g2), (7, o_s2)):
        ref[...] = small[r, :n]
    for r in range(4):
        o_eb[pl.ds(r * n, n)] = small[8 + r, :n]
    outs = ((f_ge, o_ge), (f_gs, o_gs), (b_trip, o_trip), (b_lout, o_lout), (b_tg, o_tg), (f_go, o_go))
    wide = {0: (b_ge, f_ge), 1: (b_gs, f_gs), 5: (b_go, f_go)}
    stores = []
    for i, (src, dst) in enumerate(outs):
        loads[i].wait()
        if i in wide:
            wide[i][1][...] = wide[i][0][...].astype(F32)
        copy = pltpu.make_async_copy(src, dst, sem_out.at[i])
        copy.start()
        stores.append(copy)
    for copy in stores:
        copy.wait()


def finish_call(lout, tg, trip, go, ge, gs, bias, small, n):
    vm = pl.BlockSpec(memory_space=pltpu.VMEM)
    hbm = pl.BlockSpec(memory_space=pl.ANY)

    def like(x, dtype=None):
        return jax.ShapeDtypeStruct(x.shape, dtype or x.dtype)

    vec = jax.ShapeDtypeStruct((n,), F32)
    big = (lout, tg, trip, go, ge, gs)
    return pl.pallas_call(
        finish_kernel,
        out_shape=(
            like(lout),
            like(tg),
            like(trip),
            vec,
            vec,
            like(go, F32),
            vec,
            vec,
            vec,
            like(ge, F32),
            jax.ShapeDtypeStruct((4 * n,), F32),
            like(gs, F32),
            vec,
            vec,
            vec,
        ),
        in_specs=[hbm] * 6 + [vm] * 2,
        out_specs=(hbm, hbm, hbm, vm, vm, hbm, vm, vm, vm, hbm, vm, hbm, vm, vm, vm),
        scratch_shapes=[pltpu.VMEM(x.shape, x.dtype) for x in big]
        + [pltpu.VMEM(x.shape, F32) for x in (go, ge, gs)]
        + [pltpu.SemaphoreType.DMA((6,)), pltpu.SemaphoreType.DMA((6,))],
        compiler_params=pltpu.CompilerParams(vmem_limit_bytes=VMEM_BYTES),
        name="finish",
    )(*big, bias, small)


def norm_parts(hidden):
    center = hidden - jnp.mean(hidden, axis=-1, keepdims=True)
    factor = lax.rsqrt(jnp.mean(center * center, axis=-1, keepdims=True) + EPS)
    return center * factor, factor


def norm_back(grad, normal, factor, gain):
    c = grad * gain
    mean = jnp.mean(c, axis=-1, keepdims=True)
    inner = jnp.mean(c * normal, axis=-1, keepdims=True)
    return factor * (c - mean - normal * inner)


NT = (((1,), (1,)), ((), ()))
TN = (((0,), (0,)), ((), ()))


def middle(
    refs,
    grads,
    shrink_ready,
    shrink_go,
    context_ready,
    loads,
    out_sem,
    wo,
    we,
    ws,
    nl,
    nlt,
    n1,
    r1,
    act,
    slope,
    sl,
):
    tok, ctx, par, eb, cot, lout, gfirst, vecs, ebg = refs
    g_out, g_exp, g_shr = grads
    rows, width = tok.shape
    ff = eb.shape[1]
    zs = g_out.shape[1]
    n = width // (2 * zs)
    tile = min(128, rows)
    wide = 256
    vecs[...] = jnp.zeros_like(vecs)

    def add_row(r, value):
        vecs[r : r + 1, :] = vecs[r : r + 1, :] + jnp.sum(value, axis=0, keepdims=True)

    loads[0].wait()

    @pl.loop(0, width // wide)
    def _(j):
        at = pl.ds(pl.multiple_of(j * wide, wide), wide)
        gfirst[:, at] = jnp.dot(ctx[...], wo[:, at], preferred_element_type=F32)

    @pl.loop(0, rows // tile)
    def _(i):
        at = pl.ds(pl.multiple_of(i * tile, tile), tile)
        normal, factor = norm_parts(tok[at, :].astype(F32) + gfirst[at, :] + par[2:3, :])
        n1[at, :] = normal
        r1[at, :] = factor
        nl[at, :] = (normal * par[3:4, :] + par[4:5, :]).astype(BF16)

    loads[1].wait()

    @pl.loop(0, ff // wide)
    def _(j):
        at = pl.ds(pl.multiple_of(j * wide, wide), wide)
        u = jnp.dot(nl[...], we[:, at], preferred_element_type=F32) + eb[:, at]
        phi = 0.5 + 0.5 * lax.erf(u * 0.5**0.5)
        act[:, at] = (u * phi).astype(BF16)
        slope[:, at] = (phi + u * (jnp.exp(-0.5 * u * u) * (2.0 * 3.141592653589793) ** -0.5)).astype(BF16)

    nlt[...] = nl[...].T
    loads[2].wait()

    @pl.loop(0, width // wide)
    def _(j):
        at = pl.ds(pl.multiple_of(j * wide, wide), wide)
        gfirst[:, at] = jnp.dot(act[...], ws[:, at], preferred_element_type=F32)

    @pl.loop(0, rows // tile)
    def _(i):
        at = pl.ds(pl.multiple_of(i * tile, tile), tile)
        second = n1[at, :] * par[3:4, :] + par[4:5, :] + par[5:6, :] + gfirst[at, :]
        normal, factor = norm_parts(second)
        nl[at, :] = (normal * par[6:7, :] + par[7:8, :]).astype(BF16)
        e = cot[at, :].astype(F32)
        add_row(6, e * normal)
        add_row(7, e)
        back = norm_back(e, normal, factor, par[6:7, :])
        gfirst[at, :] = back
        low = back.astype(BF16)
        sl[at, :] = low
        add_row(5, low.astype(F32))

    result = pltpu.make_async_copy(nl, lout, out_sem)
    result.start()
    per = max(1, 384 // (4 * n))

    @pl.loop(0, ff // (per * 4 * n))
    def _(j):
        at = pl.ds(pl.multiple_of(j * per * 4 * n, LANES), per * 4 * n)
        g = lax.dot_general(act[:, at], sl[...], TN, preferred_element_type=F32)
        for k in range(per):
            fi = j * per + k
            for qi in range(SEQ):
                lo = (k * SEQ + qi) * n
                g_shr[fi % 2, fi // 2, qi] = g[lo : lo + n].astype(BF16)

    shrink_ready()

    @pl.loop(0, ff // wide)
    def _(j):
        at = pl.ds(pl.multiple_of(j * wide, wide), wide)
        back = lax.dot_general(sl[...], ws[at, :], NT, preferred_element_type=F32)
        low = (back * slope[:, at].astype(F32)).astype(BF16)
        act[:, at] = low
        ebg[:, at] = jnp.sum(low.astype(F32), axis=0, keepdims=True)

    shrink_go()

    @pl.loop(0, width // wide)
    def _(j):
        at = pl.ds(pl.multiple_of(j * wide, wide), wide)
        gfirst[:, at] += lax.dot_general(act[...], we[at, :], NT, preferred_element_type=F32)

    @pl.loop(0, rows // tile)
    def _(i):
        at = pl.ds(pl.multiple_of(i * tile, tile), tile)
        e = gfirst[at, :]
        normal = n1[at, :]
        add_row(3, e * normal)
        add_row(4, e)
        back = norm_back(e, normal, r1[at, :], par[3:4, :])
        gfirst[at, :] = back
        low = back.astype(BF16)
        sl[at, :] = low
        add_row(2, low.astype(F32))

    context_ready()
    q = n // SEQ

    def keep(grad, g, j, at):
        if q % 8 == 0:
            for fi in range(2 * zs):
                for qi in range(SEQ):
                    lo = fi * n + qi * q
                    grad[fi % 2, fi // 2, qi, :, at] = g[lo : lo + q].astype(BF16)
        else:
            blocks = ff // SEQ // wide
            for fi in range(2 * zs):
                grad[fi % 2, fi // 2, j // blocks, :, pl.ds(pl.multiple_of(j % blocks * wide, wide), wide)] = g[
                    fi * n : (fi + 1) * n
                ].astype(BF16)

    @pl.loop(0, ff // wide)
    def _(j):
        at = pl.ds(pl.multiple_of(j * wide, wide), wide)
        keep(g_exp, jnp.dot(nlt[...], act[:, at], preferred_element_type=F32), j, at)

    if q % 8 == 0:

        @pl.loop(0, width // wide)
        def _(j):
            at = pl.ds(pl.multiple_of(j * wide, wide), wide)
            keep(g_out, lax.dot_general(ctx[...], sl[:, at], TN, preferred_element_type=F32), j, at)

    else:
        w = width // SEQ
        for qi in range(SEQ):
            g = lax.dot_general(ctx[...], sl[:, qi * w : (qi + 1) * w], TN, preferred_element_type=F32)
            for fi in range(2 * zs):
                g_out[fi % 2, fi // 2, qi, :, 0:w] = g[fi * n : (fi + 1) * n].astype(BF16)

    result.wait()


def collect_kernel(
    zs,
    qa_hbm,
    ka_hbm,
    v_hbm,
    own_hbm,
    kt_hbm,
    tt_hbm,
    trip,
    tokens,
    ctx,
    par,
    eb,
    cot,
    wo_hbm,
    we_hbm,
    ws_hbm,
    lout,
    tg_out,
    trip_out,
    bias_out,
    small_out,
    go_out,
    ge_out,
    gs_out,
    wland,
    dsend,
    drecv,
    grecv,
    gfirst,
    vecs,
    ebg,
    tsend,
    tcore,
    tz,
    tfin,
    svec,
    svcore,
    svz,
    svseq,
    ao,
    ae,
    a_s,
    co,
    ce,
    cs,
    xo,
    xe,
    xs,
    yo,
    ye,
    ys,
    x2o,
    x2e,
    x2s,
    y2o,
    y2e,
    y2s,
    zo,
    ze,
    zsm,
    fo,
    fe,
    fs,
    send,
    recv,
    local,
):
    s = lax.axis_index("seq")
    f = lax.axis_index("fsdp")
    z, c = f // 2, f % 2
    rows, width = tokens.shape
    half = rows // 2
    length = rows * SEQ
    n = trip.shape[0]
    hw = HL * HEAD_DIM
    s1, s2, s3 = ring(s)
    zpeers = [((z + j) % zs, (z - j + zs) % zs) for j in range(1, zs)]
    sib = (s, z * 2 + 1 - c)
    net = Net(send, recv)
    lane = lax.broadcasted_iota(jnp.int32, (1, LANES), 1)

    barrier = pltpu.get_barrier_semaphore()
    partners = [(s1, f), (s2, f), (s3, f), sib] + [(s, zt * 2 + c) for zt, _ in zpeers]
    for partner in partners:
        pl.semaphore_signal(barrier, inc=1, device_id=partner, device_id_type=MESH)

    w_z = [net.slot() for _ in zpeers]
    w_sib = [net.slot() for _ in range(zs)]
    own_copy = pltpu.make_async_copy(trip, wland.at[z, c], local.at[0])
    own_copy.start()

    def enter():
        pl.semaphore_wait(barrier, len(partners))
        for j, (zt, _) in enumerate(zpeers):
            net.begin(w_z[j], lambda zt=zt: (trip, wland.at[z, c], (s, zt * 2 + c)))
        net.begin(w_sib[0], lambda: (trip, wland.at[z, c], sib))

    def shrink_ready():
        enter()
        core_start(2)

    d_sem = [[net.slot() for _ in range(3)] for _ in range(HL)]
    grads, core = (ao, ae, a_s), (co, ce, cs)
    c_sem = [net.slot() for _ in range(3)]

    def core_start(i):
        net.begin(c_sem[i], lambda: (grads[i].at[1 - c], core[i], sib))

    v_core = net.slot()
    v_z = [net.slot() for _ in zpeers]
    v_seq = [net.slot() for _ in range(3)]

    def small_start():
        for zi in range(zs):
            for ci in range(2):
                fi = zi * 2 + ci
                svec[ci, zi] = jnp.zeros((16, LANES), F32)
                svec[ci, zi, 0:8, 0:n] = vecs[:, fi * n : (fi + 1) * n]
                for r in range(4):
                    at = fi * 4 * n + r * n
                    svec[ci, zi, 8 + r : 9 + r, 0:n] = ebg[:, at : at + n]
        net.start(v_core, svec.at[1 - c], svcore, sib)

    xr, yr, x2r, y2r, zr, fin = (xo, xe, xs), (yo, ye, ys), (x2o, x2e, x2s), (y2o, y2e, y2s), (zo, ze, zsm), (fo, fe, fs)
    x_sem = [[net.slot() for _ in range(4)] for _ in range(3)]
    x2_sem = [[net.slot() for _ in range(2)] for _ in range(3)]
    z_sem = [[net.slot() for _ in zpeers] for _ in range(3)]
    a_sem = [[net.slot() for _ in range(4)] for _ in range(3)]

    def cols(i, which):
        w = grads[i].shape[-1] // 2
        return pl.ds(which * w, w)

    def plane_start(i):
        net.arrived(c_sem[i], core[i], sib)

        @pl.loop(0, zs * SEQ)
        def _(k):
            zi, qi = k // SEQ, k % SEQ
            total = grads[i][c, zi, qi].astype(F32) + core[i][zi, qi].astype(F32)
            grads[i][c, zi, qi] = total.astype(BF16)

        x, y = cols(i, 0), cols(i, 1)
        net.begin(x_sem[i][0], lambda: (grads[i].at[c, :, s3, :, x], xr[i].at[:, 1], (s1, f)))
        net.begin(x_sem[i][2], lambda: (grads[i].at[c, :, s3, :, y], yr[i].at[:, 1], (s2, f)))
        net.begin(x_sem[i][1], lambda: (grads[i].at[c, :, s1, :, x], xr[i].at[:, 0], (s1, f)))
        net.begin(x_sem[i][3], lambda: (grads[i].at[c, :, s2, :, y], yr[i].at[:, 0], (s2, f)))

    def add_into(i, part, qi, which, from_ref):
        w = grads[i].shape[-1] // 2

        @pl.loop(0, zs)
        def _(zi):
            a = grads[i][c, zi, qi, :, which * w : (which + 1) * w].astype(F32)
            b = (from_ref[zi] if part is None else from_ref[zi, part]).astype(F32)
            grads[i][c, zi, qi, :, which * w : (which + 1) * w] = (a + b).astype(BF16)

    def plane_second(i):
        net.arrived(x_sem[i][0], xr[i].at[:, 1], (s1, f))
        add_into(i, 1, s2, 0, xr[i])
        net.begin(x2_sem[i][0], lambda: (grads[i].at[c, :, s2, :, cols(i, 0)], x2r[i], (s2, f)))
        net.arrived(x_sem[i][2], yr[i].at[:, 1], (s2, f))
        add_into(i, 1, s1, 1, yr[i])
        net.begin(x2_sem[i][1], lambda: (grads[i].at[c, :, s1, :, cols(i, 1)], y2r[i], (s1, f)))
        net.arrived(x_sem[i][1], xr[i].at[:, 0], (s1, f))
        add_into(i, 0, s, 0, xr[i])
        net.arrived(x_sem[i][3], yr[i].at[:, 0], (s2, f))
        add_into(i, 0, s, 1, yr[i])

    def along_z(i):
        net.arrived(x2_sem[i][0], x2r[i], (s2, f))
        add_into(i, None, s, 0, x2r[i])
        net.arrived(x2_sem[i][1], y2r[i], (s1, f))
        add_into(i, None, s, 1, y2r[i])
        for j, (zt, _) in enumerate(zpeers):
            net.begin(z_sem[i][j], lambda zt=zt, j=j: (grads[i].at[c, zt, s], zr[i].at[j], (s, zt * 2 + c)))

    def own_rows(i):
        total = grads[i][c, z, s].astype(F32)
        for j, (_, zf) in enumerate(zpeers):
            net.arrived(z_sem[i][j], zr[i].at[j], (s, zf * 2 + c))
            total = total + zr[i][j].astype(F32)
        fin[i][s] = total.astype(BF16)
        net.begin(a_sem[i][0], lambda: (fin[i].at[s], fin[i].at[s], (s1, f)))
        net.begin(a_sem[i][1], lambda: (fin[i].at[s], fin[i].at[s], (s2, f)))

    def spread(i):
        net.arrived(a_sem[i][0], fin[i].at[s1], (s1, f))
        net.begin(a_sem[i][2], lambda: (fin[i].at[s1, :, cols(i, 0)], fin[i].at[s1, :, cols(i, 0)], (s2, f)))
        net.arrived(a_sem[i][1], fin[i].at[s2], (s2, f))
        net.begin(a_sem[i][3], lambda: (fin[i].at[s2, :, cols(i, 1)], fin[i].at[s2, :, cols(i, 1)], (s1, f)))

    final_out = (go_out, ge_out, gs_out)

    def spread_end(i):
        net.arrived(a_sem[i][2], fin[i].at[s3, :, cols(i, 0)], (s2, f))
        net.arrived(a_sem[i][3], fin[i].at[s3, :, cols(i, 1)], (s1, f))
        copy = pltpu.make_async_copy(fin[i], final_out[i], local.at[1 + i])
        copy.start()
        return copy

    def context_ready(wo, al):
        for t in range(SEQ):
            at = t * hw
            back = lax.dot_general(al[...], wo[at : at + hw, :], NT, preferred_element_type=F32).astype(BF16)
            for h in range(HL):
                dsend[t, h, :, 0:HEAD_DIM] = back[0:half, h * HEAD_DIM : (h + 1) * HEAD_DIM]
                dsend[t, h, :, HEAD_DIM:LANES] = back[half:rows, h * HEAD_DIM : (h + 1) * HEAD_DIM]
        for h in range(HL):
            for k, peer in enumerate((s3, s1, s2)):
                net.begin(d_sem[h][k], lambda peer=peer, h=h: (dsend.at[peer, h], drecv.at[s, h], (peer, f)))
        drecv[s] = dsend[s]

    def tokens_part(wo, we, ws, nl, nlt, n1, r1, act, slope, sl):
        loads = []
        for i, (src, dst) in enumerate(((wo_hbm, wo), (we_hbm, we), (ws_hbm, ws))):
            copy = pltpu.make_async_copy(src, dst, local.at[1 + i])
            copy.start()
            loads.append(copy)
        middle(
            (tokens, ctx, par, eb, cot, lout, gfirst, vecs, ebg),
            grads,
            shrink_ready,
            lambda: plane_start(2),
            lambda: context_ready(wo, sl),
            loads,
            local.at[4],
            wo,
            we,
            ws,
            nl,
            nlt,
            n1,
            r1,
            act,
            slope,
            sl,
        )

    ff = eb.shape[1]
    pl.run_scoped(
        tokens_part,
        pltpu.VMEM((width, width), BF16),
        pltpu.VMEM((width, ff), BF16),
        pltpu.VMEM((ff, width), BF16),
        pltpu.VMEM((rows, width), BF16),
        pltpu.VMEM((width, rows), BF16),
        pltpu.VMEM((rows, width), F32),
        pltpu.VMEM((rows, 1), F32),
        pltpu.VMEM((rows, ff), BF16),
        pltpu.VMEM((rows, ff), BF16),
        pltpu.VMEM((rows, width), BF16),
    )
    core_start(1)
    core_start(0)
    small_start()
    own_copy.wait()

    def attention_part(qa, ka, vv, own, k_t, tok_t, da, dq_t, acc_k, acc_v, gm, gsend, gmr, wfull, wtmp=None):
        loads = []
        pairs = ((qa_hbm, qa), (ka_hbm, ka), (v_hbm, vv), (own_hbm, own), (kt_hbm, k_t), (tt_hbm, tok_t))
        for i, (src, dst) in enumerate(pairs):
            copy = pltpu.make_async_copy(src, dst, local.at[1 + i])
            copy.start()
            loads.append(copy)
        gm[...] = jnp.zeros_like(gm)
        plane_start(1)
        plane_start(0)
        for copy in loads:
            copy.wait()

        net.arrived(v_core, svcore, sib)
        svec[c] = svec[c] + svcore[...]
        for j, (zt, _) in enumerate(zpeers):
            net.start(v_z[j], svec.at[c, zt], svz.at[j], (s, zt * 2 + c))

        g_sem = [[net.slot() for _ in range(3)] for _ in range(HL)]
        tc_sem = [net.slot() for _ in range(HL)]
        tz_sem = [[net.slot() for _ in zpeers] for _ in range(HL)]
        ts_sem = [[net.slot() for _ in range(3)] for _ in range(HL)]

        def prepare(h):
            for k, peer in enumerate((s3, s1, s2)):
                net.arrived(d_sem[h][k], drecv.at[peer, h], (peer, f))

            @pl.loop(0, SEQ)
            def _(t):
                grad = drecv[t, h].astype(F32)
                prod = grad * own[t, h].astype(F32)
                left = lane < HEAD_DIM
                for k in range(2):
                    inner = -jnp.sum(jnp.where(left if k == 0 else jnp.logical_not(left), prod, 0.0), axis=-1, keepdims=True)
                    hi = inner.astype(BF16).astype(F32)
                    here = grad if k == 0 else pltpu.roll(grad, HEAD_DIM, 1)
                    here = jnp.where(left, here, jnp.where(lane == HEAD_DIM, hi, jnp.where(lane == HEAD_DIM + 1, inner - hi, 0.0)))
                    at = pl.multiple_of(t * rows + k * half, half)
                    da[pl.ds(at, half), :] = here.astype(BF16)

            dq_t[...] = jnp.zeros_like(dq_t)

        def key_block(h, r):
            acc_k[...] = jnp.zeros_like(acc_k)
            acc_v[...] = jnp.zeros_like(acc_v)
            keys = pl.multiple_of(r * rows, rows)
            nt = (((1,), (1,)), ((), ()))

            @pl.loop(0, length // QB)
            def _(i):
                at = pl.multiple_of(i * QB, QB)
                q = qa[h, pl.ds(at, QB), :]
                grad = da[pl.ds(at, QB), :]
                probs = jnp.exp(lax.dot_general(ka[h, pl.ds(keys, rows), :], q, nt, preferred_element_type=F32))
                inner = lax.dot_general(vv[h, pl.ds(keys, rows), :], grad, nt, preferred_element_type=F32)
                ds = (probs * inner).astype(BF16)
                acc_v[...] += jnp.dot(probs.astype(BF16), grad, preferred_element_type=F32)
                acc_k[...] += jnp.dot(ds, q, preferred_element_type=F32)
                dq_t[:, pl.ds(at, QB)] += jnp.dot(k_t[h, :, pl.ds(keys, rows)], ds, preferred_element_type=F32)

            gm[pl.ds(keys, rows), HEAD_DIM:LANES] = acc_k[:, 0:HEAD_DIM].astype(BF16)
            gm[pl.ds(keys, rows), LANES : LANES + HEAD_DIM] = acc_v[:, 0:HEAD_DIM].astype(BF16)

        rt = tsend.shape[3]
        vrow = n + n // 2
        brow = rt - 16

        def head_done(h):
            @pl.loop(0, SEQ)
            def _(t):
                at = pl.multiple_of(t * rows, rows)
                dq = (dq_t[:, pl.ds(at, rows)].T * (HEAD_DIM**-0.5)).astype(BF16)
                gm[pl.ds(at, rows), 0:HEAD_DIM] = dq
                for k in range(3):
                    for p in range(2):
                        piece = gm[pl.ds(at + p * half, half), k * HEAD_DIM : (k + 1) * HEAD_DIM]
                        gsend[h, t, k, :, p * HEAD_DIM : (p + 1) * HEAD_DIM] = piece

            for k, peer in enumerate((s3, s1, s2)):
                net.start(g_sem[h][k], gsend.at[h, peer], grecv.at[h, s], (peer, f))
            grecv[h, s] = gsend[h, s]
            sums = jnp.sum(gm[...].astype(F32), axis=0, keepdims=True).astype(BF16)
            whole = jnp.dot(tok_t[...], gm[...], preferred_element_type=F32)
            for zi in range(zs):
                for ci in range(2):
                    fi = zi * 2 + ci
                    grad = whole[fi * n : (fi + 1) * n].astype(BF16)
                    tsend[h, ci, zi, 0:n, :] = grad[:, 0:LANES]
                    tsend[h, ci, zi, n:vrow, 0:HEAD_DIM] = grad[0 : n // 2, LANES : LANES + HEAD_DIM]
                    tsend[h, ci, zi, n:vrow, HEAD_DIM:LANES] = grad[n // 2 : n, LANES : LANES + HEAD_DIM]
                    tsend[h, ci, zi, brow:rt, :] = jnp.broadcast_to(sums[:, 0:LANES], (16, LANES))
                    tsend[h, ci, zi, brow + 8 : rt, :] = jnp.broadcast_to(sums[:, LANES : 2 * LANES], (8, LANES))
            net.start(tc_sem[h], tsend.at[h, 1 - c], tcore.at[h], sib)

        def triple_z(h):
            net.arrived(tc_sem[h], tcore.at[h], sib)
            tsend[h, c] = (tsend[h, c].astype(F32) + tcore[h].astype(F32)).astype(BF16)
            for j, (zt, _) in enumerate(zpeers):
                net.begin(tz_sem[h][j], lambda zt=zt, j=j: (tsend.at[h, c, zt], tz.at[h, j], (s, zt * 2 + c)))

        def triple_own(h):
            total = tsend[h, c, z].astype(F32)
            for j, (_, zf) in enumerate(zpeers):
                net.arrived(tz_sem[h][j], tz.at[h, j], (s, zf * 2 + c))
                total = total + tz[h, j].astype(F32)
            tfin[h, s] = total.astype(BF16)
            for k, peer in enumerate((s3, s1, s2)):
                net.begin(ts_sem[h][k], lambda peer=peer: (tfin.at[h, s], tfin.at[h, s], (peer, f)))

        def rows_in(h):
            for k, peer in enumerate((s3, s1, s2)):
                net.arrived(g_sem[h][k], grecv.at[h, peer], (peer, f))
            for t in range(SEQ):
                for k in range(3):
                    at = k * width + t * hw + h * HEAD_DIM
                    gmr[0:half, at : at + HEAD_DIM] = grecv[h, t, k, :, 0:HEAD_DIM]
                    gmr[half:rows, at : at + HEAD_DIM] = grecv[h, t, k, :, HEAD_DIM:LANES]

        def attend_back(h, *steps):
            @pl.loop(0, SEQ)
            def _(r):
                key_block(h, r)
                for k, step in enumerate(steps):

                    @pl.when(r == k)
                    def _(step=step):
                        for call, arg in step:
                            call(arg)

        plane_second(2)
        prepare(0)
        attend_back(0)
        head_done(0)
        for j, (_, zf) in enumerate(zpeers):
            net.arrived(w_z[j], wland.at[zf, c], (s, zf * 2 + c))
            net.start(w_sib[j + 1], wland.at[zf, c], wland.at[zf, c], sib)
        prepare(1)
        attend_back(
            1,
            [(plane_second, 1), (triple_z, 0)],
            [(along_z, 2), (plane_second, 0)],
        )
        head_done(1)
        total = svec[c, z]
        for j, (_, zf) in enumerate(zpeers):
            net.arrived(v_z[j], svz.at[j], (s, zf * 2 + c))
            total = total + svz[j]
        svseq[s] = total
        for k, peer in enumerate((s3, s1, s2)):
            net.start(v_seq[k], svseq.at[s], svseq.at[s], (peer, f))
        prepare(2)
        attend_back(
            2,
            [(triple_own, 0)],
            [(own_rows, 2), (along_z, 1)],
            [(along_z, 0), (triple_z, 1)],
        )
        head_done(2)
        spread(2)
        rows_in(0)
        net.arrived(w_sib[0], wland.at[z, 1 - c], sib)
        for j, (_, zf) in enumerate(zpeers):
            net.arrived(w_sib[j + 1], wland.at[zf, 1 - c], sib)
        depth = zs if zs <= 4 else 1
        for base in range(0, zs, depth):
            if zs > 4:
                copy = pltpu.make_async_copy(wland.at[pl.ds(base, depth)], wtmp, local.at[0])
                copy.start()
                copy.wait()
            for zi in range(depth):
                for ci in range(2):
                    fi = (base + zi) * 2 + ci
                    wfull[fi * n : (fi + 1) * n, :] = (wtmp if zs > 4 else wland)[zi, ci]
        triple_own(1)
        triple_z(2)
        own_rows(1)
        own_rows(0)
        rows_in(1)
        triple_own(2)
        spread(1)
        spread(0)
        rows_in(2)
        wide = 256

        @pl.loop(0, width // wide)
        def _(j):
            at = pl.ds(pl.multiple_of(j * wide, wide), wide)
            back = lax.dot_general(gmr[...], wfull[at, :], NT, preferred_element_type=F32)
            tg_out[:, at] = (gfirst[:, at] + back).astype(BF16)

        copies = [spread_end(2), spread_end(1)]
        for k, peer in enumerate((s3, s1, s2)):
            net.arrived(v_seq[k], svseq.at[peer], (peer, f))
        small_out[...] = svseq[0] + svseq[1] + svseq[2] + svseq[3]
        for h in range(HL):
            for k, peer in enumerate((s3, s1, s2)):
                net.arrived(ts_sem[h][k], tfin.at[h, peer], (peer, f))
        q_row, v_row = [], []
        for t in range(SEQ):
            for h in range(HL):
                at = t * hw + h * HEAD_DIM
                block = tfin[h, t].astype(F32)
                trip_out[:, at : at + HEAD_DIM] = block[0:n, 0:HEAD_DIM]
                trip_out[:, width + at : width + at + HEAD_DIM] = block[0:n, HEAD_DIM:LANES]
                trip_out[0 : n // 2, 2 * width + at : 2 * width + at + HEAD_DIM] = block[n:vrow, 0:HEAD_DIM]
                trip_out[n // 2 : n, 2 * width + at : 2 * width + at + HEAD_DIM] = block[n:vrow, HEAD_DIM:LANES]
                q_row.append(block[brow : brow + 1, 0:HEAD_DIM])
                v_row.append(block[brow + 8 : brow + 9, 0:HEAD_DIM])
        q_row, v_row = jnp.concatenate(q_row, axis=1), jnp.concatenate(v_row, axis=1)
        bias_out[...] = jnp.zeros_like(bias_out)
        for fi in range(2 * zs):

            @pl.when(f == fi)
            def _(fi=fi):
                bias_out[0:1, 0:n] = q_row[:, fi * n : (fi + 1) * n]
                bias_out[1:2, 0:n] = v_row[:, fi * n : (fi + 1) * n]

        copies.append(spread_end(0))
        for copy in copies:
            copy.wait()
        net.drain()

    pl.run_scoped(
        attention_part,
        pltpu.VMEM((HL, length, LANES), BF16),
        pltpu.VMEM((HL, length, LANES), BF16),
        pltpu.VMEM((HL, length, LANES), BF16),
        pltpu.VMEM((SEQ, HL, half, LANES), BF16),
        pltpu.VMEM((HL, HEAD_DIM, length), BF16),
        pltpu.VMEM((width, length), BF16),
        pltpu.VMEM((length, LANES), BF16),
        pltpu.VMEM((HEAD_DIM, length), F32),
        pltpu.VMEM((rows, LANES), F32),
        pltpu.VMEM((rows, LANES), F32),
        pltpu.VMEM((length, 2 * LANES), BF16),
        pltpu.VMEM((HL, SEQ, 3, half, LANES), BF16),
        pltpu.VMEM((rows, 3 * width), BF16),
        pltpu.VMEM((width, 3 * width), BF16),
        *([pltpu.VMEM((1, 2, n, 3 * width), BF16)] if zs > 4 else []),
    )


QB = 512
VMEM_BYTES = 127 << 19


def collect_call(qa, ka, vv, own, kt, tt, triple, tokens, ctx, par, eb, cot, wo, we, ws):
    rows, width = tokens.shape
    length = rows * SEQ
    n = triple.shape[0]
    zs = width // n // 2
    p = zs - 1
    ff = eb.shape[1]
    q = n // SEQ
    rt = (n + n // 2 + 7) // 8 * 8 + 16
    half = rows // 2
    slots = 3 * HL + 3 + 1 + p + 3 + p + zs + 3 * (4 + 2 + p + 4) + HL * (3 + 1 + p + 3)
    vm = pl.BlockSpec(memory_space=pltpu.VMEM)
    hbm = pl.BlockSpec(memory_space=pl.ANY)
    if q % 8 == 0:
        shapes = ((q, width), (q, ff), (n, width))
    else:
        shapes = ((n, 256), (n, ff // SEQ), (n, width))

    def per_weight(make):
        return [pltpu.VMEM(make(a, b), BF16) for a, b in shapes]

    outs = pl.pallas_call(
        functools.partial(collect_kernel, zs),
        out_shape=(
            jax.ShapeDtypeStruct((rows, width), BF16),
            jax.ShapeDtypeStruct((rows, width), BF16),
            jax.ShapeDtypeStruct((n, 3 * width), F32),
            jax.ShapeDtypeStruct((8, LANES), F32),
            jax.ShapeDtypeStruct((16, LANES), F32),
        )
        + tuple(jax.ShapeDtypeStruct((SEQ, a, b), BF16) for a, b in shapes)
        + ((jax.ShapeDtypeStruct((zs, 2, n, 3 * width), BF16),) if zs > 4 else ()),
        in_specs=[hbm] * 6 + [vm] * 6 + [hbm] * 3,
        out_specs=(hbm, vm, vm, vm, vm, hbm, hbm, hbm) + ((hbm,) if zs > 4 else ()),
        scratch_shapes=([] if zs > 4 else [pltpu.VMEM((zs, 2, n, 3 * width), BF16)])
        + [
            pltpu.VMEM((SEQ, HL, half, LANES), BF16),
            pltpu.VMEM((SEQ, HL, half, LANES), BF16),
            pltpu.VMEM((HL, SEQ, 3, half, LANES), BF16),
            pltpu.VMEM((rows, width), F32),
            pltpu.VMEM((8, width), F32),
            pltpu.VMEM((1, ff), F32),
            pltpu.VMEM((HL, 2, zs, rt, LANES), BF16),
            pltpu.VMEM((HL, zs, rt, LANES), BF16),
            pltpu.VMEM((HL, p, rt, LANES), BF16),
            pltpu.VMEM((HL, SEQ, rt, LANES), BF16),
            pltpu.VMEM((2, zs, 16, LANES), F32),
            pltpu.VMEM((zs, 16, LANES), F32),
            pltpu.VMEM((p, 16, LANES), F32),
            pltpu.VMEM((SEQ, 16, LANES), F32),
        ]
        + per_weight(lambda a, b: (2, zs, SEQ, a, b))
        + per_weight(lambda a, b: (zs, SEQ, a, b))
        + per_weight(lambda a, b: (zs, 2, a, b // 2))
        + per_weight(lambda a, b: (zs, 2, a, b // 2))
        + per_weight(lambda a, b: (zs, a, b // 2))
        + per_weight(lambda a, b: (zs, a, b // 2))
        + per_weight(lambda a, b: (p, a, b))
        + per_weight(lambda a, b: (SEQ, a, b))
        + [
            pltpu.SemaphoreType.DMA((slots,)),
            pltpu.SemaphoreType.DMA((slots,)),
            pltpu.SemaphoreType.DMA((8,)),
        ],
        compiler_params=pltpu.CompilerParams(
            collective_id=1, has_side_effects=True, vmem_limit_bytes=VMEM_BYTES
        ),
        name="collect",
    )(qa, ka, vv, own, kt, tt, triple, tokens, ctx, par, eb, cot, wo, we, ws)
    lout, tg, trip, bias, small, go, ge, gs = outs[:8]
    if q % 8 == 0:
        go, ge = go.reshape(n, width), ge.reshape(n, ff)
    else:
        go = go[:, :, : width // SEQ].transpose(1, 0, 2).reshape(n, width)
        ge = ge.transpose(1, 0, 2).reshape(n, ff)
    return lout, tg, trip, bias, small, go, ge, gs.reshape(4 * n, width)


def body(
    tokens,
    segment,
    padding,
    triple_weight,
    query_bias,
    value_bias,
    output_weight,
    output_bias,
    first_gain,
    first_shift,
    expand_weight,
    expand_bias,
    shrink_weight,
    shrink_bias,
    second_gain,
    second_shift,
    cotangent,
):
    n = output_weight.shape[0]
    small = (
        query_bias,
        value_bias,
        output_bias,
        first_gain,
        first_shift,
        shrink_bias,
        second_gain,
        second_shift,
        expand_bias,
    )
    qa, ka, vv, own, kt, tt, context, par, eb, wo, we, ws = gather_call(
        tokens[0], segment, padding, triple_weight, small, output_weight, expand_weight, shrink_weight
    )
    layer_out, tokens_grad, triple_grad, bias_grad, small_grad, go, ge, gs = collect_call(
        qa, ka, vv, own, kt, tt, triple_weight, tokens[0], context, par, eb, cotangent[0], wo, we, ws
    )
    outs = finish_call(layer_out, tokens_grad, triple_grad, go, ge, gs, bias_grad, small_grad, n)
    return (outs[0][None], outs[1][None]) + tuple(outs[2:])


def solution(mesh):
    return jax.shard_map(
        body,
        mesh=mesh,
        in_specs=(
            P("fsdp", "seq", None),
            P("fsdp", None),
            P("fsdp", None),
            P("fsdp", None),
            P("fsdp"),
            P("fsdp"),
            P("fsdp", None),
            P("fsdp"),
            P("fsdp"),
            P("fsdp"),
            P("fsdp", None),
            P("fsdp"),
            P("fsdp", None),
            P("fsdp"),
            P("fsdp"),
            P("fsdp"),
            P("fsdp", "seq", None),
        ),
        out_specs=(
            P("fsdp", "seq", None),
            P("fsdp", "seq", None),
            P("fsdp", None),
            P("fsdp"),
            P("fsdp"),
            P("fsdp", None),
            P("fsdp"),
            P("fsdp"),
            P("fsdp"),
            P("fsdp", None),
            P("fsdp"),
            P("fsdp", None),
            P("fsdp"),
            P("fsdp"),
            P("fsdp"),
        ),
        check_vma=False,
    )
```

```python
import functools

import jax
import jax.numpy as jnp
from jax import lax
from jax.experimental import pallas as pl
from jax.experimental.pallas import tpu as pltpu
from jax.sharding import PartitionSpec as P

HEADS = 12
HEAD_DIM = 64
EPS = 1e-06
MASKED = -1e30
MESH = pl.DeviceIdType.MESH
F32 = jnp.float32
BF16 = jnp.bfloat16
SEQ = 4
HL = HEADS // SEQ
LANES = 128
NEAR = 512


def ring(s):
    return (s + 1 - 2 * (s % 2), (s + 2) % 4, 3 - s)


class Net:
    def __init__(self, send, recv):
        self.send, self.recv, self.next = send, recv, 0
        self.pending = {}

    def slot(self):
        self.next += 1
        return self.next - 1

    def copy(self, i, src, dst, device):
        return pltpu.make_async_remote_copy(
            src_ref=src,
            dst_ref=dst,
            send_sem=self.send.at[i],
            recv_sem=self.recv.at[i],
            device_id=device,
            device_id_type=MESH,
        )

    def start(self, i, src, dst, device):
        copy = self.copy(i, src, dst, device)
        copy.start()
        self.pending[i] = copy.wait_send

    def begin(self, i, make):
        self.copy(i, *make()).start()
        self.pending[i] = lambda: self.copy(i, *make()).wait_send()

    def arrived(self, i, dst, device):
        self.copy(i, dst, dst, device).wait_recv()

    def drain(self):
        for wait in self.pending.values():
            wait()
        self.pending = {}


def gather_kernel(
    zs,
    tok,
    seg,
    pad,
    trip,
    v0,
    v1,
    v2,
    v3,
    v4,
    v5,
    v6,
    v7,
    v8,
    wo,
    we,
    ws,
    qa_out,
    ka_out,
    v_out,
    own_out,
    kt_out,
    tt_out,
    ctx_out,
    par_out,
    eb_out,
    wo_out,
    we_out,
    ws_out,
    wo_all,
    we_all,
    ws_all,
    tokbuf,
    small,
    wsend,
    wbuf,
    wpad,
    smallbuf,
    qa,
    ka,
    vv,
    kt,
    tt,
    qmask,
    kmask,
    ctxsend,
    ctxrecv,
    send,
    recv,
    local,
):
    s = lax.axis_index("seq")
    f = lax.axis_index("fsdp")
    z, c = f // 2, f % 2
    rows, width = tok.shape
    length = rows * SEQ
    part = wsend.shape[1]
    n = trip.shape[0]
    hw = HL * HEAD_DIM
    s1, s2, s3 = ring(s)
    zpeers = [((z + j) % zs, (z - j + zs) % zs) for j in range(1, zs)]
    sib = (s, z * 2 + 1 - c)

    barrier = pltpu.get_barrier_semaphore()
    partners = [(s1, f), (s2, f), (s3, f), sib] + [(s, zt * 2 + c) for zt, _ in zpeers]
    for partner in partners:
        pl.semaphore_signal(barrier, inc=1, device_id=partner, device_id_type=MESH)
    small[...] = jnp.zeros_like(small)
    for r, ref in enumerate((v0, v1, v2, v3, v4, v5, v6, v7)):
        small[r : r + 1, 0:n] = ref[...].astype(F32).reshape(1, n)
    for r in range(4):
        small[8 + r : 9 + r, 0:n] = v8[pl.ds(r * n, n)].astype(F32).reshape(1, n)

    for t in range(SEQ):

        @pl.when(s == t)
        def _(t=t):
            for j in range(3):
                wsend[:, j * hw : (j + 1) * hw] = trip[:, j * width + t * hw : j * width + (t + 1) * hw]

    pl.semaphore_wait(barrier, len(partners))

    net = Net(send, recv)
    half = rows // 2
    lo, hi = pl.ds(0, half), pl.ds(half, half)

    t_1lo, t_1hi, t_2lo, t_2hi, t_3lo, t_3hi = [net.slot() for _ in range(6)]
    net.start(t_1lo, tok.at[lo], tokbuf.at[s, lo], (s1, f))
    net.start(t_2hi, tok.at[hi], tokbuf.at[s, hi], (s2, f))
    w_z = [net.slot() for _ in zpeers]
    p_z = [net.slot() for _ in zpeers]
    w_sib = [net.slot() for _ in range(zs)]
    p_sib = [net.slot() for _ in range(zs)]

    for j, (zt, _) in enumerate(zpeers):
        net.start(w_z[j], wsend, wbuf.at[z, c], (s, zt * 2 + c))
        net.start(p_z[j], small, smallbuf.at[z, c], (s, zt * 2 + c))
    net.start(w_sib[0], wsend, wbuf.at[z, c], sib)
    net.start(p_sib[0], small, smallbuf.at[z, c], sib)
    net.start(t_1hi, tok.at[hi], tokbuf.at[s, hi], (s1, f))
    net.start(t_2lo, tok.at[lo], tokbuf.at[s, lo], (s2, f))
    weights = ((wo, wo_all), (we, we_all), (ws, ws_all))
    f_z = [[net.slot() for _ in weights] for _ in zpeers]

    near = pl.ds(0, NEAR)
    far = pl.ds(NEAR, width - NEAR)
    f_far = [net.slot() for _ in zpeers]

    def quarter(i, zi, src):
        ref = weights[i][1].at[zi, c, src]
        return ref.at[:, near] if i == 2 else ref

    def along(i):
        mine = weights[i][0].at[s]
        mine = mine.at[:, near] if i == 2 else mine
        for j, (zt, _) in enumerate(zpeers):
            net.start(f_z[j][i], mine, quarter(i, z, s), (s, zt * 2 + c))

    def along_whole():
        for j, (zt, _) in enumerate(zpeers):
            net.start(f_z[j][0], wo, wo_all.at[z, c], (s, zt * 2 + c))
        for j, (zt, _) in enumerate(zpeers):
            net.start(f_far[j], ws.at[:, :, far], ws_all.at[z, c, :, :, far], (s, zt * 2 + c))

    f_sib = [[net.slot() for _ in weights] for _ in range(zs)]
    for i, (mine, full) in enumerate(weights):
        net.start(f_sib[0][i], mine, full.at[z, c], sib)
    for mine, full in weights:
        full[z, c] = mine[...]
    wbuf[z, c] = wsend[...]
    smallbuf[z, c] = small[...]
    tokbuf[s] = tok[...]

    row_id = lax.broadcasted_iota(jnp.int32, (LANES, length), 0) - HEAD_DIM
    seg_row = jnp.broadcast_to(seg[...], (LANES, length))
    pad_row = jnp.broadcast_to(pad[...], (LANES, length))
    here = (row_id == seg_row) & (row_id >= 0)
    live_row = row_id == 32
    q_t = jnp.where(live_row, pad_row.astype(F32), jnp.where(here, 1.0, 0.0))
    qmask[...] = q_t.T
    inside = (row_id >= 0) & (row_id < 16)
    k_t = jnp.where(inside & jnp.logical_not(here & (pad_row == 1)), MASKED, 0.0)
    k_t = jnp.where((row_id >= 16) & (row_id < 19), 1.0, k_t)
    kmask[...] = k_t.T.astype(BF16)

    net.arrived(t_1lo, tokbuf.at[s1, lo], (s1, f))
    net.start(t_3lo, tokbuf.at[s1, lo], tokbuf.at[s1, lo], (s2, f))
    net.arrived(t_2hi, tokbuf.at[s2, hi], (s2, f))
    net.start(t_3hi, tokbuf.at[s2, hi], tokbuf.at[s2, hi], (s1, f))

    for j, (_, zf) in enumerate(zpeers):
        net.arrived(w_z[j], wbuf.at[zf, c], (s, zf * 2 + c))
        net.start(w_sib[j + 1], wbuf.at[zf, c], wbuf.at[zf, c], sib)
        net.arrived(p_z[j], smallbuf.at[zf, c], (s, zf * 2 + c))
        net.start(p_sib[j + 1], smallbuf.at[zf, c], smallbuf.at[zf, c], sib)
    along(1)

    net.arrived(w_sib[0], wbuf.at[z, 1 - c], sib)
    net.arrived(p_sib[0], smallbuf.at[z, 1 - c], sib)
    for j, (_, zf) in enumerate(zpeers):
        net.arrived(w_sib[j + 1], wbuf.at[zf, 1 - c], sib)
        net.arrived(p_sib[j + 1], smallbuf.at[zf, 1 - c], sib)

    for zi in range(zs):
        for ci in range(2):
            fi = zi * 2 + ci
            block = smallbuf[zi, ci]
            par_out[:, fi * n : (fi + 1) * n] = block[:, :n]
            for r in range(4):
                at = fi * 4 * n + r * n
                eb_out[:, at : at + n] = block[8 + r : 9 + r, :n]

    wpad[...] = jnp.zeros_like(wpad)
    for zi in range(zs):
        for ci in range(2):
            fi = zi * 2 + ci
            for k in range(3 * HL):
                wpad[fi * n : (fi + 1) * n, k * LANES : k * LANES + HEAD_DIM] = wbuf[
                    zi, ci, :, k * HEAD_DIM : (k + 1) * HEAD_DIM
                ]
    bias = jnp.zeros((2, HL * LANES), F32)
    zero = jnp.zeros((2, HEAD_DIM), F32)
    for t in range(SEQ):
        pieces = []
        for h in range(HL):
            pieces += [par_out[0:2, t * hw + h * HEAD_DIM : t * hw + (h + 1) * HEAD_DIM], zero]
        bias = jnp.where(s == t, jnp.concatenate(pieces, axis=1), bias)
    lane = lax.broadcasted_iota(jnp.int32, (1, LANES), 1)
    ones_lane = jnp.where((lane == HEAD_DIM) | (lane == HEAD_DIM + 1), 1.0, 0.0)

    def project(block):
        x = tokbuf[block]
        at = pl.ds(pl.multiple_of(block * rows, rows), rows)
        tt[:, at] = x.T
        group = HL * LANES

        def part(k):
            return jnp.dot(x, wpad[:, k * group : (k + 1) * group], preferred_element_type=F32)

        qm = jnp.where(lane < HEAD_DIM + 16, qmask[at, :], 0.0).astype(BF16)
        q = ((part(0) + bias[0:1, :]).astype(BF16) * BF16(HEAD_DIM**-0.5))
        k = part(1).astype(BF16)
        v = part(2) + bias[1:2, :]
        for h in range(HL):
            cut = slice(h * LANES, (h + 1) * LANES)
            qa[h, at, :] = q[:, cut] + qm
            ka[h, at, :] = k[:, cut] + kmask[at, :]
            vv[h, at, :] = (v[:, cut] + ones_lane).astype(BF16)

    project(s)
    net.arrived(t_1hi, tokbuf.at[s1, hi], (s1, f))
    project(s1)
    net.arrived(t_2lo, tokbuf.at[s2, lo], (s2, f))
    project(s2)
    along(2)
    net.arrived(t_3lo, tokbuf.at[s3, lo], (s2, f))
    net.arrived(t_3hi, tokbuf.at[s3, hi], (s1, f))
    project(s3)

    f_1 = [[net.slot() for _ in weights] for _ in zpeers]
    f_2 = [[net.slot() for _ in weights] for _ in zpeers]
    f_3lo = [[net.slot() for _ in weights] for _ in zpeers]
    f_3hi = [[net.slot() for _ in weights] for _ in zpeers]

    def halves(i, zf, src, which):
        w = (NEAR if i == 2 else weights[i][1].shape[-1]) // 2
        return weights[i][1].at[zf, c, src, :, pl.ds(which * w, w)]

    def spread(i):
        for j, (_, zf) in enumerate(zpeers):
            net.arrived(f_z[j][i], quarter(i, zf, s), (s, zf * 2 + c))
            net.start(f_1[j][i], quarter(i, zf, s), quarter(i, zf, s), (s1, f))
            net.start(f_2[j][i], quarter(i, zf, s), quarter(i, zf, s), (s2, f))

    def pass_on(i):
        for j, (_, zf) in enumerate(zpeers):
            net.arrived(f_1[j][i], quarter(i, zf, s1), (s1, f))
            net.start(f_3lo[j][i], halves(i, zf, s1, 0), halves(i, zf, s1, 0), (s2, f))
            net.arrived(f_2[j][i], quarter(i, zf, s2), (s2, f))
            net.start(f_3hi[j][i], halves(i, zf, s2, 1), halves(i, zf, s2, 1), (s1, f))

    def finish(i):
        for j, (_, zf) in enumerate(zpeers):
            if i == 0:
                net.arrived(f_z[j][0], wo_all.at[zf, c], (s, zf * 2 + c))
            else:
                net.arrived(f_3lo[j][i], halves(i, zf, s3, 0), (s2, f))
                net.arrived(f_3hi[j][i], halves(i, zf, s3, 1), (s1, f))
            if i == 2:
                net.arrived(f_far[j], ws_all.at[zf, c, :, :, far], (s, zf * 2 + c))
            full = weights[i][1]
            net.start(f_sib[j + 1][i], full.at[zf, c], full.at[zf, c], sib)

    c_1, c_2, c_3 = [net.slot() for _ in range(3)]
    qt = min(256, rows)

    def attend(block, first=0, last=HL):
        @pl.loop(first, last)
        def _(h):
            @pl.loop(0, rows // qt)
            def _(i):
                at = pl.multiple_of(block * rows + i * qt, qt)
                scores = lax.dot_general(
                    qa[h, pl.ds(at, qt), :],
                    ka[h],
                    (((1,), (1,)), ((), ())),
                    preferred_element_type=F32,
                )
                top = jnp.max(scores, axis=-1, keepdims=True)
                probs = jnp.exp(scores - top).astype(BF16)
                out = jnp.dot(probs, vv[h], preferred_element_type=F32)
                total = out[:, HEAD_DIM : HEAD_DIM + 1]
                live = qmask[pl.ds(at, qt), HEAD_DIM + 32 : HEAD_DIM + 33]
                ctx = (out * (live / total)).astype(BF16)[:, :HEAD_DIM]
                lse = jnp.where(live > 0.0, top + jnp.log(total), -MASKED)
                lse = -lse
                hi = lse.astype(BF16).astype(F32)
                mid = (lse - hi).astype(BF16).astype(F32)
                rest = lse - hi - mid
                base = HEAD_DIM + 16
                extra = jnp.where(lane == base, hi, jnp.where(lane == base + 1, mid, jnp.where(lane == base + 2, rest, 0.0)))
                qa[h, pl.ds(at, qt), :] = qa[h, pl.ds(at, qt), :] + extra.astype(BF16)
                per = half // qt
                down = pl.multiple_of((i % per) * qt, qt)

                @pl.when(i < per)
                def _():
                    ctxsend[block, h, pl.ds(down, qt), 0:HEAD_DIM] = ctx

                @pl.when(i >= per)
                def _():
                    ctxsend[block, h, pl.ds(down, qt), HEAD_DIM:LANES] = ctx

    spread(1)
    attend(s3)
    net.start(c_3, ctxsend.at[s3], ctxrecv.at[s], (s3, f))
    along_whole()
    spread(2)
    attend(s1)
    net.start(c_1, ctxsend.at[s1], ctxrecv.at[s], (s1, f))
    pass_on(1)
    attend(s2)
    net.start(c_2, ctxsend.at[s2], ctxrecv.at[s], (s2, f))
    pass_on(2)
    attend(s)
    ctxrecv[s] = ctxsend[s]
    outs = []

    def save(i, src, dst):
        copy = pltpu.make_async_copy(src, dst, local.at[3 + i])
        copy.start()
        outs.append(copy)

    for i, (src, dst) in enumerate(((qa, qa_out), (ka, ka_out), (vv, v_out), (ctxsend, own_out))):
        save(i, src, dst)

    @pl.loop(0, HL)
    def _(h):
        kt[h] = ka[h].T[0:HEAD_DIM]

    save(4, kt, kt_out)
    save(5, tt, tt_out)
    net.arrived(c_3, ctxrecv.at[s3], (s3, f))
    net.arrived(c_1, ctxrecv.at[s1], (s1, f))
    net.arrived(c_2, ctxrecv.at[s2], (s2, f))
    for t in range(SEQ):
        for h in range(HL):
            at = t * hw + h * HEAD_DIM
            ctx_out[0:half, at : at + HEAD_DIM] = ctxrecv[t, h, :, 0:HEAD_DIM]
            ctx_out[half:rows, at : at + HEAD_DIM] = ctxrecv[t, h, :, HEAD_DIM:LANES]
    for i in range(3):
        finish(i)
    for i, (dst, (_, full)) in enumerate(zip((wo_out, we_out, ws_out), weights)):
        save(6 + 2 * i, full.at[:, c], dst.at[:, c])
    for i, (dst, (_, full)) in enumerate(zip((wo_out, we_out, ws_out), weights)):
        net.arrived(f_sib[0][i], full.at[z, 1 - c], sib)
        for j, (_, zf) in enumerate(zpeers):
            net.arrived(f_sib[j + 1][i], full.at[zf, 1 - c], sib)
        save(7 + 2 * i, full.at[:, 1 - c], dst.at[:, 1 - c])
    for copy in outs:
        copy.wait()
    net.drain()


def gather_slots(zs):
    p = zs - 1
    return 6 + 2 * p + 2 * zs + 3 * p + 3 * zs + 13 * p + 3


def gather_call(tokens, segment, padding, triple, small, wo, we, ws):
    rows, width = tokens.shape
    length = rows * SEQ
    n = triple.shape[0]
    shards = width // n
    zs = shards // 2
    hw = HL * HEAD_DIM
    ff = we.shape[1]
    slots = gather_slots(zs)
    vm = pl.BlockSpec(memory_space=pltpu.VMEM)
    hbm = pl.BlockSpec(memory_space=pl.ANY)
    q, qs = n // SEQ, ws.shape[0] // SEQ
    out_shape = (
        jax.ShapeDtypeStruct((HL, length, LANES), BF16),
        jax.ShapeDtypeStruct((HL, length, LANES), BF16),
        jax.ShapeDtypeStruct((HL, length, LANES), BF16),
        jax.ShapeDtypeStruct((SEQ, HL, rows // 2, LANES), BF16),
        jax.ShapeDtypeStruct((HL, HEAD_DIM, length), BF16),
        jax.ShapeDtypeStruct((width, length), BF16),
        jax.ShapeDtypeStruct((rows, width), BF16),
        jax.ShapeDtypeStruct((16, width), F32),
        jax.ShapeDtypeStruct((1, ff), F32),
        jax.ShapeDtypeStruct((zs, 2, SEQ, q, width), BF16),
        jax.ShapeDtypeStruct((zs, 2, SEQ, q, ff), BF16),
        jax.ShapeDtypeStruct((zs, 2, SEQ, qs, width), BF16),
    )
    outs = pl.pallas_call(
        functools.partial(gather_kernel, zs),
        out_shape=out_shape,
        in_specs=[vm] * 16,
        out_specs=(hbm, hbm, hbm, hbm, hbm, hbm, vm, vm, vm, hbm, hbm, hbm),
        scratch_shapes=[
            pltpu.VMEM((zs, 2, SEQ, q, width), BF16),
            pltpu.VMEM((zs, 2, SEQ, q, ff), BF16),
            pltpu.VMEM((zs, 2, SEQ, qs, width), BF16),
            pltpu.VMEM((SEQ, rows, width), BF16),
            pltpu.VMEM((16, LANES), F32),
            pltpu.VMEM((n, 3 * hw), BF16),
            pltpu.VMEM((zs, 2, n, 3 * hw), BF16),
            pltpu.VMEM((width, 3 * HL * LANES), BF16),
            pltpu.VMEM((zs, 2, 16, LANES), F32),
            pltpu.VMEM((HL, length, LANES), BF16),
            pltpu.VMEM((HL, length, LANES), BF16),
            pltpu.VMEM((HL, length, LANES), BF16),
            pltpu.VMEM((HL, HEAD_DIM, length), BF16),
            pltpu.VMEM((width, length), BF16),
            pltpu.VMEM((length, LANES), F32),
            pltpu.VMEM((length, LANES), BF16),
            pltpu.VMEM((SEQ, HL, rows // 2, LANES), BF16),
            pltpu.VMEM((SEQ, HL, rows // 2, LANES), BF16),
            pltpu.SemaphoreType.DMA((slots,)),
            pltpu.SemaphoreType.DMA((slots,)),
            pltpu.SemaphoreType.DMA((16,)),
        ],
        compiler_params=pltpu.CompilerParams(
            collective_id=0, has_side_effects=True, vmem_limit_bytes=60 << 20
        ),
        name="gather_attend",
    )(
        tokens,
        segment,
        padding,
        triple,
        *small,
        wo.reshape(SEQ, q, width),
        we.reshape(SEQ, q, ff),
        ws.reshape(SEQ, qs, width),
    )
    qa, ka, vv, own, kt, tt, ctx, par, eb, wof, wef, wsf = outs
    return (
        qa,
        ka,
        vv,
        own,
        kt,
        tt,
        ctx,
        par,
        eb,
        wof.reshape(width, width),
        wef.reshape(width, ff),
        wsf.reshape(ff, width),
    )


def finish_kernel(
    lout,
    tg,
    trip,
    go,
    ge,
    gs,
    bias,
    small,
    o_lout,
    o_tg,
    o_trip,
    o_qb,
    o_vb,
    o_go,
    o_ob,
    o_g1,
    o_s1,
    o_ge,
    o_eb,
    o_gs,
    o_sb,
    o_g2,
    o_s2,
    b_lout,
    b_tg,
    b_trip,
    b_go,
    b_ge,
    b_gs,
    f_go,
    f_ge,
    f_gs,
    sem_in,
    sem_out,
):
    ins = ((ge, b_ge), (gs, b_gs), (trip, b_trip), (lout, b_lout), (tg, b_tg), (go, b_go))
    loads = [pltpu.make_async_copy(src, dst, sem_in.at[i]) for i, (src, dst) in enumerate(ins)]
    for copy in loads:
        copy.start()
    n = o_qb.shape[0]
    o_qb[...] = bias[0, :n]
    o_vb[...] = bias[1, :n]
    for r, ref in ((2, o_ob), (3, o_g1), (4, o_s1), (5, o_sb), (6, o_g2), (7, o_s2)):
        ref[...] = small[r, :n]
    for r in range(4):
        o_eb[pl.ds(r * n, n)] = small[8 + r, :n]
    outs = ((f_ge, o_ge), (f_gs, o_gs), (b_trip, o_trip), (b_lout, o_lout), (b_tg, o_tg), (f_go, o_go))
    wide = {0: (b_ge, f_ge), 1: (b_gs, f_gs), 5: (b_go, f_go)}
    stores = []
    for i, (src, dst) in enumerate(outs):
        loads[i].wait()
        if i in wide:
            wide[i][1][...] = wide[i][0][...].astype(F32)
        copy = pltpu.make_async_copy(src, dst, sem_out.at[i])
        copy.start()
        stores.append(copy)
    for copy in stores:
        copy.wait()


def finish_call(lout, tg, trip, go, ge, gs, bias, small, n):
    vm = pl.BlockSpec(memory_space=pltpu.VMEM)
    hbm = pl.BlockSpec(memory_space=pl.ANY)

    def like(x, dtype=None):
        return jax.ShapeDtypeStruct(x.shape, dtype or x.dtype)

    vec = jax.ShapeDtypeStruct((n,), F32)
    big = (lout, tg, trip, go, ge, gs)
    return pl.pallas_call(
        finish_kernel,
        out_shape=(
            like(lout),
            like(tg),
            like(trip),
            vec,
            vec,
            like(go, F32),
            vec,
            vec,
            vec,
            like(ge, F32),
            jax.ShapeDtypeStruct((4 * n,), F32),
            like(gs, F32),
            vec,
            vec,
            vec,
        ),
        in_specs=[hbm] * 6 + [vm] * 2,
        out_specs=(hbm, hbm, hbm, vm, vm, hbm, vm, vm, vm, hbm, vm, hbm, vm, vm, vm),
        scratch_shapes=[pltpu.VMEM(x.shape, x.dtype) for x in big]
        + [pltpu.VMEM(x.shape, F32) for x in (go, ge, gs)]
        + [pltpu.SemaphoreType.DMA((6,)), pltpu.SemaphoreType.DMA((6,))],
        compiler_params=pltpu.CompilerParams(vmem_limit_bytes=VMEM_BYTES),
        name="finish",
    )(*big, bias, small)


def norm_parts(hidden):
    center = hidden - jnp.mean(hidden, axis=-1, keepdims=True)
    factor = lax.rsqrt(jnp.mean(center * center, axis=-1, keepdims=True) + EPS)
    return center * factor, factor


def norm_back(grad, normal, factor, gain):
    c = grad * gain
    mean = jnp.mean(c, axis=-1, keepdims=True)
    inner = jnp.mean(c * normal, axis=-1, keepdims=True)
    return factor * (c - mean - normal * inner)


NT = (((1,), (1,)), ((), ()))
TN = (((0,), (0,)), ((), ()))


def middle(
    refs,
    grads,
    shrink_ready,
    shrink_go,
    context_ready,
    loads,
    out_sem,
    wo,
    we,
    ws,
    nl,
    nlt,
    n1,
    r1,
    act,
    slope,
    sl,
):
    tok, ctx, par, eb, cot, lout, gfirst, vecs, ebg = refs
    g_out, g_exp, g_shr = grads
    rows, width = tok.shape
    ff = eb.shape[1]
    zs = g_out.shape[1]
    n = width // (2 * zs)
    tile = min(128, rows)
    wide = 256
    vecs[...] = jnp.zeros_like(vecs)

    def add_row(r, value):
        vecs[r : r + 1, :] = vecs[r : r + 1, :] + jnp.sum(value, axis=0, keepdims=True)

    loads[0].wait()

    @pl.loop(0, width // wide)
    def _(j):
        at = pl.ds(pl.multiple_of(j * wide, wide), wide)
        gfirst[:, at] = jnp.dot(ctx[...], wo[:, at], preferred_element_type=F32)

    @pl.loop(0, rows // tile)
    def _(i):
        at = pl.ds(pl.multiple_of(i * tile, tile), tile)
        normal, factor = norm_parts(tok[at, :].astype(F32) + gfirst[at, :] + par[2:3, :])
        n1[at, :] = normal
        r1[at, :] = factor
        nl[at, :] = (normal * par[3:4, :] + par[4:5, :]).astype(BF16)

    loads[1].wait()

    @pl.loop(0, ff // wide)
    def _(j):
        at = pl.ds(pl.multiple_of(j * wide, wide), wide)
        u = jnp.dot(nl[...], we[:, at], preferred_element_type=F32) + eb[:, at]
        phi = 0.5 + 0.5 * lax.erf(u * 0.5**0.5)
        act[:, at] = (u * phi).astype(BF16)
        slope[:, at] = (phi + u * (jnp.exp(-0.5 * u * u) * (2.0 * 3.141592653589793) ** -0.5)).astype(BF16)

    nlt[...] = nl[...].T
    loads[2].wait()

    @pl.loop(0, width // wide)
    def _(j):
        at = pl.ds(pl.multiple_of(j * wide, wide), wide)
        gfirst[:, at] = jnp.dot(act[...], ws[:, at], preferred_element_type=F32)

    @pl.loop(0, rows // tile)
    def _(i):
        at = pl.ds(pl.multiple_of(i * tile, tile), tile)
        second = n1[at, :] * par[3:4, :] + par[4:5, :] + par[5:6, :] + gfirst[at, :]
        normal, factor = norm_parts(second)
        nl[at, :] = (normal * par[6:7, :] + par[7:8, :]).astype(BF16)
        e = cot[at, :].astype(F32)
        add_row(6, e * normal)
        add_row(7, e)
        back = norm_back(e, normal, factor, par[6:7, :])
        gfirst[at, :] = back
        low = back.astype(BF16)
        sl[at, :] = low
        add_row(5, low.astype(F32))

    result = pltpu.make_async_copy(nl, lout, out_sem)
    result.start()
    per = max(1, 384 // (4 * n))

    @pl.loop(0, ff // (per * 4 * n))
    def _(j):
        at = pl.ds(pl.multiple_of(j * per * 4 * n, LANES), per * 4 * n)
        g = lax.dot_general(act[:, at], sl[...], TN, preferred_element_type=F32)
        for k in range(per):
            fi = j * per + k
            for qi in range(SEQ):
                lo = (k * SEQ + qi) * n
                g_shr[fi % 2, fi // 2, qi] = g[lo : lo + n].astype(BF16)

    shrink_ready()

    @pl.loop(0, ff // wide)
    def _(j):
        at = pl.ds(pl.multiple_of(j * wide, wide), wide)
        back = lax.dot_general(sl[...], ws[at, :], NT, preferred_element_type=F32)
        low = (back * slope[:, at].astype(F32)).astype(BF16)
        act[:, at] = low
        ebg[:, at] = jnp.sum(low.astype(F32), axis=0, keepdims=True)

    shrink_go()

    @pl.loop(0, width // wide)
    def _(j):
        at = pl.ds(pl.multiple_of(j * wide, wide), wide)
        gfirst[:, at] += lax.dot_general(act[...], we[at, :], NT, preferred_element_type=F32)

    @pl.loop(0, rows // tile)
    def _(i):
        at = pl.ds(pl.multiple_of(i * tile, tile), tile)
        e = gfirst[at, :]
        normal = n1[at, :]
        add_row(3, e * normal)
        add_row(4, e)
        back = norm_back(e, normal, r1[at, :], par[3:4, :])
        gfirst[at, :] = back
        low = back.astype(BF16)
        sl[at, :] = low
        add_row(2, low.astype(F32))

    context_ready()
    q = n // SEQ

    def keep(grad, g, j, at):
        if q % 8 == 0:
            for fi in range(2 * zs):
                for qi in range(SEQ):
                    lo = fi * n + qi * q
                    grad[fi % 2, fi // 2, qi, :, at] = g[lo : lo + q].astype(BF16)
        else:
            blocks = ff // SEQ // wide
            for fi in range(2 * zs):
                grad[fi % 2, fi // 2, j // blocks, :, pl.ds(pl.multiple_of(j % blocks * wide, wide), wide)] = g[
                    fi * n : (fi + 1) * n
                ].astype(BF16)

    @pl.loop(0, ff // wide)
    def _(j):
        at = pl.ds(pl.multiple_of(j * wide, wide), wide)
        keep(g_exp, jnp.dot(nlt[...], act[:, at], preferred_element_type=F32), j, at)

    if q % 8 == 0:

        @pl.loop(0, width // wide)
        def _(j):
            at = pl.ds(pl.multiple_of(j * wide, wide), wide)
            keep(g_out, lax.dot_general(ctx[...], sl[:, at], TN, preferred_element_type=F32), j, at)

    else:
        w = width // SEQ
        for qi in range(SEQ):
            g = lax.dot_general(ctx[...], sl[:, qi * w : (qi + 1) * w], TN, preferred_element_type=F32)
            for fi in range(2 * zs):
                g_out[fi % 2, fi // 2, qi, :, 0:w] = g[fi * n : (fi + 1) * n].astype(BF16)

    result.wait()


def collect_kernel(
    zs,
    qa_hbm,
    ka_hbm,
    v_hbm,
    own_hbm,
    kt_hbm,
    tt_hbm,
    trip,
    tokens,
    ctx,
    par,
    eb,
    cot,
    wo_hbm,
    we_hbm,
    ws_hbm,
    lout,
    tg_out,
    trip_out,
    bias_out,
    small_out,
    go_out,
    ge_out,
    gs_out,
    wland,
    dsend,
    drecv,
    grecv,
    gfirst,
    vecs,
    ebg,
    tsend,
    tcore,
    tz,
    tfin,
    svec,
    svcore,
    svz,
    svseq,
    ao,
    ae,
    a_s,
    co,
    ce,
    cs,
    xo,
    xe,
    xs,
    yo,
    ye,
    ys,
    x2o,
    x2e,
    x2s,
    y2o,
    y2e,
    y2s,
    zo,
    ze,
    zsm,
    fo,
    fe,
    fs,
    send,
    recv,
    local,
):
    s = lax.axis_index("seq")
    f = lax.axis_index("fsdp")
    z, c = f // 2, f % 2
    rows, width = tokens.shape
    half = rows // 2
    length = rows * SEQ
    n = trip.shape[0]
    hw = HL * HEAD_DIM
    s1, s2, s3 = ring(s)
    zpeers = [((z + j) % zs, (z - j + zs) % zs) for j in range(1, zs)]
    sib = (s, z * 2 + 1 - c)
    net = Net(send, recv)
    lane = lax.broadcasted_iota(jnp.int32, (1, LANES), 1)

    barrier = pltpu.get_barrier_semaphore()
    partners = [(s1, f), (s2, f), (s3, f), sib] + [(s, zt * 2 + c) for zt, _ in zpeers]
    for partner in partners:
        pl.semaphore_signal(barrier, inc=1, device_id=partner, device_id_type=MESH)

    w_z = [net.slot() for _ in zpeers]
    w_sib = [net.slot() for _ in range(zs)]
    own_copy = pltpu.make_async_copy(trip, wland.at[z, c], local.at[0])
    own_copy.start()

    def enter():
        pl.semaphore_wait(barrier, len(partners))
        for j, (zt, _) in enumerate(zpeers):
            net.begin(w_z[j], lambda zt=zt: (trip, wland.at[z, c], (s, zt * 2 + c)))
        net.begin(w_sib[0], lambda: (trip, wland.at[z, c], sib))

    def shrink_ready():
        enter()
        core_start(2)

    d_sem = [[net.slot() for _ in range(3)] for _ in range(HL)]
    grads, core = (ao, ae, a_s), (co, ce, cs)
    c_sem = [net.slot() for _ in range(3)]

    def core_start(i):
        net.begin(c_sem[i], lambda: (grads[i].at[1 - c], core[i], sib))

    v_core = net.slot()
    v_z = [net.slot() for _ in zpeers]
    v_seq = [net.slot() for _ in range(3)]

    def small_start():
        for zi in range(zs):
            for ci in range(2):
                fi = zi * 2 + ci
                svec[ci, zi] = jnp.zeros((16, LANES), F32)
                svec[ci, zi, 0:8, 0:n] = vecs[:, fi * n : (fi + 1) * n]
                for r in range(4):
                    at = fi * 4 * n + r * n
                    svec[ci, zi, 8 + r : 9 + r, 0:n] = ebg[:, at : at + n]
        net.start(v_core, svec.at[1 - c], svcore, sib)

    xr, yr, x2r, y2r, zr, fin = (xo, xe, xs), (yo, ye, ys), (x2o, x2e, x2s), (y2o, y2e, y2s), (zo, ze, zsm), (fo, fe, fs)
    x_sem = [[net.slot() for _ in range(4)] for _ in range(3)]
    x2_sem = [[net.slot() for _ in range(2)] for _ in range(3)]
    z_sem = [[net.slot() for _ in zpeers] for _ in range(3)]
    a_sem = [[net.slot() for _ in range(4)] for _ in range(3)]

    def cols(i, which):
        w = grads[i].shape[-1] // 2
        return pl.ds(which * w, w)

    def plane_start(i):
        net.arrived(c_sem[i], core[i], sib)

        @pl.loop(0, zs * SEQ)
        def _(k):
            zi, qi = k // SEQ, k % SEQ
            total = grads[i][c, zi, qi].astype(F32) + core[i][zi, qi].astype(F32)
            grads[i][c, zi, qi] = total.astype(BF16)

        x, y = cols(i, 0), cols(i, 1)
        net.begin(x_sem[i][0], lambda: (grads[i].at[c, :, s3, :, x], xr[i].at[:, 1], (s1, f)))
        net.begin(x_sem[i][2], lambda: (grads[i].at[c, :, s3, :, y], yr[i].at[:, 1], (s2, f)))
        net.begin(x_sem[i][1], lambda: (grads[i].at[c, :, s1, :, x], xr[i].at[:, 0], (s1, f)))
        net.begin(x_sem[i][3], lambda: (grads[i].at[c, :, s2, :, y], yr[i].at[:, 0], (s2, f)))

    def add_into(i, part, qi, which, from_ref):
        w = grads[i].shape[-1] // 2

        @pl.loop(0, zs)
        def _(zi):
            a = grads[i][c, zi, qi, :, which * w : (which + 1) * w].astype(F32)
            b = (from_ref[zi] if part is None else from_ref[zi, part]).astype(F32)
            grads[i][c, zi, qi, :, which * w : (which + 1) * w] = (a + b).astype(BF16)

    def plane_second(i):
        net.arrived(x_sem[i][0], xr[i].at[:, 1], (s1, f))
        add_into(i, 1, s2, 0, xr[i])
        net.begin(x2_sem[i][0], lambda: (grads[i].at[c, :, s2, :, cols(i, 0)], x2r[i], (s2, f)))
        net.arrived(x_sem[i][2], yr[i].at[:, 1], (s2, f))
        add_into(i, 1, s1, 1, yr[i])
        net.begin(x2_sem[i][1], lambda: (grads[i].at[c, :, s1, :, cols(i, 1)], y2r[i], (s1, f)))
        net.arrived(x_sem[i][1], xr[i].at[:, 0], (s1, f))
        add_into(i, 0, s, 0, xr[i])
        net.arrived(x_sem[i][3], yr[i].at[:, 0], (s2, f))
        add_into(i, 0, s, 1, yr[i])

    def along_z(i):
        net.arrived(x2_sem[i][0], x2r[i], (s2, f))
        add_into(i, None, s, 0, x2r[i])
        net.arrived(x2_sem[i][1], y2r[i], (s1, f))
        add_into(i, None, s, 1, y2r[i])
        for j, (zt, _) in enumerate(zpeers):
            net.begin(z_sem[i][j], lambda zt=zt, j=j: (grads[i].at[c, zt, s], zr[i].at[j], (s, zt * 2 + c)))

    def own_rows(i):
        total = grads[i][c, z, s].astype(F32)
        for j, (_, zf) in enumerate(zpeers):
            net.arrived(z_sem[i][j], zr[i].at[j], (s, zf * 2 + c))
            total = total + zr[i][j].astype(F32)
        fin[i][s] = total.astype(BF16)
        net.begin(a_sem[i][0], lambda: (fin[i].at[s], fin[i].at[s], (s1, f)))
        net.begin(a_sem[i][1], lambda: (fin[i].at[s], fin[i].at[s], (s2, f)))

    def spread(i):
        net.arrived(a_sem[i][0], fin[i].at[s1], (s1, f))
        net.begin(a_sem[i][2], lambda: (fin[i].at[s1, :, cols(i, 0)], fin[i].at[s1, :, cols(i, 0)], (s2, f)))
        net.arrived(a_sem[i][1], fin[i].at[s2], (s2, f))
        net.begin(a_sem[i][3], lambda: (fin[i].at[s2, :, cols(i, 1)], fin[i].at[s2, :, cols(i, 1)], (s1, f)))

    final_out = (go_out, ge_out, gs_out)

    def spread_end(i):
        net.arrived(a_sem[i][2], fin[i].at[s3, :, cols(i, 0)], (s2, f))
        net.arrived(a_sem[i][3], fin[i].at[s3, :, cols(i, 1)], (s1, f))
        copy = pltpu.make_async_copy(fin[i], final_out[i], local.at[1 + i])
        copy.start()
        return copy

    def context_send(h):
        for k, peer in enumerate((s3, s1, s2)):
            net.begin(d_sem[h][k], lambda peer=peer, h=h: (dsend.at[peer, h], drecv.at[s, h], (peer, f)))

    def context_ready(wo, al):
        for t in range(SEQ):
            at = t * hw
            back = lax.dot_general(al[...], wo[at : at + hw, :], NT, preferred_element_type=F32).astype(BF16)
            for h in range(HL):
                dsend[t, h, :, 0:HEAD_DIM] = back[0:half, h * HEAD_DIM : (h + 1) * HEAD_DIM]
                dsend[t, h, :, HEAD_DIM:LANES] = back[half:rows, h * HEAD_DIM : (h + 1) * HEAD_DIM]
        context_send(0)
        drecv[s] = dsend[s]

    def tokens_part(wo, we, ws, nl, nlt, n1, r1, act, slope, sl):
        loads = []
        for i, (src, dst) in enumerate(((wo_hbm, wo), (we_hbm, we), (ws_hbm, ws))):
            copy = pltpu.make_async_copy(src, dst, local.at[1 + i])
            copy.start()
            loads.append(copy)
        middle(
            (tokens, ctx, par, eb, cot, lout, gfirst, vecs, ebg),
            grads,
            shrink_ready,
            lambda: plane_start(2),
            lambda: context_ready(wo, sl),
            loads,
            local.at[4],
            wo,
            we,
            ws,
            nl,
            nlt,
            n1,
            r1,
            act,
            slope,
            sl,
        )

    ff = eb.shape[1]
    pl.run_scoped(
        tokens_part,
        pltpu.VMEM((width, width), BF16),
        pltpu.VMEM((width, ff), BF16),
        pltpu.VMEM((ff, width), BF16),
        pltpu.VMEM((rows, width), BF16),
        pltpu.VMEM((width, rows), BF16),
        pltpu.VMEM((rows, width), F32),
        pltpu.VMEM((rows, 1), F32),
        pltpu.VMEM((rows, ff), BF16),
        pltpu.VMEM((rows, ff), BF16),
        pltpu.VMEM((rows, width), BF16),
    )
    core_start(1)
    core_start(0)
    context_send(1)
    small_start()
    own_copy.wait()

    def attention_part(qa, ka, vv, own, k_t, tok_t, da, dq_t, acc_k, acc_v, gm, gsend, gmr, wfull, wtmp=None):
        loads = []
        pairs = ((qa_hbm, qa), (ka_hbm, ka), (v_hbm, vv), (own_hbm, own), (kt_hbm, k_t), (tt_hbm, tok_t))
        for i, (src, dst) in enumerate(pairs):
            copy = pltpu.make_async_copy(src, dst, local.at[1 + i])
            copy.start()
            loads.append(copy)
        gm[...] = jnp.zeros_like(gm)
        plane_start(1)
        plane_start(0)
        for copy in loads:
            copy.wait()

        net.arrived(v_core, svcore, sib)
        svec[c] = svec[c] + svcore[...]
        for j, (zt, _) in enumerate(zpeers):
            net.start(v_z[j], svec.at[c, zt], svz.at[j], (s, zt * 2 + c))

        g_sem = [[net.slot() for _ in range(3)] for _ in range(HL)]
        tc_sem = [net.slot() for _ in range(HL)]
        tz_sem = [[net.slot() for _ in zpeers] for _ in range(HL)]
        ts_sem = [[net.slot() for _ in range(3)] for _ in range(HL)]

        def prepare(h):
            for k, peer in enumerate((s3, s1, s2)):
                net.arrived(d_sem[h][k], drecv.at[peer, h], (peer, f))

            @pl.loop(0, SEQ)
            def _(t):
                grad = drecv[t, h].astype(F32)
                prod = grad * own[t, h].astype(F32)
                left = lane < HEAD_DIM
                for k in range(2):
                    inner = -jnp.sum(jnp.where(left if k == 0 else jnp.logical_not(left), prod, 0.0), axis=-1, keepdims=True)
                    hi = inner.astype(BF16).astype(F32)
                    here = grad if k == 0 else pltpu.roll(grad, HEAD_DIM, 1)
                    here = jnp.where(left, here, jnp.where(lane == HEAD_DIM, hi, jnp.where(lane == HEAD_DIM + 1, inner - hi, 0.0)))
                    at = pl.multiple_of(t * rows + k * half, half)
                    da[pl.ds(at, half), :] = here.astype(BF16)

            dq_t[...] = jnp.zeros_like(dq_t)

        def key_block(h, r):
            acc_k[...] = jnp.zeros_like(acc_k)
            acc_v[...] = jnp.zeros_like(acc_v)
            keys = pl.multiple_of(r * rows, rows)
            nt = (((1,), (1,)), ((), ()))

            @pl.loop(0, length // QB)
            def _(i):
                at = pl.multiple_of(i * QB, QB)
                q = qa[h, pl.ds(at, QB), :]
                grad = da[pl.ds(at, QB), :]
                probs = jnp.exp(lax.dot_general(ka[h, pl.ds(keys, rows), :], q, nt, preferred_element_type=F32))
                inner = lax.dot_general(vv[h, pl.ds(keys, rows), :], grad, nt, preferred_element_type=F32)
                ds = (probs * inner).astype(BF16)
                acc_v[...] += jnp.dot(probs.astype(BF16), grad, preferred_element_type=F32)
                acc_k[...] += jnp.dot(ds, q, preferred_element_type=F32)
                dq_t[:, pl.ds(at, QB)] += jnp.dot(k_t[h, :, pl.ds(keys, rows)], ds, preferred_element_type=F32)

            gm[pl.ds(keys, rows), HEAD_DIM:LANES] = acc_k[:, 0:HEAD_DIM].astype(BF16)
            gm[pl.ds(keys, rows), LANES : LANES + HEAD_DIM] = acc_v[:, 0:HEAD_DIM].astype(BF16)

        rt = tsend.shape[3]
        vrow = n + n // 2
        brow = rt - 16

        def head_done(h):
            @pl.loop(0, SEQ)
            def _(t):
                at = pl.multiple_of(t * rows, rows)
                dq = (dq_t[:, pl.ds(at, rows)].T * (HEAD_DIM**-0.5)).astype(BF16)
                gm[pl.ds(at, rows), 0:HEAD_DIM] = dq
                for k in range(3):
                    for p in range(2):
                        piece = gm[pl.ds(at + p * half, half), k * HEAD_DIM : (k + 1) * HEAD_DIM]
                        gsend[h, t, k, :, p * HEAD_DIM : (p + 1) * HEAD_DIM] = piece

            for k, peer in enumerate((s3, s1, s2)):
                net.start(g_sem[h][k], gsend.at[h, peer], grecv.at[h, s], (peer, f))
            grecv[h, s] = gsend[h, s]
            sums = jnp.sum(gm[...].astype(F32), axis=0, keepdims=True).astype(BF16)
            whole = jnp.dot(tok_t[...], gm[...], preferred_element_type=F32)
            for zi in range(zs):
                for ci in range(2):
                    fi = zi * 2 + ci
                    grad = whole[fi * n : (fi + 1) * n].astype(BF16)
                    tsend[h, ci, zi, 0:n, :] = grad[:, 0:LANES]
                    tsend[h, ci, zi, n:vrow, 0:HEAD_DIM] = grad[0 : n // 2, LANES : LANES + HEAD_DIM]
                    tsend[h, ci, zi, n:vrow, HEAD_DIM:LANES] = grad[n // 2 : n, LANES : LANES + HEAD_DIM]
                    tsend[h, ci, zi, brow:rt, :] = jnp.broadcast_to(sums[:, 0:LANES], (16, LANES))
                    tsend[h, ci, zi, brow + 8 : rt, :] = jnp.broadcast_to(sums[:, LANES : 2 * LANES], (8, LANES))
            net.start(tc_sem[h], tsend.at[h, 1 - c], tcore.at[h], sib)

        def triple_z(h):
            net.arrived(tc_sem[h], tcore.at[h], sib)
            tsend[h, c] = (tsend[h, c].astype(F32) + tcore[h].astype(F32)).astype(BF16)
            for j, (zt, _) in enumerate(zpeers):
                net.begin(tz_sem[h][j], lambda zt=zt, j=j: (tsend.at[h, c, zt], tz.at[h, j], (s, zt * 2 + c)))

        def triple_own(h):
            total = tsend[h, c, z].astype(F32)
            for j, (_, zf) in enumerate(zpeers):
                net.arrived(tz_sem[h][j], tz.at[h, j], (s, zf * 2 + c))
                total = total + tz[h, j].astype(F32)
            tfin[h, s] = total.astype(BF16)
            for k, peer in enumerate((s3, s1, s2)):
                net.begin(ts_sem[h][k], lambda peer=peer: (tfin.at[h, s], tfin.at[h, s], (peer, f)))

        def rows_in(h):
            for k, peer in enumerate((s3, s1, s2)):
                net.arrived(g_sem[h][k], grecv.at[h, peer], (peer, f))
            for t in range(SEQ):
                for k in range(3):
                    at = k * width + t * hw + h * HEAD_DIM
                    gmr[0:half, at : at + HEAD_DIM] = grecv[h, t, k, :, 0:HEAD_DIM]
                    gmr[half:rows, at : at + HEAD_DIM] = grecv[h, t, k, :, HEAD_DIM:LANES]

        def attend_back(h, *steps):
            @pl.loop(0, SEQ)
            def _(r):
                key_block(h, r)
                for k, step in enumerate(steps):

                    @pl.when(r == k)
                    def _(step=step):
                        for call, arg in step:
                            call(arg)

        plane_second(2)
        prepare(0)
        context_send(2)
        attend_back(0, [], [], [], [(plane_second, 1)])
        head_done(0)
        for j, (_, zf) in enumerate(zpeers):
            net.arrived(w_z[j], wland.at[zf, c], (s, zf * 2 + c))
            net.start(w_sib[j + 1], wland.at[zf, c], wland.at[zf, c], sib)
        prepare(1)
        attend_back(
            1,
            [(triple_z, 0)],
            [(along_z, 2), (plane_second, 0)],
        )
        head_done(1)
        total = svec[c, z]
        for j, (_, zf) in enumerate(zpeers):
            net.arrived(v_z[j], svz.at[j], (s, zf * 2 + c))
            total = total + svz[j]
        svseq[s] = total
        for k, peer in enumerate((s3, s1, s2)):
            net.start(v_seq[k], svseq.at[s], svseq.at[s], (peer, f))
        prepare(2)
        attend_back(
            2,
            [(along_z, 1), (triple_own, 0)],
            [(own_rows, 2), (along_z, 0)],
            [(triple_z, 1)],
        )
        head_done(2)
        spread(2)
        rows_in(0)
        net.arrived(w_sib[0], wland.at[z, 1 - c], sib)
        for j, (_, zf) in enumerate(zpeers):
            net.arrived(w_sib[j + 1], wland.at[zf, 1 - c], sib)
        depth = zs if zs <= 4 else 1
        for base in range(0, zs, depth):
            if zs > 4:
                copy = pltpu.make_async_copy(wland.at[pl.ds(base, depth)], wtmp, local.at[0])
                copy.start()
                copy.wait()
            for zi in range(depth):
                for ci in range(2):
                    fi = (base + zi) * 2 + ci
                    wfull[fi * n : (fi + 1) * n, :] = (wtmp if zs > 4 else wland)[zi, ci]
        triple_own(1)
        triple_z(2)
        own_rows(1)
        own_rows(0)
        rows_in(1)
        triple_own(2)
        spread(1)
        spread(0)
        rows_in(2)
        wide = 256

        @pl.loop(0, width // wide)
        def _(j):
            at = pl.ds(pl.multiple_of(j * wide, wide), wide)
            back = lax.dot_general(gmr[...], wfull[at, :], NT, preferred_element_type=F32)
            tg_out[:, at] = (gfirst[:, at] + back).astype(BF16)

        copies = [spread_end(2), spread_end(1)]
        for k, peer in enumerate((s3, s1, s2)):
            net.arrived(v_seq[k], svseq.at[peer], (peer, f))
        small_out[...] = svseq[0] + svseq[1] + svseq[2] + svseq[3]
        for h in range(HL):
            for k, peer in enumerate((s3, s1, s2)):
                net.arrived(ts_sem[h][k], tfin.at[h, peer], (peer, f))
        q_row, v_row = [], []
        for t in range(SEQ):
            for h in range(HL):
                at = t * hw + h * HEAD_DIM
                block = tfin[h, t].astype(F32)
                trip_out[:, at : at + HEAD_DIM] = block[0:n, 0:HEAD_DIM]
                trip_out[:, width + at : width + at + HEAD_DIM] = block[0:n, HEAD_DIM:LANES]
                trip_out[0 : n // 2, 2 * width + at : 2 * width + at + HEAD_DIM] = block[n:vrow, 0:HEAD_DIM]
                trip_out[n // 2 : n, 2 * width + at : 2 * width + at + HEAD_DIM] = block[n:vrow, HEAD_DIM:LANES]
                q_row.append(block[brow : brow + 1, 0:HEAD_DIM])
                v_row.append(block[brow + 8 : brow + 9, 0:HEAD_DIM])
        q_row, v_row = jnp.concatenate(q_row, axis=1), jnp.concatenate(v_row, axis=1)
        bias_out[...] = jnp.zeros_like(bias_out)
        for fi in range(2 * zs):

            @pl.when(f == fi)
            def _(fi=fi):
                bias_out[0:1, 0:n] = q_row[:, fi * n : (fi + 1) * n]
                bias_out[1:2, 0:n] = v_row[:, fi * n : (fi + 1) * n]

        copies.append(spread_end(0))
        for copy in copies:
            copy.wait()
        net.drain()

    pl.run_scoped(
        attention_part,
        pltpu.VMEM((HL, length, LANES), BF16),
        pltpu.VMEM((HL, length, LANES), BF16),
        pltpu.VMEM((HL, length, LANES), BF16),
        pltpu.VMEM((SEQ, HL, half, LANES), BF16),
        pltpu.VMEM((HL, HEAD_DIM, length), BF16),
        pltpu.VMEM((width, length), BF16),
        pltpu.VMEM((length, LANES), BF16),
        pltpu.VMEM((HEAD_DIM, length), F32),
        pltpu.VMEM((rows, LANES), F32),
        pltpu.VMEM((rows, LANES), F32),
        pltpu.VMEM((length, 2 * LANES), BF16),
        pltpu.VMEM((HL, SEQ, 3, half, LANES), BF16),
        pltpu.VMEM((rows, 3 * width), BF16),
        pltpu.VMEM((width, 3 * width), BF16),
        *([pltpu.VMEM((1, 2, n, 3 * width), BF16)] if zs > 4 else []),
    )


QB = 512
VMEM_BYTES = 127 << 19


def collect_call(qa, ka, vv, own, kt, tt, triple, tokens, ctx, par, eb, cot, wo, we, ws):
    rows, width = tokens.shape
    length = rows * SEQ
    n = triple.shape[0]
    zs = width // n // 2
    p = zs - 1
    ff = eb.shape[1]
    q = n // SEQ
    rt = (n + n // 2 + 7) // 8 * 8 + 16
    half = rows // 2
    slots = 3 * HL + 3 + 1 + p + 3 + p + zs + 3 * (4 + 2 + p + 4) + HL * (3 + 1 + p + 3)
    vm = pl.BlockSpec(memory_space=pltpu.VMEM)
    hbm = pl.BlockSpec(memory_space=pl.ANY)
    if q % 8 == 0:
        shapes = ((q, width), (q, ff), (n, width))
    else:
        shapes = ((n, 256), (n, ff // SEQ), (n, width))

    def per_weight(make):
        return [pltpu.VMEM(make(a, b), BF16) for a, b in shapes]

    outs = pl.pallas_call(
        functools.partial(collect_kernel, zs),
        out_shape=(
            jax.ShapeDtypeStruct((rows, width), BF16),
            jax.ShapeDtypeStruct((rows, width), BF16),
            jax.ShapeDtypeStruct((n, 3 * width), F32),
            jax.ShapeDtypeStruct((8, LANES), F32),
            jax.ShapeDtypeStruct((16, LANES), F32),
        )
        + tuple(jax.ShapeDtypeStruct((SEQ, a, b), BF16) for a, b in shapes)
        + ((jax.ShapeDtypeStruct((zs, 2, n, 3 * width), BF16),) if zs > 4 else ()),
        in_specs=[hbm] * 6 + [vm] * 6 + [hbm] * 3,
        out_specs=(hbm, vm, vm, vm, vm, hbm, hbm, hbm) + ((hbm,) if zs > 4 else ()),
        scratch_shapes=([] if zs > 4 else [pltpu.VMEM((zs, 2, n, 3 * width), BF16)])
        + [
            pltpu.VMEM((SEQ, HL, half, LANES), BF16),
            pltpu.VMEM((SEQ, HL, half, LANES), BF16),
            pltpu.VMEM((HL, SEQ, 3, half, LANES), BF16),
            pltpu.VMEM((rows, width), F32),
            pltpu.VMEM((8, width), F32),
            pltpu.VMEM((1, ff), F32),
            pltpu.VMEM((HL, 2, zs, rt, LANES), BF16),
            pltpu.VMEM((HL, zs, rt, LANES), BF16),
            pltpu.VMEM((HL, p, rt, LANES), BF16),
            pltpu.VMEM((HL, SEQ, rt, LANES), BF16),
            pltpu.VMEM((2, zs, 16, LANES), F32),
            pltpu.VMEM((zs, 16, LANES), F32),
            pltpu.VMEM((p, 16, LANES), F32),
            pltpu.VMEM((SEQ, 16, LANES), F32),
        ]
        + per_weight(lambda a, b: (2, zs, SEQ, a, b))
        + per_weight(lambda a, b: (zs, SEQ, a, b))
        + per_weight(lambda a, b: (zs, 2, a, b // 2))
        + per_weight(lambda a, b: (zs, 2, a, b // 2))
        + per_weight(lambda a, b: (zs, a, b // 2))
        + per_weight(lambda a, b: (zs, a, b // 2))
        + per_weight(lambda a, b: (p, a, b))
        + per_weight(lambda a, b: (SEQ, a, b))
        + [
            pltpu.SemaphoreType.DMA((slots,)),
            pltpu.SemaphoreType.DMA((slots,)),
            pltpu.SemaphoreType.DMA((8,)),
        ],
        compiler_params=pltpu.CompilerParams(
            collective_id=1, has_side_effects=True, vmem_limit_bytes=VMEM_BYTES
        ),
        name="collect",
    )(qa, ka, vv, own, kt, tt, triple, tokens, ctx, par, eb, cot, wo, we, ws)
    lout, tg, trip, bias, small, go, ge, gs = outs[:8]
    if q % 8 == 0:
        go, ge = go.reshape(n, width), ge.reshape(n, ff)
    else:
        go = go[:, :, : width // SEQ].transpose(1, 0, 2).reshape(n, width)
        ge = ge.transpose(1, 0, 2).reshape(n, ff)
    return lout, tg, trip, bias, small, go, ge, gs.reshape(4 * n, width)


def body(
    tokens,
    segment,
    padding,
    triple_weight,
    query_bias,
    value_bias,
    output_weight,
    output_bias,
    first_gain,
    first_shift,
    expand_weight,
    expand_bias,
    shrink_weight,
    shrink_bias,
    second_gain,
    second_shift,
    cotangent,
):
    n = output_weight.shape[0]
    small = (
        query_bias,
        value_bias,
        output_bias,
        first_gain,
        first_shift,
        shrink_bias,
        second_gain,
        second_shift,
        expand_bias,
    )
    qa, ka, vv, own, kt, tt, context, par, eb, wo, we, ws = gather_call(
        tokens[0], segment, padding, triple_weight, small, output_weight, expand_weight, shrink_weight
    )
    layer_out, tokens_grad, triple_grad, bias_grad, small_grad, go, ge, gs = collect_call(
        qa, ka, vv, own, kt, tt, triple_weight, tokens[0], context, par, eb, cotangent[0], wo, we, ws
    )
    outs = finish_call(layer_out, tokens_grad, triple_grad, go, ge, gs, bias_grad, small_grad, n)
    return (outs[0][None], outs[1][None]) + tuple(outs[2:])


def solution(mesh):
    return jax.shard_map(
        body,
        mesh=mesh,
        in_specs=(
            P("fsdp", "seq", None),
            P("fsdp", None),
            P("fsdp", None),
            P("fsdp", None),
            P("fsdp"),
            P("fsdp"),
            P("fsdp", None),
            P("fsdp"),
            P("fsdp"),
            P("fsdp"),
            P("fsdp", None),
            P("fsdp"),
            P("fsdp", None),
            P("fsdp"),
            P("fsdp"),
            P("fsdp"),
            P("fsdp", "seq", None),
        ),
        out_specs=(
            P("fsdp", "seq", None),
            P("fsdp", "seq", None),
            P("fsdp", None),
            P("fsdp"),
            P("fsdp"),
            P("fsdp", None),
            P("fsdp"),
            P("fsdp"),
            P("fsdp"),
            P("fsdp", None),
            P("fsdp"),
            P("fsdp", None),
            P("fsdp"),
            P("fsdp"),
            P("fsdp"),
        ),
        check_vma=False,
    )
```
